128 devices in a mesh: dp: 16 (over x, z), tensor: 8 (over y, core).
Axes of the slice: x: 4, y: 4, z: 4, core: 2. Of those that a mesh axis runs over, the one named last changes fastest.
Arguments:
- attn_out: bfloat16 [8192, 8192], P('dp', 'tensor'), may hold values from -6 to 6
- frozen_weight: bfloat16 [8192, 8192], P('tensor', 'dp'), may hold values from -0.0625 to 0.0625
- vector_bank: float32 [256, 256], replicated, may hold values from -0.18 to 0.18
- logits_a: float32 [16, 32, 2], P(None, 'tensor'), may hold values from -2 to 2
- index_a: int32 [16, 32, 2], P(None, 'tensor'), may hold values from 0 to 255, all different within a row
- logits_b: float32 [16, 32, 2], P(None, 'tensor'), may hold values from -2 to 2
- index_b: int32 [16, 32, 2], P(None, 'tensor'), may hold values from 0 to 255, all different within a row
- out_grad: bfloat16 [8192, 8192], P('dp'), may hold values from -6 to 6
Outputs:
- layer_out: bfloat16 [8192, 8192], P('dp', 'tensor')
- attn_grad: bfloat16 [8192, 8192], P('dp', 'tensor')
- bank_grad: float32 [256, 256], replicated
- logits_a_grad: float32 [16, 32, 2], P(None, 'tensor')
- logits_b_grad: float32 [16, 32, 2], P(None, 'tensor')
The draws below stay inside these ranges and needn't reach their ends.
Inputs may be any that keep to these rules, and one draw needn't show every extreme that they name: `index_a`: the 2 entries of one sub-vector differ. `index_b`: the 2 entries of one sub-vector differ.
All inputs are finite; a program needn't handle non-finite values.
Results may differ from the reference program's by a relative error of at most 0.014.
Values may be sent and summed in bfloat16 or wider, within the bound.
No kernel may reach another device: no remote copies, remote signals or barrier semaphores. Data moves between devices by JAX's collectives and lax.ppermute only.
A program may use at most 128 MiB of HBM per device.

```python
import jax
import jax.numpy as jnp
from jax import lax

D = 8192
ATTN = 8192
RANK = 16
SUBLEN = 256
BANK = 256
TOP = 2
TOKENS = 8192
JA = 32
JB = 32
N_TENSOR = 8


def block_levels(own_key, extent, cuts, low, top_value):
    gain = 1.0
    for position, blocks in cuts:
        draws = jax.random.uniform(jax.random.fold_in(jax.random.fold_in(own_key, 6), position), (blocks,), jnp.float32, low / len(cuts), top_value / len(cuts))
        gain = gain * jnp.repeat(jnp.exp(draws), extent[position] // blocks).reshape((-1,) + (1,) * (len(extent) - 1 - position))
    return gain


def choose_distinct(stream_key, rows, number_of, top, lift):
    sequence = jax.random.permutation(jax.random.fold_in(stream_key, 1), number_of)
    boost = sequence
    for power in range(3):
        boost = boost * boost // number_of
    boost = boost * lift // number_of
    lots = jax.random.randint(jax.random.fold_in(stream_key, 2), (rows, number_of), 0, 4096) + boost
    fixed_rows = jax.random.permutation(jax.random.fold_in(stream_key, 3), rows)[jnp.arange(number_of) % rows]
    lots = jnp.where(jnp.arange(rows)[:, None] == fixed_rows[None, :], 1 << 14, lots)
    priority = lots * number_of + jnp.arange(number_of)
    return lax.top_k(priority.astype(jnp.int32), top)[1].astype(jnp.int32)


def normal_values(stream_key, shape, spread, bound, pieces=(), held_as=jnp.bfloat16):
    entries = jax.random.normal(stream_key, shape, jnp.float32) * spread
    if len(pieces) > 0:
        entries = block_levels(stream_key, shape, pieces, -0.22, 0.18) * entries
    return jnp.clip(entries, min=-bound, max=bound).astype(held_as)


def setup_inputs(seed: int = 0) -> dict:
    keys = jax.random.split(jax.random.key(seed), 9)
    attn_out = normal_values(keys[0], (TOKENS, ATTN), 1.0, 6.0, ((0, 16), (1, 8)))
    frozen_weight = normal_values(keys[1], (ATTN, D), ATTN ** -0.5, 0.0625, ((0, 8), (1, 16)))
    vector_bank = normal_values(keys[2], (BANK, SUBLEN), 0.03, 0.18, (), jnp.float32)
    logits_a = jnp.clip(jax.random.uniform(keys[3], (RANK, JA, TOP), jnp.float32, -2.0, 2.0) * block_levels(keys[3], (RANK, JA, TOP), ((1, 8),), -0.4, 0.0), -2.0, 2.0)
    index_a = choose_distinct(keys[4], RANK * JA, BANK, TOP, 64).reshape((RANK, JA, TOP))
    logits_b = jnp.clip(jax.random.uniform(keys[5], (RANK, JB, TOP), jnp.float32, -2.0, 2.0) * block_levels(keys[5], (RANK, JB, TOP), ((1, 8),), -0.4, 0.0), -2.0, 2.0)
    index_b = choose_distinct(keys[6], RANK * JB, BANK, TOP, 64).reshape((RANK, JB, TOP))
    out_grad = normal_values(keys[7], (TOKENS, D), 1.0, 6.0, ((0, 16),))
    return {"attn_out": attn_out, "frozen_weight": frozen_weight, "vector_bank": vector_bank, "logits_a": logits_a, "index_a": index_a, "logits_b": logits_b, "index_b": index_b, "out_grad": out_grad}


adapter_scale = 2.0


def compose(logits, indices, vector_bank):
    weights = jax.nn.sigmoid(logits - logits[..., ::-1])
    levels = jnp.arange(vector_bank.shape[0], dtype=jnp.int32)
    picked = (indices[..., None] == levels).astype(jnp.float32)
    mixing = jnp.sum(picked * weights[..., None], axis=2)
    blocks = jnp.einsum("rjb,bc->rjc", mixing, vector_bank, precision=lax.Precision.HIGHEST)
    return weights, picked, mixing, blocks.reshape(blocks.shape[0], -1)


def compose_back(grad_rows, weights, picked, mixing, vector_bank):
    blocks = grad_rows.reshape(mixing.shape[0], mixing.shape[1], -1)
    bank_part = jnp.einsum("rjb,rjc->bc", mixing, blocks, precision=lax.Precision.HIGHEST)
    projected = jnp.einsum("rjc,bc->rjb", blocks, vector_bank, precision=lax.Precision.HIGHEST)
    dots = jnp.sum(picked * projected[:, :, None, :], axis=3)
    logit_grad = weights * (dots - jnp.sum(weights * dots, axis=2, keepdims=True))
    return bank_part, logit_grad


def reference(attn_out, frozen_weight, vector_bank, logits_a, index_a, logits_b, index_b, out_grad):
    weights_a, picked_a, mixing_a, rows_a = compose(logits_a, index_a, vector_bank)
    weights_b, picked_b, mixing_b, rows_b = compose(logits_b, index_b, vector_bank)
    down_a = rows_a.astype(jnp.bfloat16)
    up_b = rows_b.astype(jnp.bfloat16)
    low_bf = jnp.dot(attn_out, down_a.T, preferred_element_type=jnp.float32).astype(jnp.bfloat16)
    back_bf = jnp.dot(out_grad, up_b.T, preferred_element_type=jnp.float32).astype(jnp.bfloat16)
    width = ATTN // N_TENSOR

    def add_block(carry, block):
        columns = lax.dynamic_slice_in_dim(attn_out, block * width, width, 1)
        weight_rows = lax.dynamic_slice_in_dim(frozen_weight, block * width, width, 0)
        partial_value = jnp.dot(columns, weight_rows, preferred_element_type=jnp.float32).astype(jnp.bfloat16)
        partial_value = lax.optimization_barrier(partial_value)
        return carry + partial_value.astype(jnp.float32), None

    summed, _ = lax.scan(add_block, jnp.zeros((attn_out.shape[0], D), jnp.float32), jnp.arange(N_TENSOR, dtype=jnp.int32))
    layer_out = (summed + adapter_scale * jnp.dot(low_bf, up_b, preferred_element_type=jnp.float32)).astype(jnp.bfloat16)
    main = lax.dot_general(out_grad, frozen_weight, (((1,), (1,)), ((), ())), preferred_element_type=jnp.float32)
    attn_grad = (main + adapter_scale * jnp.dot(back_bf, down_a, preferred_element_type=jnp.float32)).astype(jnp.bfloat16)
    factor = adapter_scale / TOKENS
    grad_a = factor * lax.dot_general(back_bf, attn_out, (((0,), (0,)), ((), ())), preferred_element_type=jnp.float32)
    grad_b = factor * lax.dot_general(low_bf, out_grad, (((0,), (0,)), ((), ())), preferred_element_type=jnp.float32)
    bank_a, logit_grad_a = compose_back(grad_a, weights_a, picked_a, mixing_a, vector_bank)
    bank_b, logit_grad_b = compose_back(grad_b, weights_b, picked_b, mixing_b, vector_bank)
    return layer_out, attn_grad, bank_a + bank_b, logit_grad_a, logit_grad_b
```

```python
import jax
import jax.numpy as jnp
from jax import lax
from jax.sharding import PartitionSpec as P

adapter_scale = 2.0
SIDE = 4
BOTH = ("dp", "tensor")
LANES = [[0, 2, 4, 6], [1, 3, 5, 7]]
SWAP = [(t, t ^ 1) for t in range(8)]


def device(x, z, y, c):
    return (x * SIDE + z) * 8 + y * 2 + c


def pairs(move):
    found = []
    for x in range(SIDE):
        for z in range(SIDE):
            for y in range(SIDE):
                for c in range(2):
                    to = move(x, z, y, c)
                    if to is not None:
                        found.append((device(x, z, y, c), device(*to)))
    return found


def ring(stage, step):
    def move(x, z, y, c):
        if (stage == 0) == (c == 0):
            return ((x + step) % SIDE, z, y, c)
        return (x, (z + step) % SIDE, y, c)

    return pairs(move)


def shift(value, stage, step):
    return lax.ppermute(value, BOTH, ring(stage, step))


def ring_gather(own, stage):
    rows = own.shape[0]
    below = shift(own, stage, 1)
    above = shift(own, stage, -1)
    top = shift(below[: rows // 2], stage, 1)
    bottom = shift(above[rows // 2 :], stage, -1)
    across = jnp.concatenate([top, bottom], axis=0)
    return [own, above, across, below]


def exchange(value, axis, groups=None):
    return lax.all_to_all(
        value, axis, split_axis=0, concat_axis=0, tiled=True, axis_index_groups=groups
    )


def from_everyone(value, axis):
    copies = jnp.broadcast_to(value[None], (lax.axis_size(axis), *value.shape))
    return exchange(copies, axis)


def total_everywhere(value, axis):
    size = lax.axis_size(axis)
    parts = exchange(value.reshape(size, value.shape[0] // size, *value.shape[1:]), axis)
    return jnp.sum(parts, axis=0)


def compose(logits, indices, vector_bank):
    weights = jax.nn.sigmoid(logits - logits[..., ::-1])
    levels = jnp.arange(vector_bank.shape[0], dtype=jnp.int32)
    picked = (indices[..., None] == levels).astype(jnp.float32)
    mixing = jnp.sum(picked * weights[..., None], axis=2)
    blocks = jnp.einsum("rjb,bc->rjc", mixing, vector_bank, precision=lax.Precision.HIGHEST)
    return (weights, picked, mixing, blocks.reshape(blocks.shape[0], -1))


def compose_back(grad_rows, weights, picked, mixing, vector_bank):
    blocks = grad_rows.reshape(mixing.shape[0], mixing.shape[1], -1)
    bank_part = jnp.einsum("rjb,rjc->bc", mixing, blocks, precision=lax.Precision.HIGHEST)
    projected = jnp.einsum("rjc,bc->rjb", blocks, vector_bank, precision=lax.Precision.HIGHEST)
    dots = jnp.sum(picked * projected[:, :, None, :], axis=3)
    logit_grad = weights * (dots - jnp.sum(weights * dots, axis=2, keepdims=True))
    return (bank_part, logit_grad)


def settle(piece, step, z, core):
    def from_second(parity):
        def move(x, z, y, c):
            if c == 1 and y % 2 == parity:
                return (x, z, (x + step) % SIDE, y // 2)
            return None

        return lax.ppermute(piece, BOTH, pairs(move))

    def move(x, z, y, c):
        return (x, z, y, 1) if c == 0 and (z + step) % SIDE >= 2 else None

    crossed = lax.ppermute(piece, BOTH, pairs(move))
    spot = (z + step) % SIDE
    first = jnp.where(core == 0, piece, crossed)
    first = jnp.where(spot // 2 == core, first, jnp.zeros_like(first))
    return first, spot % 2, [from_second(0), from_second(1)]


def local(attn_out, frozen_weight, vector_bank, logits_a, index_a, logits_b, index_b, out_grad):
    tokens, height = attn_out.shape
    shard = frozen_weight.shape[1]
    half, part = shard // 2, shard // 4
    f32, bf16 = jnp.float32, jnp.bfloat16
    dp, tensor = lax.axis_index("dp"), lax.axis_index("tensor")
    x, z, core = dp // SIDE, dp % SIDE, tensor % 2
    near, far = jnp.where(core == 0, x, z), jnp.where(core == 0, z, x)

    left, right = frozen_weight[:, :half], frozen_weight[:, half:]
    mine = jnp.where(core == 0, left, right)
    theirs = jnp.where(core == 0, right, left)
    swapped = lax.ppermute(theirs, "tensor", SWAP)
    blocks = []
    for h in range(2):
        cols = slice(h * part, (h + 1) * part)
        own = jnp.concatenate([mine[:, cols], swapped[:, cols]], axis=0)
        line = jnp.concatenate(ring_gather(own, 0), axis=1)
        blocks.append(ring_gather(line, 1))

    wide = jnp.concatenate([attn_out, lax.ppermute(attn_out, "tensor", SWAP)], axis=1)

    grads = out_grad.reshape(tokens, SIDE, SIDE, 2, 2, part)
    grads = jnp.where(core == 0, grads[:, :, :, 0], jnp.swapaxes(grads[:, :, :, 1], 1, 2))
    grads = grads.transpose(2, 1, 3, 0, 4)

    def grad_chunk(i, h):
        return jnp.concatenate(
            [
                lax.dynamic_slice(
                    grads,
                    ((far + i) % SIDE, (near + k) % SIDE, h, 0, 0),
                    (1, 1, 1, tokens, part),
                ).reshape(tokens, part)
                for k in range(SIDE)
            ],
            axis=1,
        )

    weights_a, picked_a, mixing_a, rows_a = compose(logits_a, index_a, vector_bank)
    weights_b, picked_b, mixing_b, rows_b = compose(logits_b, index_b, vector_bank)
    down_a, up_b = rows_a.astype(bf16), rows_b.astype(bf16)
    grad_cols = lax.dynamic_slice_in_dim(out_grad, tensor * height, height, 1)
    low_part = jnp.dot(attn_out, down_a.T, preferred_element_type=f32)
    back_part = jnp.dot(grad_cols, up_b.T, preferred_element_type=f32)
    totals = total_everywhere(jnp.concatenate([low_part, back_part], axis=1), "tensor")
    totals = from_everyone(totals.astype(bf16), "tensor").reshape(tokens, -1)
    rank = down_a.shape[0]
    low_bf, back_bf = totals[:, :rank], totals[:, rank:]

    factor = adapter_scale / (tokens * lax.axis_size("dp"))
    grad_a = lax.dot_general(
        back_bf, attn_out, (((0,), (0,)), ((), ())), preferred_element_type=f32
    )
    grad_b = lax.dot_general(
        low_bf, grad_cols, (((0,), (0,)), ((), ())), preferred_element_type=f32
    )
    both = factor * jnp.concatenate([grad_a, grad_b], axis=0)
    both = from_everyone(total_everywhere(both, "dp"), "dp").reshape(2 * rank, -1)
    bank_a, logit_grad_a = compose_back(both[:rank], weights_a, picked_a, mixing_a, vector_bank)
    bank_b, logit_grad_b = compose_back(both[rank:], weights_b, picked_b, mixing_b, vector_bank)
    bank_grad = total_everywhere(bank_a + bank_b, "tensor")
    bank_grad = from_everyone(bank_grad, "tensor").reshape(vector_bank.shape)

    grown = jnp.zeros((tokens, 2 * height), f32)
    firsts = [0.0, 0.0]
    seconds = [0.0, 0.0]
    for i in (0, 1, 3, 2):
        reduced = []
        for h in range(2):
            block = blocks[h][i]
            product = jnp.dot(wide, block, preferred_element_type=f32).astype(bf16)
            slots = jnp.stack([product[:, k * part : (k + 1) * part] for k in range(SIDE)])
            slots = lax.dynamic_slice_in_dim(
                jnp.concatenate([slots, slots]), (SIDE - near) % SIDE, SIDE, 0
            )
            arrived = exchange(slots, "tensor", LANES)
            reduced.append(jnp.sum(arrived.astype(f32), axis=0).astype(bf16))
            grown = grown + lax.dot_general(
                grad_chunk(i, h), block, (((1,), (1,)), ((), ())), preferred_element_type=f32
            )
        first, spot, second = settle(jnp.concatenate(reduced, axis=1), i, z, core)
        for s in range(2):
            firsts[s] = firsts[s] + jnp.where(spot == s, first, jnp.zeros_like(first))
            seconds[s] = seconds[s] + second[s]
    summed = jnp.concatenate([firsts[0], seconds[0], firsts[1], seconds[1]], axis=1)
    layer_out = (
        summed.astype(f32) + adapter_scale * jnp.dot(low_bf, up_b, preferred_element_type=f32)
    ).astype(bf16)
    other = lax.ppermute(grown[:, height:].astype(bf16), "tensor", SWAP)
    attn_grad = (
        grown[:, :height]
        + other.astype(f32)
        + adapter_scale * jnp.dot(back_bf, down_a, preferred_element_type=f32)
    ).astype(bf16)
    return (layer_out, attn_grad, bank_grad, logit_grad_a, logit_grad_b)


def solution(mesh):
    return jax.shard_map(
        local,
        mesh=mesh,
        in_specs=(
            P("dp", "tensor"),
            P("tensor", "dp"),
            P(),
            P(None, "tensor", None),
            P(None, "tensor", None),
            P(None, "tensor", None),
            P(None, "tensor", None),
            P("dp", None),
        ),
        out_specs=(
            P("dp", "tensor"),
            P("dp", "tensor"),
            P(),
            P(None, "tensor", None),
            P(None, "tensor", None),
        ),
        check_vma=False,
    )
```

```python
import functools

import jax
import jax.numpy as jnp
from jax import lax
from jax.experimental import pallas as pl
from jax.experimental.pallas import tpu as pltpu
from jax.sharding import PartitionSpec as P

adapter_scale = 2.0
SIDE = 4
BOTH = ("dp", "tensor")
LANES = [[0, 2, 4, 6], [1, 3, 5, 7]]
SWAP = [(t, t ^ 1) for t in range(8)]


def device(x, z, y, c):
    return (x * SIDE + z) * 8 + y * 2 + c


def pairs(move):
    found = []
    for x in range(SIDE):
        for z in range(SIDE):
            for y in range(SIDE):
                for c in range(2):
                    to = move(x, z, y, c)
                    if to is not None:
                        found.append((device(x, z, y, c), device(*to)))
    return found


def ring(stage, step):
    def move(x, z, y, c):
        if (stage == 0) == (c == 0):
            return ((x + step) % SIDE, z, y, c)
        return (x, (z + step) % SIDE, y, c)

    return pairs(move)


def shift(value, stage, step):
    return lax.ppermute(value, BOTH, ring(stage, step))


def ring_gather(own, stage, h):
    below = shift(own, stage, 1)
    above = shift(own, stage, -1)
    across = shift(below, stage, 1) if h == 0 else shift(above, stage, -1)
    return [own, above, across, below]


def exchange(value, axis, groups=None):
    return lax.all_to_all(
        value, axis, split_axis=0, concat_axis=0, tiled=True, axis_index_groups=groups
    )


def over_tensor(value):
    value = value + lax.ppermute(value, "tensor", SWAP)
    value = value + lax.ppermute(value, "tensor", [(t, t ^ 2) for t in range(8)])
    return value + lax.ppermute(value, "tensor", [(t, t ^ 4) for t in range(8)])


def over_dp(value):
    for bit in (1, 4, 2, 8):
        value = value + lax.ppermute(value, "dp", [(d, d ^ bit) for d in range(16)])
    return value


def after(value, *events):
    return lax.optimization_barrier((value, *events))[0]


def forward_kernel(count, near_ref, wide_ref, *refs):
    lines, out_ref, total = refs[:count], refs[count], refs[count + 1]
    step = pl.program_id(0)
    weights = jnp.concatenate([line[k] for line in lines for k in range(SIDE)], axis=1)
    product = jnp.dot(wide_ref[...], weights, preferred_element_type=jnp.float32)

    @pl.when(step == 0)
    def _():
        total[...] = product

    @pl.when(step > 0)
    def _():
        total[...] += product

    @pl.when(step == pl.num_programs(0) - 1)
    def _():
        part = out_ref.shape[2] // count
        for k in range(SIDE):
            slot = lax.rem(near_ref[0] + k, SIDE)
            for m in range(count):
                lane = (m * SIDE + k) * part
                out_ref[slot, :, m * part : (m + 1) * part] = total[:, lane : lane + part].astype(
                    out_ref.dtype
                )


def forward(near, wide, lines):
    tokens, depth = wide.shape
    part = lines[0].shape[2]
    count = len(lines)
    block = depth // 4
    return pl.pallas_call(
        functools.partial(forward_kernel, count),
        out_shape=jax.ShapeDtypeStruct((SIDE, tokens, count * part), jnp.bfloat16),
        grid_spec=pltpu.PrefetchScalarGridSpec(
            num_scalar_prefetch=1,
            grid=(4,),
            in_specs=[pl.BlockSpec((tokens, block), lambda i, n: (0, i))]
            + [pl.BlockSpec((SIDE, block, part), lambda i, n: (0, i, 0))] * count,
            out_specs=pl.BlockSpec((SIDE, tokens, count * part), lambda i, n: (0, 0, 0)),
            scratch_shapes=[pltpu.VMEM((tokens, count * SIDE * part), jnp.float32)],
        ),
        compiler_params=pltpu.CompilerParams(vmem_limit_bytes=40 << 20),
        cost_estimate=pl.CostEstimate(
            flops=2 * tokens * depth * count * SIDE * part,
            bytes_accessed=2 * depth * (tokens + count * SIDE * part),
            transcendentals=0,
        ),
        name="forward",
    )(near, wide, *lines)


def backward_kernel(count, first, spots_ref, *refs):
    lines, grads = refs[:count], refs[count : count * 5]
    weights = jnp.concatenate([line[k] for line in lines for k in range(SIDE)], axis=1)
    cols = jnp.concatenate([g[...] for g in grads], axis=1)
    product = lax.dot_general(
        cols, weights, (((1,), (1,)), ((), ())), preferred_element_type=jnp.float32
    )
    refs[-1][...] = product if first else refs[-2][...] + product


def backward(spots, grown, out_grad, lines):
    tokens = out_grad.shape[0]
    depth, part = lines[0].shape[1:]
    count = len(lines)
    block = depth // 4
    first = grown is None

    def column(j):
        return pl.BlockSpec((tokens, part), lambda i, n: (0, n[j]))

    total = pl.BlockSpec((tokens, block), lambda i, n: (0, i))
    return pl.pallas_call(
        functools.partial(backward_kernel, count, first),
        out_shape=jax.ShapeDtypeStruct((tokens, depth), jnp.float32),
        grid_spec=pltpu.PrefetchScalarGridSpec(
            num_scalar_prefetch=1,
            grid=(4,),
            in_specs=[pl.BlockSpec((SIDE, block, part), lambda i, n: (0, i, 0))] * count
            + [column(j) for j in range(count * SIDE)]
            + ([] if first else [total]),
            out_specs=total,
        ),
        compiler_params=pltpu.CompilerParams(vmem_limit_bytes=40 << 20),
        cost_estimate=pl.CostEstimate(
            flops=2 * tokens * depth * count * SIDE * part,
            bytes_accessed=2 * depth * count * SIDE * part + 8 * tokens * depth,
            transcendentals=0,
        ),
        name="backward",
    )(spots, *lines, *([out_grad] * (count * SIDE)), *([] if first else [grown]))


def compose(logits, indices, vector_bank):
    weights = jax.nn.sigmoid(logits - logits[..., ::-1])
    levels = jnp.arange(vector_bank.shape[0], dtype=jnp.int32)
    picked = (indices[..., None] == levels).astype(jnp.float32)
    mixing = jnp.sum(picked * weights[..., None], axis=2)
    blocks = jnp.einsum("rjb,bc->rjc", mixing, vector_bank, precision=lax.Precision.HIGHEST)
    return (weights, picked, mixing, blocks.reshape(blocks.shape[0], -1))


def compose_back(grad_rows, weights, picked, mixing, vector_bank):
    blocks = grad_rows.reshape(mixing.shape[0], mixing.shape[1], -1)
    bank_part = jnp.einsum("rjb,rjc->bc", mixing, blocks, precision=lax.Precision.HIGHEST)
    projected = jnp.einsum("rjc,bc->rjb", blocks, vector_bank, precision=lax.Precision.HIGHEST)
    dots = jnp.sum(picked * projected[:, :, None, :], axis=3)
    logit_grad = weights * (dots - jnp.sum(weights * dots, axis=2, keepdims=True))
    return (bank_part, logit_grad)


def settle(piece, step, z, core):
    def from_second(parity):
        def move(x, z, y, c):
            if c == 1 and y % 2 == parity:
                return (x, z, (x + step) % SIDE, y // 2)
            return None

        return lax.ppermute(piece, BOTH, pairs(move))

    def move(x, z, y, c):
        return (x, z, y, 1) if c == 0 and (z + step) % SIDE >= 2 else None

    crossed = lax.ppermute(piece, BOTH, pairs(move))
    spot = (z + step) % SIDE
    first = jnp.where(core == 0, piece, crossed)
    first = jnp.where(spot // 2 == core, first, jnp.zeros_like(first))
    return first, spot % 2, [from_second(0), from_second(1)]


def local(attn_out, frozen_weight, vector_bank, logits_a, index_a, logits_b, index_b, out_grad):
    tokens, height = attn_out.shape
    shard = frozen_weight.shape[1]
    half, part = shard // 2, shard // 4
    f32, bf16 = jnp.float32, jnp.bfloat16
    dp, tensor = lax.axis_index("dp"), lax.axis_index("tensor")
    x, z, core = dp // SIDE, dp % SIDE, tensor % 2
    near, far = jnp.where(core == 0, x, z), jnp.where(core == 0, z, x)
    spot = near.astype(jnp.int32).reshape(1)

    left, right = frozen_weight[:, :half], frozen_weight[:, half:]
    mine = jnp.where(core == 0, left, right)
    theirs = jnp.where(core == 0, right, left)
    swapped = lax.ppermute(theirs, "tensor", SWAP)
    lines = []
    for h in range(2):
        cols = slice(h * part, (h + 1) * part)
        own = jnp.concatenate([mine[:, cols], swapped[:, cols]], axis=0)
        lines.append(jnp.stack(ring_gather(own, 0, h)))
    blocks = [ring_gather(lines[h], 1, h) for h in range(2)]

    def columns(i, h):
        far_at = (far + i) % SIDE
        spots = []
        for k in range(SIDE):
            near_at = (near + k) % SIDE
            x_at = jnp.where(core == 0, near_at, far_at)
            z_at = jnp.where(core == 0, far_at, near_at)
            spots.append((x_at * SIDE + z_at) * 4 + core * 2 + h)
        return spots

    def spots_of(chunks):
        return jnp.stack([s for i, h in chunks for s in columns(i, h)]).astype(jnp.int32)

    wide = jnp.concatenate([attn_out, lax.ppermute(attn_out, "tensor", SWAP)], axis=1)

    weights_a, picked_a, mixing_a, rows_a = compose(logits_a, index_a, vector_bank)
    weights_b, picked_b, mixing_b, rows_b = compose(logits_b, index_b, vector_bank)
    down_a, up_b = rows_a.astype(bf16), rows_b.astype(bf16)
    rank = down_a.shape[0]
    grad_cols = lax.dynamic_slice_in_dim(out_grad, tensor * height, height, 1)
    cols_by_cols = (((1,), (1,)), ((), ()))
    rows_by_rows = (((0,), (0,)), ((), ()))
    low_part = lax.dot_general(down_a, attn_out, cols_by_cols, preferred_element_type=f32)
    back_part = lax.dot_general(up_b, grad_cols, cols_by_cols, preferred_element_type=f32)
    totals = jnp.concatenate([low_part, back_part], axis=0)
    totals = over_tensor(after(totals, lines[0])).astype(bf16)
    low_bf, back_bf = totals[:rank], totals[rank:]

    factor = adapter_scale / (tokens * lax.axis_size("dp"))
    grad_a = jnp.dot(back_bf, attn_out, preferred_element_type=f32)
    grad_b = jnp.dot(low_bf, grad_cols, preferred_element_type=f32)
    both = over_dp(factor * jnp.concatenate([grad_a, grad_b], axis=0))
    bank_a, logit_grad_a = compose_back(both[:rank], weights_a, picked_a, mixing_a, vector_bank)
    bank_b, logit_grad_b = compose_back(both[rank:], weights_b, picked_b, mixing_b, vector_bank)
    bank_grad = over_tensor(bank_a + bank_b)

    here = [(0, 0), (0, 1)]
    beside = [(1, 0), (3, 0), (1, 1), (3, 1)]
    across = [(2, 0), (2, 1)]

    def take(chunks):
        return [blocks[h][i] for i, h in chunks]

    piece = lax.psum_scatter(
        forward(spot, wide, take(here)),
        "tensor",
        scatter_dimension=0,
        axis_index_groups=LANES,
        tiled=True,
    )[0]
    grown = backward(spots_of(here), None, out_grad, take(here))
    arrived = exchange(forward(spot, wide, take(beside)), "tensor", LANES)
    arrived = jnp.sum(arrived.astype(f32), axis=0).astype(bf16)
    above = jnp.concatenate([arrived[:, :part], arrived[:, 2 * part : 3 * part]], axis=1)
    below = jnp.concatenate([arrived[:, part : 2 * part], arrived[:, 3 * part :]], axis=1)
    grown = backward(spots_of(beside), grown, out_grad, take(beside))

    ordered = [piece, above, jnp.zeros_like(piece), below]
    slots = []
    for s in range(SIDE):
        turn = (s - far) % SIDE
        slots.append(
            jnp.where(turn == 0, piece, jnp.where(turn == 1, above, jnp.where(turn == 3, below, 0)))
        )
    slots = jnp.stack(slots).astype(bf16)
    moved = exchange(slots, "tensor", LANES)
    crossed = lax.ppermute(jnp.where(core == 0, slots[2:], moved[:2]), "tensor", SWAP)
    firsts = jnp.where(core == 0, slots[:2], crossed)
    seconds = jnp.where(core == 0, crossed, moved[2:])

    arrived = exchange(forward(spot, wide, take(across)), "tensor", LANES)
    piece = jnp.sum(arrived.astype(f32), axis=0).astype(bf16)
    grown = backward(spots_of(across), grown, out_grad, take(across))
    first, place, second = settle(piece, 2, z, core)
    cols = []
    for s in range(2):
        cols.append(firsts[s] + jnp.where(place == s, first, jnp.zeros_like(first)))
        cols.append(seconds[s] + second[s])
    summed = jnp.concatenate(cols, axis=1)
    layer_out = (
        summed.astype(f32)
        + adapter_scale * lax.dot_general(low_bf, up_b, rows_by_rows, preferred_element_type=f32)
    ).astype(bf16)
    other = lax.ppermute(grown[:, height:].astype(bf16), "tensor", SWAP)
    attn_grad = (
        grown[:, :height]
        + other.astype(f32)
        + adapter_scale * lax.dot_general(back_bf, down_a, rows_by_rows, preferred_element_type=f32)
    ).astype(bf16)
    return (layer_out, attn_grad, bank_grad, logit_grad_a, logit_grad_b)


def solution(mesh):
    return jax.shard_map(
        local,
        mesh=mesh,
        in_specs=(
            P("dp", "tensor"),
            P("tensor", "dp"),
            P(),
            P(None, "tensor", None),
            P(None, "tensor", None),
            P(None, "tensor", None),
            P(None, "tensor", None),
            P("dp", None),
        ),
        out_specs=(
            P("dp", "tensor"),
            P("dp", "tensor"),
            P(),
            P(None, "tensor", None),
            P(None, "tensor", None),
        ),
        check_vma=False,
    )
```

```python
import functools

import jax
import jax.numpy as jnp
from jax import lax
from jax.experimental import pallas as pl
from jax.experimental.pallas import tpu as pltpu
from jax.sharding import PartitionSpec as P

adapter_scale = 2.0
SIDE = 4
BOTH = ("dp", "tensor")
LANES = [[0, 2, 4, 6], [1, 3, 5, 7]]
SWAP = [(t, t ^ 1) for t in range(8)]


def device(x, z, y, c):
    return (x * SIDE + z) * 8 + y * 2 + c


def pairs(move):
    found = []
    for x in range(SIDE):
        for z in range(SIDE):
            for y in range(SIDE):
                for c in range(2):
                    to = move(x, z, y, c)
                    if to is not None:
                        found.append((device(x, z, y, c), device(*to)))
    return found


def ring(stage, step):
    def move(x, z, y, c):
        if (stage == 0) == (c == 0):
            return ((x + step) % SIDE, z, y, c)
        return (x, (z + step) % SIDE, y, c)

    return pairs(move)


def shift(value, stage, step):
    return lax.ppermute(value, BOTH, ring(stage, step))


def first_ring(own, h):
    below = shift(own, 0, 1)
    above = shift(own, 0, -1)
    across = shift(below, 0, 1) if h == 0 else shift(above, 0, -1)
    return [own, above, across, below]


def second_ring(own):
    below = shift(own, 1, 1)
    above = shift(own, 1, -1)
    passed = lax.optimization_barrier((below[:SIDE], above[SIDE:]))
    return above, below, passed, [shift(passed[0], 1, 1), shift(passed[1], 1, -1)]


def exchange(value, axis, groups=None):
    return lax.all_to_all(
        value, axis, split_axis=0, concat_axis=0, tiled=True, axis_index_groups=groups
    )


def over_tensor(value):
    value = value + lax.ppermute(value, "tensor", SWAP)
    value = value + lax.ppermute(value, "tensor", [(t, t ^ 2) for t in range(8)])
    return value + lax.ppermute(value, "tensor", [(t, t ^ 4) for t in range(8)])


def over_side(value, axis):
    def from_step(step):
        def move(x, z, y, c):
            if axis == 0:
                return ((x + step) % SIDE, z, y, c)
            return (x, (z + step) % SIDE, y, c)

        return lax.ppermute(value, BOTH, pairs(move))

    return [value, from_step(1), from_step(2), from_step(3)]


def total_of(parts):
    return (parts[0] + parts[2]) + (parts[1] + parts[3])


def after(value, *events):
    return lax.optimization_barrier((value, *events))[0]


def forward_kernel(offsets, near_ref, wide_ref, *refs):
    count = len(offsets)
    lines, outs, held, sems = refs[:count], refs[count:-2], refs[-2], refs[-1]
    copies = [
        pltpu.make_async_copy(lines[m].at[pl.ds(offsets[m], SIDE)], held.at[m], sems.at[m])
        for m in range(count)
    ]
    for copy in copies:
        copy.start()
    part = held.shape[3]
    for m in range(count):
        copies[m].wait()
        order = [lax.rem(near_ref[0] + k, SIDE) for k in range(SIDE)]
        weights = jnp.concatenate([held[m, k] for k in order], axis=1)
        product = jnp.dot(wide_ref[...], weights, preferred_element_type=jnp.float32)
        product = product.astype(jnp.bfloat16)
        for k in range(SIDE):
            piece = product[:, k * part : (k + 1) * part]
            if len(outs) == 1:
                outs[0][k, :, m * part : (m + 1) * part] = piece
            else:
                outs[k][:, m * part : (m + 1) * part] = piece


def forward(start, wide, lines, apart=False):
    tokens, depth = wide.shape
    part = lines[0][0].shape[2]
    count = len(lines)
    shape = (tokens, count * part) if apart else (SIDE, tokens, count * part)
    outs = jax.ShapeDtypeStruct(shape, jnp.bfloat16)
    spec = pl.BlockSpec(shape, lambda i, n: (0,) * len(shape))
    return pl.pallas_call(
        functools.partial(forward_kernel, [offset for _, offset in lines]),
        out_shape=[outs] * SIDE if apart else outs,
        grid_spec=pltpu.PrefetchScalarGridSpec(
            num_scalar_prefetch=1,
            grid=(1,),
            in_specs=[pl.BlockSpec((tokens, depth), lambda i, n: (0, 0))]
            + [pl.BlockSpec(memory_space=pl.ANY)] * count,
            out_specs=[spec] * SIDE if apart else spec,
            scratch_shapes=[
                pltpu.VMEM((count, SIDE, depth, part), jnp.bfloat16),
                pltpu.SemaphoreType.DMA((count,)),
            ],
        ),
        compiler_params=pltpu.CompilerParams(vmem_limit_bytes=28 << 20),
        cost_estimate=pl.CostEstimate(
            flops=tokens * depth * count * part,
            bytes_accessed=depth * part * count,
            transcendentals=0,
        ),
        name="forward",
    )(start, wide, *[line for line, _ in lines])


def arrange_kernel(far_ref, here_ref, beside_ref, out_ref):
    part = here_ref.shape[2] // 2
    far = far_ref[0]

    def total(ref, lane):
        parts = [ref[y, :, lane : lane + part].astype(jnp.float32) for y in range(SIDE)]
        return (parts[0] + parts[1] + parts[2] + parts[3]).astype(out_ref.dtype)

    for h in range(2):
        lanes = slice(h * part, (h + 1) * part)
        out_ref[far, :, lanes] = total(here_ref, h * part)
        out_ref[lax.rem(far + 1, SIDE), :, lanes] = total(beside_ref, 2 * h * part)
        out_ref[lax.rem(far + 3, SIDE), :, lanes] = total(beside_ref, (2 * h + 1) * part)
        out_ref[lax.rem(far + 2, SIDE), :, lanes] = jnp.zeros_like(here_ref[0, :, lanes])


def arrange(far, here, beside):
    tokens = here.shape[1]
    rows = tokens // 4
    return pl.pallas_call(
        arrange_kernel,
        out_shape=jax.ShapeDtypeStruct(here.shape, here.dtype),
        grid_spec=pltpu.PrefetchScalarGridSpec(
            num_scalar_prefetch=1,
            grid=(4,),
            in_specs=[
                pl.BlockSpec((SIDE, rows, here.shape[2]), lambda i, n: (0, i, 0)),
                pl.BlockSpec((SIDE, rows, beside.shape[2]), lambda i, n: (0, i, 0)),
            ],
            out_specs=pl.BlockSpec((SIDE, rows, here.shape[2]), lambda i, n: (0, i, 0)),
        ),
        compiler_params=pltpu.CompilerParams(vmem_limit_bytes=16 << 20),
        cost_estimate=pl.CostEstimate(
            flops=4 * here.size, bytes_accessed=2 * (2 * here.size + beside.size), transcendentals=0
        ),
        name="arrange",
    )(far, here, beside)


def backward_kernel(count, first, spots_ref, *refs):
    lines, grads = refs[:count], refs[count : count * 5]
    weights = jnp.concatenate([line[k] for line in lines for k in range(SIDE)], axis=1)
    cols = jnp.concatenate([g[...] for g in grads], axis=1)
    product = lax.dot_general(
        cols, weights, (((1,), (1,)), ((), ())), preferred_element_type=jnp.float32
    )
    refs[-1][...] = product if first else refs[-2][...] + product


def backward(spots, grown, out_grad, lines):
    tokens = out_grad.shape[0]
    depth, part = lines[0][0].shape[1:]
    count = len(lines)
    block = depth // 4
    first = grown is None

    def held(place):
        return pl.BlockSpec((SIDE, block, part), lambda i, n: (place, i, 0))

    def column(j):
        return pl.BlockSpec((tokens, part), lambda i, n: (0, n[j]))

    total = pl.BlockSpec((tokens, block), lambda i, n: (0, i))
    return pl.pallas_call(
        functools.partial(backward_kernel, count, first),
        out_shape=jax.ShapeDtypeStruct((tokens, depth), jnp.float32),
        grid_spec=pltpu.PrefetchScalarGridSpec(
            num_scalar_prefetch=1,
            grid=(4,),
            in_specs=[held(offset // SIDE) for _, offset in lines]
            + [column(j) for j in range(count * SIDE)]
            + ([] if first else [total]),
            out_specs=total,
        ),
        compiler_params=pltpu.CompilerParams(vmem_limit_bytes=28 << 20),
        cost_estimate=pl.CostEstimate(
            flops=tokens * depth * count * part,
            bytes_accessed=depth * part * count,
            transcendentals=0,
        ),
        name="backward",
    )(spots, *[line for line, _ in lines], *([out_grad] * (count * SIDE)), *([] if first else [grown]))


def compose(logits, indices, vector_bank):
    weights = jax.nn.sigmoid(logits - logits[..., ::-1])
    levels = jnp.arange(vector_bank.shape[0], dtype=jnp.int32)
    picked = (indices[..., None] == levels).astype(jnp.float32)
    mixing = jnp.sum(picked * weights[..., None], axis=2)
    blocks = jnp.einsum("rjb,bc->rjc", mixing, vector_bank, precision=lax.Precision.HIGHEST)
    return (weights, picked, mixing, blocks.reshape(blocks.shape[0], -1))


def compose_back(grad_rows, weights, picked, mixing, vector_bank):
    blocks = grad_rows.reshape(mixing.shape[0], mixing.shape[1], -1)
    bank_part = jnp.einsum("rjb,rjc->bc", mixing, blocks, precision=lax.Precision.HIGHEST)
    projected = jnp.einsum("rjc,bc->rjb", blocks, vector_bank, precision=lax.Precision.HIGHEST)
    dots = jnp.sum(picked * projected[:, :, None, :], axis=3)
    logit_grad = weights * (dots - jnp.sum(weights * dots, axis=2, keepdims=True))
    return (bank_part, logit_grad)


def settle(piece, step, z, core):
    def from_second(parity):
        def move(x, z, y, c):
            if c == 1 and y % 2 == parity:
                return (x, z, (x + step) % SIDE, y // 2)
            return None

        return lax.ppermute(piece, BOTH, pairs(move))

    def move(x, z, y, c):
        return (x, z, y, 1) if c == 0 and (z + step) % SIDE >= 2 else None

    crossed = lax.ppermute(piece, BOTH, pairs(move))
    spot = (z + step) % SIDE
    first = jnp.where(core == 0, piece, crossed)
    first = jnp.where(spot // 2 == core, first, jnp.zeros_like(first))
    return first, spot % 2, [from_second(0), from_second(1)]


def local(attn_out, frozen_weight, vector_bank, logits_a, index_a, logits_b, index_b, out_grad):
    tokens, height = attn_out.shape
    shard = frozen_weight.shape[1]
    half, part = shard // 2, shard // 4
    f32, bf16 = jnp.float32, jnp.bfloat16
    dp, tensor = lax.axis_index("dp"), lax.axis_index("tensor")
    x, z, core = dp // SIDE, dp % SIDE, tensor % 2
    near, far = jnp.where(core == 0, x, z), jnp.where(core == 0, z, x)
    side = tensor // 2
    turned = ((SIDE - near) % SIDE).astype(jnp.int32).reshape(1)
    turned_here = ((SIDE - near + side) % SIDE).astype(jnp.int32).reshape(1)

    left, right = frozen_weight[:, :half], frozen_weight[:, half:]
    mine = jnp.where(core == 0, left, right)
    theirs = jnp.where(core == 0, right, left)
    swapped = lax.ppermute(theirs, "tensor", SWAP)
    shards = []
    for h in range(2):
        cols = slice(h * part, (h + 1) * part)
        shards.append(jnp.concatenate([mine[:, cols], swapped[:, cols]], axis=0))
    logits_a, logits_b, *shards = lax.optimization_barrier((logits_a, logits_b, *shards))
    lines = first_ring(shards[0], 0) + first_ring(shards[1], 1)
    def columns(i, h):
        far_at = (far + i) % SIDE
        spots = []
        for k in range(SIDE):
            near_at = (near + k) % SIDE
            x_at = jnp.where(core == 0, near_at, far_at)
            z_at = jnp.where(core == 0, far_at, near_at)
            spots.append((x_at * SIDE + z_at) * 4 + core * 2 + h)
        return spots

    def spots_of(chunks):
        return jnp.stack([s for i, h in chunks for s in columns(i, h)]).astype(jnp.int32)

    wide = jnp.concatenate([attn_out, lax.ppermute(attn_out, "tensor", SWAP)], axis=1)

    weights_a, picked_a, mixing_a, rows_a = compose(logits_a, index_a, vector_bank)
    weights_b, picked_b, mixing_b, rows_b = compose(logits_b, index_b, vector_bank)
    down_a, up_b = rows_a.astype(bf16), rows_b.astype(bf16)
    rank = down_a.shape[0]
    grad_cols = lax.dynamic_slice_in_dim(out_grad, tensor * height, height, 1)
    cols_by_cols = (((1,), (1,)), ((), ()))
    rows_by_rows = (((0,), (0,)), ((), ()))
    low_part = lax.dot_general(down_a, attn_out, cols_by_cols, preferred_element_type=f32)
    back_part = lax.dot_general(up_b, grad_cols, cols_by_cols, preferred_element_type=f32)
    totals = jnp.concatenate([low_part, back_part], axis=0)
    own, totals = lax.optimization_barrier((jnp.stack(lines), totals))
    above, below, passed, corner = second_ring(own)
    blocks = [
        [(own, h * SIDE), (above, h * SIDE), (corner[h], 0), (below, h * SIDE)] for h in range(2)
    ]
    totals = over_tensor(totals).astype(bf16)
    low_bf, back_bf = totals[:rank], totals[rank:]

    factor = adapter_scale / (tokens * lax.axis_size("dp"))
    grad_a = jnp.dot(back_bf, attn_out, preferred_element_type=f32)
    grad_b = jnp.dot(low_bf, grad_cols, preferred_element_type=f32)
    both = factor * jnp.concatenate([grad_a, grad_b], axis=0)
    both_parts = over_side(both, 0)

    here = [(0, 0), (0, 1)]
    beside = [(1, 0), (3, 0), (1, 1), (3, 1)]
    across = [(2, 0), (2, 1)]

    def take(chunks):
        return [blocks[h][i] for i, h in chunks]

    sent_here = forward(turned, wide, take(here))
    slots_here = exchange(sent_here, "tensor", LANES)
    grown = backward(spots_of(here), None, out_grad, take(here))
    both = total_of(both_parts)
    turned, both, *_ = lax.optimization_barrier((turned, both, sent_here, grown, *passed))
    sent_beside = forward(turned, wide, take(beside))
    slots_here, sent_beside = lax.optimization_barrier((slots_here, sent_beside))
    slots_beside = exchange(sent_beside, "tensor", LANES)
    both_parts = over_side(both, 1)
    grown = backward(spots_of(beside), grown, out_grad, take(beside))
    both = total_of(lax.optimization_barrier((*both_parts, grown))[:SIDE])
    bank_a, logit_grad_a = compose_back(both[:rank], weights_a, picked_a, mixing_a, vector_bank)
    bank_b, logit_grad_b = compose_back(both[rank:], weights_b, picked_b, mixing_b, vector_bank)

    slots = arrange(far.astype(jnp.int32).reshape(1), slots_here, after(slots_beside, grown))
    moved = exchange(slots, "tensor", LANES)
    crossed = lax.ppermute(jnp.where(core == 0, slots[2:], moved[:2]), "tensor", SWAP)
    firsts = jnp.where(core == 0, slots[:2], crossed)
    seconds = jnp.where(core == 0, crossed, moved[2:])

    sent = forward(turned_here, wide, take(across), apart=True)
    arrived = [sent[0]]
    for step in range(1, SIDE):
        turns = [(t, (t + 2 * step) % 8) for t in range(8)]
        arrived.append(lax.ppermute(sent[step], "tensor", turns))
    piece = total_of([a.astype(f32) for a in arrived]).astype(bf16)
    bank_grad = over_tensor(after(bank_a + bank_b, *sent))
    grown = backward(after(spots_of(across), *sent), grown, out_grad, take(across))
    first, place, second = settle(piece, 2, z, core)
    cols = []
    for s in range(2):
        cols.append(firsts[s] + jnp.where(place == s, first, jnp.zeros_like(first)))
        cols.append(seconds[s] + second[s])
    summed = jnp.concatenate(cols, axis=1)
    layer_out = (
        summed.astype(f32)
        + adapter_scale * lax.dot_general(low_bf, up_b, rows_by_rows, preferred_element_type=f32)
    ).astype(bf16)
    other = lax.ppermute(grown[:, height:].astype(bf16), "tensor", SWAP)
    attn_grad = (
        grown[:, :height]
        + other.astype(f32)
        + adapter_scale * lax.dot_general(back_bf, down_a, rows_by_rows, preferred_element_type=f32)
    ).astype(bf16)
    return (layer_out, attn_grad, bank_grad, logit_grad_a, logit_grad_b)


def solution(mesh):
    return jax.shard_map(
        local,
        mesh=mesh,
        in_specs=(
            P("dp", "tensor"),
            P("tensor", "dp"),
            P(),
            P(None, "tensor", None),
            P(None, "tensor", None),
            P(None, "tensor", None),
            P(None, "tensor", None),
            P("dp", None),
        ),
        out_specs=(
            P("dp", "tensor"),
            P("dp", "tensor"),
            P(),
            P(None, "tensor", None),
            P(None, "tensor", None),
        ),
        check_vma=False,
    )
```

```python
import functools

import jax
import jax.numpy as jnp
from jax import lax
from jax.experimental import pallas as pl
from jax.experimental.pallas import tpu as pltpu
from jax.sharding import PartitionSpec as P

adapter_scale = 2.0
SIDE = 4
BOTH = ("dp", "tensor")
LANES = [[0, 2, 4, 6], [1, 3, 5, 7]]
SWAP = [(t, t ^ 1) for t in range(8)]


def device(x, z, y, c):
    return (x * SIDE + z) * 8 + y * 2 + c


def pairs(move):
    found = []
    for x in range(SIDE):
        for z in range(SIDE):
            for y in range(SIDE):
                for c in range(2):
                    to = move(x, z, y, c)
                    if to is not None:
                        found.append((device(x, z, y, c), device(*to)))
    return found


def ring(stage, step):
    def move(x, z, y, c):
        if (stage == 0) == (c == 0):
            return ((x + step) % SIDE, z, y, c)
        return (x, (z + step) % SIDE, y, c)

    return pairs(move)


def shift(value, stage, step):
    return lax.ppermute(value, BOTH, ring(stage, step))


def ring_gather(own, stage, h):
    below = shift(own, stage, 1)
    above = shift(own, stage, -1)
    across = shift(below, stage, 1) if h == 0 else shift(above, stage, -1)
    return [own, above, across, below]


def exchange(value, axis, groups=None):
    return lax.all_to_all(
        value, axis, split_axis=0, concat_axis=0, tiled=True, axis_index_groups=groups
    )


def over_tensor(value):
    value = value + lax.ppermute(value, "tensor", SWAP)
    value = value + lax.ppermute(value, "tensor", [(t, t ^ 2) for t in range(8)])
    return value + lax.ppermute(value, "tensor", [(t, t ^ 4) for t in range(8)])


def over_side(value, axis):
    def from_step(step):
        def move(x, z, y, c):
            if axis == 0:
                return ((x + step) % SIDE, z, y, c)
            return (x, (z + step) % SIDE, y, c)

        return lax.ppermute(value, BOTH, pairs(move))

    return [value, from_step(1), from_step(2), from_step(3)]


def total_of(parts):
    return (parts[0] + parts[2]) + (parts[1] + parts[3])


def after(value, *events):
    return lax.optimization_barrier((value, *events))[0]


def forward_kernel(count, start_ref, wide_ref, *refs):
    lines, outs, held, sems = refs[:count], refs[-6:-2], refs[-2], refs[-1]
    outs = refs[-3:-2] if len(refs) < count + 6 else outs
    copies = [pltpu.make_async_copy(lines[m], held.at[m], sems.at[m]) for m in range(count)]
    for copy in copies:
        copy.start()
    part = held.shape[3]
    order = [lax.rem(start_ref[0] + k, SIDE) for k in range(SIDE)]
    for m in range(count):
        copies[m].wait()
        weights = jnp.concatenate([held[m, k] for k in order], axis=1)
        product = jnp.dot(wide_ref[...], weights, preferred_element_type=jnp.float32)
        product = product.astype(jnp.bfloat16)
        for k in range(SIDE):
            piece = product[:, k * part : (k + 1) * part]
            if len(outs) == 1:
                outs[0][k, :, m * part : (m + 1) * part] = piece
            else:
                outs[k][:, m * part : (m + 1) * part] = piece


def forward(start, wide, lines, apart=False, places=1, into=None):
    tokens, depth = wide.shape
    part = lines[0].shape[2]
    count = len(lines)
    cols = count * part
    if apart:
        outs = [pltpu.HBM((tokens, cols), jnp.bfloat16)] * SIDE
        specs = [pl.BlockSpec((tokens, cols), lambda i, n: (0, 0))] * SIDE
    else:
        place = 0 if into is None else 1
        outs = pltpu.HBM((SIDE, tokens, places * cols), jnp.bfloat16)
        specs = pl.BlockSpec((SIDE, tokens, cols), lambda i, n: (0, 0, place))
    extra = [] if into is None else [into]
    return pl.pallas_call(
        functools.partial(forward_kernel, count),
        out_shape=outs,
        grid_spec=pltpu.PrefetchScalarGridSpec(
            num_scalar_prefetch=1,
            grid=(1,),
            in_specs=[pl.BlockSpec((tokens, depth), lambda i, n: (0, 0))]
            + [pl.BlockSpec(memory_space=pl.ANY)] * (count + len(extra)),
            out_specs=specs,
            scratch_shapes=[
                pltpu.VMEM((count, SIDE, depth, part), jnp.bfloat16),
                pltpu.SemaphoreType.DMA((count,)),
            ],
        ),
        input_output_aliases={} if into is None else {count + 2: 0},
        compiler_params=pltpu.CompilerParams(vmem_limit_bytes=28 << 20),
        cost_estimate=pl.CostEstimate(
            flops=tokens * depth * count * part,
            bytes_accessed=depth * part * count,
            transcendentals=0,
        ),
        name="forward",
    )(start, wide, *lines, *extra)


def arrange_kernel(far_ref, here_ref, beside_ref, out_ref):
    part = here_ref.shape[2] // 2
    far = far_ref[0]

    def total(ref, lane):
        parts = [ref[y, :, lane : lane + part].astype(jnp.float32) for y in range(SIDE)]
        return (parts[0] + parts[1] + parts[2] + parts[3]).astype(out_ref.dtype)

    for h in range(2):
        lanes = slice(h * part, (h + 1) * part)
        out_ref[far, :, lanes] = total(here_ref, h * part)
        out_ref[lax.rem(far + 1, SIDE), :, lanes] = total(beside_ref, 2 * h * part)
        out_ref[lax.rem(far + 3, SIDE), :, lanes] = total(beside_ref, (2 * h + 1) * part)
        out_ref[lax.rem(far + 2, SIDE), :, lanes] = jnp.zeros_like(here_ref[0, :, lanes])


def arrange(far, here, beside):
    tokens = here.shape[1]
    rows = tokens // 4
    return pl.pallas_call(
        arrange_kernel,
        out_shape=jax.ShapeDtypeStruct(here.shape, here.dtype),
        grid_spec=pltpu.PrefetchScalarGridSpec(
            num_scalar_prefetch=1,
            grid=(4,),
            in_specs=[
                pl.BlockSpec((SIDE, rows, here.shape[2]), lambda i, n: (0, i, 0)),
                pl.BlockSpec((SIDE, rows, beside.shape[2]), lambda i, n: (0, i, 0)),
            ],
            out_specs=pl.BlockSpec((SIDE, rows, here.shape[2]), lambda i, n: (0, i, 0)),
        ),
        compiler_params=pltpu.CompilerParams(vmem_limit_bytes=16 << 20),
        cost_estimate=pl.CostEstimate(
            flops=4 * here.size, bytes_accessed=2 * (2 * here.size + beside.size), transcendentals=0
        ),
        name="arrange",
    )(far, here, beside)


def backward_kernel(count, first, spots_ref, *refs):
    lines, grads = refs[:count], refs[count : count * 5]
    weights = jnp.concatenate([line[k] for line in lines for k in range(SIDE)], axis=1)
    cols = jnp.concatenate([g[...] for g in grads], axis=1)
    product = lax.dot_general(
        cols, weights, (((1,), (1,)), ((), ())), preferred_element_type=jnp.float32
    )
    refs[-1][...] = product if first else refs[-2][...] + product


def backward(spots, grown, out_grad, lines):
    tokens = out_grad.shape[0]
    depth, part = lines[0].shape[1:]
    count = len(lines)
    block = depth // 2
    first = grown is None

    def column(j):
        return pl.BlockSpec((tokens, part), lambda i, n: (0, n[j]))

    total = pl.BlockSpec((tokens, block), lambda i, n: (0, i))
    return pl.pallas_call(
        functools.partial(backward_kernel, count, first),
        out_shape=pltpu.HBM((tokens, depth), jnp.float32),
        grid_spec=pltpu.PrefetchScalarGridSpec(
            num_scalar_prefetch=1,
            grid=(2,),
            in_specs=[pl.BlockSpec((SIDE, block, part), lambda i, n: (0, i, 0))] * count
            + [column(j) for j in range(count * SIDE)]
            + ([] if first else [total]),
            out_specs=total,
        ),
        input_output_aliases={} if first else {5 * count + 1: 0},
        compiler_params=pltpu.CompilerParams(vmem_limit_bytes=36 << 20),
        cost_estimate=pl.CostEstimate(
            flops=tokens * depth * count * part,
            bytes_accessed=depth * part * count,
            transcendentals=0,
        ),
        name="backward",
    )(spots, *lines, *([pltpu.with_memory_space_constraint(out_grad, pltpu.HBM)] * (count * SIDE)), *([] if first else [grown]))


def compose(logits, indices, vector_bank):
    weights = jax.nn.sigmoid(logits - logits[..., ::-1])
    levels = jnp.arange(vector_bank.shape[0], dtype=jnp.int32)
    picked = (indices[..., None] == levels).astype(jnp.float32)
    mixing = jnp.sum(picked * weights[..., None], axis=2)
    blocks = jnp.einsum("rjb,bc->rjc", mixing, vector_bank, precision=lax.Precision.HIGHEST)
    return (weights, picked, mixing, blocks.reshape(blocks.shape[0], -1))


def compose_back(grad_rows, weights, picked, mixing, vector_bank):
    blocks = grad_rows.reshape(mixing.shape[0], mixing.shape[1], -1)
    bank_part = jnp.einsum("rjb,rjc->bc", mixing, blocks, precision=lax.Precision.HIGHEST)
    projected = jnp.einsum("rjc,bc->rjb", blocks, vector_bank, precision=lax.Precision.HIGHEST)
    dots = jnp.sum(picked * projected[:, :, None, :], axis=3)
    logit_grad = weights * (dots - jnp.sum(weights * dots, axis=2, keepdims=True))
    return (bank_part, logit_grad)


def settle(piece, step, z, core):
    def from_second(parity):
        def move(x, z, y, c):
            if c == 1 and y % 2 == parity:
                return (x, z, (x + step) % SIDE, y // 2)
            return None

        return lax.ppermute(piece, BOTH, pairs(move))

    def move(x, z, y, c):
        return (x, z, y, 1) if c == 0 and (z + step) % SIDE >= 2 else None

    crossed = lax.ppermute(piece, BOTH, pairs(move))
    spot = (z + step) % SIDE
    first = jnp.where(core == 0, piece, crossed)
    first = jnp.where(spot // 2 == core, first, jnp.zeros_like(first))
    return first, spot % 2, [from_second(0), from_second(1)]


def local(attn_out, frozen_weight, vector_bank, logits_a, index_a, logits_b, index_b, out_grad):
    tokens, height = attn_out.shape
    shard = frozen_weight.shape[1]
    half, part = shard // 2, shard // 4
    f32, bf16 = jnp.float32, jnp.bfloat16
    dp, tensor = lax.axis_index("dp"), lax.axis_index("tensor")
    x, z, core = dp // SIDE, dp % SIDE, tensor % 2
    near, far = jnp.where(core == 0, x, z), jnp.where(core == 0, z, x)
    side = tensor // 2
    turned = ((SIDE - near) % SIDE).astype(jnp.int32).reshape(1)
    turned_here = ((SIDE - near + side) % SIDE).astype(jnp.int32).reshape(1)

    left, right = frozen_weight[:, :half], frozen_weight[:, half:]
    mine = jnp.where(core == 0, left, right)
    theirs = jnp.where(core == 0, right, left)
    swapped = lax.ppermute(theirs, "tensor", SWAP)
    shards = []
    for h in range(2):
        cols = slice(h * part, (h + 1) * part)
        shards.append(jnp.concatenate([mine[:, cols], swapped[:, cols]], axis=0))
    logits_a, logits_b, *shards = lax.optimization_barrier((logits_a, logits_b, *shards))
    lines = [jnp.stack(ring_gather(shards[h], 0, h)) for h in range(2)]
    def columns(i, h):
        far_at = (far + i) % SIDE
        spots = []
        for k in range(SIDE):
            near_at = (near + k) % SIDE
            x_at = jnp.where(core == 0, near_at, far_at)
            z_at = jnp.where(core == 0, far_at, near_at)
            spots.append((x_at * SIDE + z_at) * 4 + core * 2 + h)
        return spots

    def spots_of(chunks):
        return jnp.stack([s for i, h in chunks for s in columns(i, h)]).astype(jnp.int32)

    wide = jnp.concatenate([attn_out, lax.ppermute(attn_out, "tensor", SWAP)], axis=1)

    weights_a, picked_a, mixing_a, rows_a = compose(logits_a, index_a, vector_bank)
    weights_b, picked_b, mixing_b, rows_b = compose(logits_b, index_b, vector_bank)
    down_a, up_b = rows_a.astype(bf16), rows_b.astype(bf16)
    rank = down_a.shape[0]
    grad_cols = lax.dynamic_slice_in_dim(out_grad, tensor * height, height, 1)
    cols_by_cols = (((1,), (1,)), ((), ()))
    rows_by_rows = (((0,), (0,)), ((), ()))
    low_part = lax.dot_general(down_a, attn_out, cols_by_cols, preferred_element_type=f32)
    back_part = lax.dot_general(up_b, grad_cols, cols_by_cols, preferred_element_type=f32)
    totals = jnp.concatenate([low_part, back_part], axis=0)
    lines[1], totals = lax.optimization_barrier((lines[1], totals))
    blocks = [ring_gather(lines[h], 1, h) for h in range(2)]
    totals = over_tensor(totals).astype(bf16)
    low_bf, back_bf = totals[:rank], totals[rank:]

    factor = adapter_scale / (tokens * lax.axis_size("dp"))
    grad_a = jnp.dot(back_bf, attn_out, preferred_element_type=f32)
    grad_b = jnp.dot(low_bf, grad_cols, preferred_element_type=f32)
    both = factor * jnp.concatenate([grad_a, grad_b], axis=0)
    both_parts = over_side(both, 0)

    here = [(0, 0), (0, 1)]
    beside = [(1, 0), (3, 0), (1, 1), (3, 1)]
    across = [(2, 0), (2, 1)]

    def take(chunks):
        return [blocks[h][i] for i, h in chunks]

    sent_here = forward(turned, wide, take(here))
    slots_here = exchange(sent_here, "tensor", LANES)
    grown = backward(after(spots_of(here), sent_here), None, out_grad, take(here))
    sent_beside = forward(after(turned, grown), wide, take(beside[:2]), places=2)
    sent_beside = forward(turned, wide, take(beside[2:]), places=2, into=sent_beside)
    slots_here, sent_beside, *both_parts = lax.optimization_barrier(
        (slots_here, sent_beside, *both_parts)
    )
    slots_beside = exchange(sent_beside, "tensor", LANES)
    both_parts = over_side(total_of(both_parts), 1)
    grown = backward(after(spots_of(beside), sent_beside), grown, out_grad, take(beside))
    sent = forward(after(turned_here, grown), wide, take(across), apart=True)
    slots_beside, *both_parts = lax.optimization_barrier((slots_beside, *both_parts, *sent))[:5]
    both = total_of(both_parts)
    bank_a, logit_grad_a = compose_back(both[:rank], weights_a, picked_a, mixing_a, vector_bank)
    bank_b, logit_grad_b = compose_back(both[rank:], weights_b, picked_b, mixing_b, vector_bank)

    slots = arrange(far.astype(jnp.int32).reshape(1), slots_here, slots_beside)
    moved = exchange(slots, "tensor", LANES)
    crossed = lax.ppermute(jnp.where(core == 0, slots[2:], moved[:2]), "tensor", SWAP)
    firsts = jnp.where(core == 0, slots[:2], crossed)
    seconds = jnp.where(core == 0, crossed, moved[2:])

    arrived = [sent[0]]
    for step in range(1, SIDE):
        turns = [(t, (t + 2 * step) % 8) for t in range(8)]
        arrived.append(lax.ppermute(sent[step], "tensor", turns))
    piece = total_of([a.astype(f32) for a in arrived]).astype(bf16)
    bank_grad = over_tensor(bank_a + bank_b)
    grown = backward(after(spots_of(across), slots), grown, out_grad, take(across))
    first, place, second = settle(piece, 2, z, core)
    cols = []
    for s in range(2):
        cols.append(firsts[s] + jnp.where(place == s, first, jnp.zeros_like(first)))
        cols.append(seconds[s] + second[s])
    summed = jnp.concatenate(cols, axis=1)
    layer_out = (
        summed.astype(f32)
        + adapter_scale * lax.dot_general(low_bf, up_b, rows_by_rows, preferred_element_type=f32)
    ).astype(bf16)
    other = lax.ppermute(grown[:, height:].astype(bf16), "tensor", SWAP)
    attn_grad = (
        grown[:, :height]
        + other.astype(f32)
        + adapter_scale * lax.dot_general(back_bf, down_a, rows_by_rows, preferred_element_type=f32)
    ).astype(bf16)
    return (layer_out, attn_grad, bank_grad, logit_grad_a, logit_grad_b)


def solution(mesh):
    return jax.shard_map(
        local,
        mesh=mesh,
        in_specs=(
            P("dp", "tensor"),
            P("tensor", "dp"),
            P(),
            P(None, "tensor", None),
            P(None, "tensor", None),
            P(None, "tensor", None),
            P(None, "tensor", None),
            P("dp", None),
        ),
        out_specs=(
            P("dp", "tensor"),
            P("dp", "tensor"),
            P(),
            P(None, "tensor", None),
            P(None, "tensor", None),
        ),
        check_vma=False,
    )
```

```python
import functools

import jax
import jax.numpy as jnp
from jax import lax
from jax.experimental import pallas as pl
from jax.experimental.pallas import tpu as pltpu
from jax.sharding import PartitionSpec as P

adapter_scale = 2.0
SIDE = 4
BOTH = ("dp", "tensor")
LANES = [[0, 2, 4, 6], [1, 3, 5, 7]]
SWAP = [(t, t ^ 1) for t in range(8)]


def device(x, z, y, c):
    return (x * SIDE + z) * 8 + y * 2 + c


def pairs(move):
    found = []
    for x in range(SIDE):
        for z in range(SIDE):
            for y in range(SIDE):
                for c in range(2):
                    to = move(x, z, y, c)
                    if to is not None:
                        found.append((device(x, z, y, c), device(*to)))
    return found


def ring(stage, step):
    def move(x, z, y, c):
        if (stage == 0) == (c == 0):
            return ((x + step) % SIDE, z, y, c)
        return (x, (z + step) % SIDE, y, c)

    return pairs(move)


def shift(value, stage, step):
    return lax.ppermute(value, BOTH, ring(stage, step))


def ring_gather(own, stage, h):
    below = shift(own, stage, 1)
    above = shift(own, stage, -1)
    across = shift(below, stage, 1) if h == 0 else shift(above, stage, -1)
    return [own, above, across, below]


def exchange(value, axis, groups=None):
    return lax.all_to_all(
        value, axis, split_axis=0, concat_axis=0, tiled=True, axis_index_groups=groups
    )


def over_tensor(value):
    value = value + lax.ppermute(value, "tensor", SWAP)
    value = value + lax.ppermute(value, "tensor", [(t, t ^ 2) for t in range(8)])
    return value + lax.ppermute(value, "tensor", [(t, t ^ 4) for t in range(8)])


def after(value, *events):
    return lax.optimization_barrier((value, *events))[0]


def with_partner(value, bit, *events):
    other = lax.ppermute(value, "dp", [(d, d ^ bit) for d in range(16)])
    return value + after(other, *events)


def total_of(parts):
    return (parts[0] + parts[2]) + (parts[1] + parts[3])


def forward_kernel(count, many, start_ref, wide_ref, *refs):
    lines, outs, held, sems = refs[:count], refs[-2 - many : -2], refs[-2], refs[-1]
    copies = [pltpu.make_async_copy(lines[m], held.at[m], sems.at[m]) for m in range(count)]
    part = held.shape[3]
    order = [lax.rem(start_ref[0] + k, SIDE) for k in range(SIDE)]

    @pl.when(pl.program_id(0) == 0)
    def _():
        for copy in copies:
            copy.start()

    for m in range(count):

        @pl.when(pl.program_id(0) == m)
        def _():
            copies[m].wait()
            weights = jnp.concatenate([held[m, k] for k in order], axis=1)
            product = jnp.dot(wide_ref[...], weights, preferred_element_type=jnp.float32)
            product = product.astype(jnp.bfloat16)
            for k in range(SIDE):
                piece = product[:, k * part : (k + 1) * part]
                if many == 1:
                    outs[0][k] = piece
                else:
                    outs[k][...] = piece


def forward(start, wide, lines, apart=False, places=1, into=None):
    tokens, depth = wide.shape
    part = lines[0].shape[2]
    count = len(lines)
    cols = count * part
    many = SIDE if apart else 1
    if apart:
        outs = [pltpu.HBM((tokens, cols), jnp.bfloat16)] * SIDE
        specs = [pl.BlockSpec((tokens, part), lambda i, n: (0, i))] * SIDE
    else:
        place = 0 if into is None else count
        outs = [pltpu.HBM((SIDE, tokens, places * cols), jnp.bfloat16)]
        specs = [pl.BlockSpec((SIDE, tokens, part), lambda i, n: (0, 0, place + i))]
    extra = [] if into is None else [into]
    made = pl.pallas_call(
        functools.partial(forward_kernel, count, many),
        out_shape=outs,
        grid_spec=pltpu.PrefetchScalarGridSpec(
            num_scalar_prefetch=1,
            grid=(count,),
            in_specs=[pl.BlockSpec(memory_space=pltpu.VMEM)]
            + [pl.BlockSpec(memory_space=pl.ANY)] * (count + len(extra)),
            out_specs=specs,
            scratch_shapes=[
                pltpu.VMEM((count, SIDE, depth, part), jnp.bfloat16),
                pltpu.SemaphoreType.DMA((count,)),
            ],
        ),
        input_output_aliases={} if into is None else {count + 2: 0},
        compiler_params=pltpu.CompilerParams(vmem_limit_bytes=24 << 20),
        cost_estimate=pl.CostEstimate(
            flops=tokens * depth * count * part,
            bytes_accessed=depth * part * count,
            transcendentals=0,
        ),
        name="forward",
    )(start, wide, *lines, *extra)
    return made if apart else made[0]


def arrange_kernel(far_ref, here_ref, beside_ref, out_ref):
    part = here_ref.shape[2] // 2
    far = far_ref[0]

    def total(ref, lane):
        parts = [ref[y, :, lane : lane + part].astype(jnp.float32) for y in range(SIDE)]
        return (parts[0] + parts[1] + parts[2] + parts[3]).astype(out_ref.dtype)

    for h in range(2):
        lanes = slice(h * part, (h + 1) * part)
        out_ref[far, :, lanes] = total(here_ref, h * part)
        out_ref[lax.rem(far + 1, SIDE), :, lanes] = total(beside_ref, 2 * h * part)
        out_ref[lax.rem(far + 3, SIDE), :, lanes] = total(beside_ref, (2 * h + 1) * part)
        out_ref[lax.rem(far + 2, SIDE), :, lanes] = jnp.zeros_like(here_ref[0, :, lanes])


def arrange(far, here, beside):
    tokens = here.shape[1]
    rows = tokens // 4
    return pl.pallas_call(
        arrange_kernel,
        out_shape=jax.ShapeDtypeStruct(here.shape, here.dtype),
        grid_spec=pltpu.PrefetchScalarGridSpec(
            num_scalar_prefetch=1,
            grid=(4,),
            in_specs=[
                pl.BlockSpec((SIDE, rows, here.shape[2]), lambda i, n: (0, i, 0)),
                pl.BlockSpec((SIDE, rows, beside.shape[2]), lambda i, n: (0, i, 0)),
            ],
            out_specs=pl.BlockSpec((SIDE, rows, here.shape[2]), lambda i, n: (0, i, 0)),
        ),
        compiler_params=pltpu.CompilerParams(vmem_limit_bytes=16 << 20),
        cost_estimate=pl.CostEstimate(
            flops=4 * here.size, bytes_accessed=2 * (2 * here.size + beside.size), transcendentals=0
        ),
        name="arrange",
    )(far, here, beside)


def backward_kernel(count, first, last, spots_ref, *refs):
    lines, grads = refs[:count], refs[count : count * 5]
    weights = jnp.concatenate([line[k] for line in lines for k in range(SIDE)], axis=1)
    cols = jnp.concatenate([g[...] for g in grads], axis=1)
    product = lax.dot_general(
        cols, weights, (((1,), (1,)), ((), ())), preferred_element_type=jnp.float32
    )
    if first:
        refs[-1][...] = product
    elif not last:
        refs[-1][...] = refs[-2][...] + product
    else:
        total = refs[-3][...] + product

        @pl.when(pl.program_id(0) < 2)
        def _():
            refs[-1][...] = total.astype(jnp.bfloat16)

        @pl.when(pl.program_id(0) >= 2)
        def _():
            refs[-2][...] = total


def backward(spots, grown, out_grad, lines, last=False):
    tokens = out_grad.shape[0]
    depth, part = lines[0].shape[1:]
    count = len(lines)
    block = depth // 4
    first = grown is None
    out_grad = pltpu.with_memory_space_constraint(out_grad, pltpu.HBM)

    def column(j):
        return pl.BlockSpec((tokens, part), lambda i, n: (0, n[j]))

    total = pl.BlockSpec((tokens, block), lambda i, n: (0, (i + 2) % 4))
    outs, specs = [pltpu.HBM((tokens, depth), jnp.float32)], [total]
    if last:
        outs = [
            jax.ShapeDtypeStruct((tokens, depth // 2), jnp.float32),
            jax.ShapeDtypeStruct((tokens, depth // 2), jnp.bfloat16),
        ]
        specs = [
            pl.BlockSpec((tokens, block), lambda i, n: (0, jnp.maximum(i - 2, 0))),
            pl.BlockSpec((tokens, block), lambda i, n: (0, jnp.minimum(i, 1))),
        ]
    made = pl.pallas_call(
        functools.partial(backward_kernel, count, first, last),
        out_shape=outs,
        grid_spec=pltpu.PrefetchScalarGridSpec(
            num_scalar_prefetch=1,
            grid=(4,),
            in_specs=[pl.BlockSpec((SIDE, block, part), lambda i, n: (0, (i + 2) % 4, 0))] * count
            + [column(j) for j in range(count * SIDE)]
            + ([] if first else [total]),
            out_specs=specs,
        ),
        input_output_aliases={} if first or last else {5 * count + 1: 0},
        compiler_params=pltpu.CompilerParams(vmem_limit_bytes=28 << 20),
        cost_estimate=pl.CostEstimate(
            flops=tokens * depth * count * part,
            bytes_accessed=depth * part * count,
            transcendentals=0,
        ),
        name="backward",
    )(spots, *lines, *([out_grad] * (count * SIDE)), *([] if first else [pltpu.with_memory_space_constraint(grown, pltpu.HBM)]))
    return made if last else made[0]


def compose(logits, indices, vector_bank):
    weights = jax.nn.sigmoid(logits - logits[..., ::-1])
    levels = jnp.arange(vector_bank.shape[0], dtype=jnp.int32)
    picked = (indices[..., None] == levels).astype(jnp.float32)
    mixing = jnp.sum(picked * weights[..., None], axis=2)
    blocks = jnp.einsum("rjb,bc->rjc", mixing, vector_bank, precision=lax.Precision.HIGHEST)
    return (weights, picked, mixing, blocks.reshape(blocks.shape[0], -1))


def compose_back(grad_rows, weights, picked, mixing, vector_bank):
    blocks = grad_rows.reshape(mixing.shape[0], mixing.shape[1], -1)
    bank_part = jnp.einsum("rjb,rjc->bc", mixing, blocks, precision=lax.Precision.HIGHEST)
    projected = jnp.einsum("rjc,bc->rjb", blocks, vector_bank, precision=lax.Precision.HIGHEST)
    dots = jnp.sum(picked * projected[:, :, None, :], axis=3)
    logit_grad = weights * (dots - jnp.sum(weights * dots, axis=2, keepdims=True))
    return (bank_part, logit_grad)


def settle(piece, step, z, core):
    def from_second(parity):
        def move(x, z, y, c):
            if c == 1 and y % 2 == parity:
                return (x, z, (x + step) % SIDE, y // 2)
            return None

        return lax.ppermute(piece, BOTH, pairs(move))

    def move(x, z, y, c):
        return (x, z, y, 1) if c == 0 and (z + step) % SIDE >= 2 else None

    crossed = lax.ppermute(piece, BOTH, pairs(move))
    spot = (z + step) % SIDE
    first = jnp.where(core == 0, piece, crossed)
    first = jnp.where(spot // 2 == core, first, jnp.zeros_like(first))
    return first, spot % 2, [from_second(0), from_second(1)]


def local(attn_out, frozen_weight, vector_bank, logits_a, index_a, logits_b, index_b, out_grad):
    tokens, height = attn_out.shape
    shard = frozen_weight.shape[1]
    half, part = shard // 2, shard // 4
    f32, bf16 = jnp.float32, jnp.bfloat16
    dp, tensor = lax.axis_index("dp"), lax.axis_index("tensor")
    x, z, core = dp // SIDE, dp % SIDE, tensor % 2
    near, far = jnp.where(core == 0, x, z), jnp.where(core == 0, z, x)
    side = tensor // 2
    turned = ((SIDE - near) % SIDE).astype(jnp.int32).reshape(1)
    turned_here = ((SIDE - near + side) % SIDE).astype(jnp.int32).reshape(1)

    left, right = frozen_weight[:, :half], frozen_weight[:, half:]
    mine = jnp.where(core == 0, left, right)
    theirs = jnp.where(core == 0, right, left)
    swapped = lax.ppermute(theirs, "tensor", SWAP)
    shards = []
    for h in range(2):
        cols = slice(h * part, (h + 1) * part)
        shards.append(jnp.concatenate([mine[:, cols], swapped[:, cols]], axis=0))
    logits_a, logits_b, *shards = lax.optimization_barrier((logits_a, logits_b, *shards))
    lines = [ring_gather(shards[h], 0, h) for h in range(2)]
    lines[0] = jnp.stack(lines[0])
    lines[0], *lines[1] = lax.optimization_barrier((lines[0], *lines[1]))
    lines[1] = jnp.stack(lines[1])
    def columns(i, h):
        far_at = (far + i) % SIDE
        spots = []
        for k in range(SIDE):
            near_at = (near + k) % SIDE
            x_at = jnp.where(core == 0, near_at, far_at)
            z_at = jnp.where(core == 0, far_at, near_at)
            spots.append((x_at * SIDE + z_at) * 4 + core * 2 + h)
        return spots

    def spots_of(chunks):
        return jnp.stack([s for i, h in chunks for s in columns(i, h)]).astype(jnp.int32)

    wide = jnp.concatenate([attn_out, lax.ppermute(attn_out, "tensor", SWAP)], axis=1)

    weights_a, picked_a, mixing_a, rows_a = compose(logits_a, index_a, vector_bank)
    weights_b, picked_b, mixing_b, rows_b = compose(logits_b, index_b, vector_bank)
    down_a, up_b = rows_a.astype(bf16), rows_b.astype(bf16)
    rank = down_a.shape[0]
    grad_cols = lax.dynamic_slice_in_dim(out_grad, tensor * height, height, 1)
    cols_by_cols = (((1,), (1,)), ((), ()))
    rows_by_rows = (((0,), (0,)), ((), ()))
    low_part = lax.dot_general(down_a, attn_out, cols_by_cols, preferred_element_type=f32)
    back_part = lax.dot_general(up_b, grad_cols, cols_by_cols, preferred_element_type=f32)
    totals = jnp.concatenate([low_part, back_part], axis=0)
    lines[1], totals = lax.optimization_barrier((lines[1], totals))
    blocks = [ring_gather(lines[h], 1, h) for h in range(2)]
    totals = over_tensor(totals).astype(bf16)
    low_bf, back_bf = totals[:rank], totals[rank:]

    factor = adapter_scale / (tokens * lax.axis_size("dp"))
    grad_a = jnp.dot(back_bf, attn_out, preferred_element_type=f32)
    grad_b = jnp.dot(low_bf, grad_cols, preferred_element_type=f32)
    both = factor * jnp.concatenate([grad_a, grad_b], axis=0)
    both = with_partner(both, 1)

    here = [(0, 0), (0, 1)]
    beside = [(1, 0), (3, 0), (1, 1), (3, 1)]
    across = [(2, 0), (2, 1)]

    def take(chunks):
        return [blocks[h][i] for i, h in chunks]

    sent_here = forward(turned, wide, take(here))
    slots_here = exchange(sent_here, "tensor", LANES)
    grown = backward(after(spots_of(here), sent_here), None, out_grad, take(here))
    sent_beside = forward(after(turned, grown), wide, take(beside[:2]), places=2)
    sent_beside = forward(
        after(turned, both, sent_beside), wide, take(beside[2:]), places=2, into=sent_beside
    )
    slots_here, sent_beside = lax.optimization_barrier((slots_here, sent_beside))
    slots_beside = exchange(sent_beside, "tensor", LANES)
    both = with_partner(both, 4, sent_beside)
    grown = backward(after(spots_of(beside), both), grown, out_grad, take(beside))
    both = with_partner(both, 2, grown)
    sent = forward(after(turned_here, both), wide, take(across), apart=True)
    both = with_partner(both, 8, *sent)
    slots_beside = after(slots_beside, *sent)
    slots = arrange(far.astype(jnp.int32).reshape(1), slots_here, slots_beside)
    moved = exchange(slots, "tensor", LANES)
    both = after(both, slots)
    bank_a, logit_grad_a = compose_back(both[:rank], weights_a, picked_a, mixing_a, vector_bank)
    bank_b, logit_grad_b = compose_back(both[rank:], weights_b, picked_b, mixing_b, vector_bank)
    crossed = lax.ppermute(jnp.where(core == 0, slots[2:], moved[:2]), "tensor", SWAP)
    firsts = jnp.where(core == 0, slots[:2], crossed)
    seconds = jnp.where(core == 0, crossed, moved[2:])

    arrived = [sent[0]]
    for step in range(1, SIDE):
        turns = [(t, (t + 2 * step) % 8) for t in range(8)]
        arrived.append(lax.ppermute(sent[step], "tensor", turns))
    piece = total_of([a.astype(f32) for a in arrived]).astype(bf16)
    bank_grad = over_tensor(bank_a + bank_b)
    grown, other = backward(
        after(spots_of(across), slots), grown, out_grad, take(across), last=True
    )
    first, place, second = settle(piece, 2, z, core)
    cols = []
    for s in range(2):
        cols.append(firsts[s] + jnp.where(place == s, first, jnp.zeros_like(first)))
        cols.append(seconds[s] + second[s])
    summed = jnp.concatenate(cols, axis=1)
    layer_out = (
        summed.astype(f32)
        + adapter_scale * lax.dot_general(low_bf, up_b, rows_by_rows, preferred_element_type=f32)
    ).astype(bf16)
    other = lax.ppermute(other, "tensor", SWAP)
    attn_grad = (
        grown
        + other.astype(f32)
        + adapter_scale * lax.dot_general(back_bf, down_a, rows_by_rows, preferred_element_type=f32)
    ).astype(bf16)
    return (layer_out, attn_grad, bank_grad, logit_grad_a, logit_grad_b)


def solution(mesh):
    return jax.shard_map(
        local,
        mesh=mesh,
        in_specs=(
            P("dp", "tensor"),
            P("tensor", "dp"),
            P(),
            P(None, "tensor", None),
            P(None, "tensor", None),
            P(None, "tensor", None),
            P(None, "tensor", None),
            P("dp", None),
        ),
        out_specs=(
            P("dp", "tensor"),
            P("dp", "tensor"),
            P(),
            P(None, "tensor", None),
            P(None, "tensor", None),
        ),
        check_vma=False,
    )
```

```python
import functools

import jax
import jax.numpy as jnp
from jax import lax
from jax.experimental import pallas as pl
from jax.experimental.pallas import tpu as pltpu
from jax.sharding import PartitionSpec as P

adapter_scale = 2.0
SIDE = 4
BOTH = ("dp", "tensor")
LANES = [[0, 2, 4, 6], [1, 3, 5, 7]]
SWAP = [(t, t ^ 1) for t in range(8)]


def device(x, z, y, c):
    return (x * SIDE + z) * 8 + y * 2 + c


def pairs(move):
    found = []
    for x in range(SIDE):
        for z in range(SIDE):
            for y in range(SIDE):
                for c in range(2):
                    to = move(x, z, y, c)
                    if to is not None:
                        found.append((device(x, z, y, c), device(*to)))
    return found


def ring(stage, step):
    def move(x, z, y, c):
        if (stage == 0) == (c == 0):
            return ((x + step) % SIDE, z, y, c)
        return (x, (z + step) % SIDE, y, c)

    return pairs(move)


def shift(value, stage, step):
    return lax.ppermute(value, BOTH, ring(stage, step))


def ring_gather(own, stage, h):
    below = shift(own, stage, 1)
    above = shift(own, stage, -1)
    across = shift(below, stage, 1) if h == 0 else shift(above, stage, -1)
    return [own, above, across, below]


def exchange(value, axis, groups=None):
    return lax.all_to_all(
        value, axis, split_axis=0, concat_axis=0, tiled=True, axis_index_groups=groups
    )


def over_tensor(value):
    value = value + lax.ppermute(value, "tensor", SWAP)
    value = value + lax.ppermute(value, "tensor", [(t, t ^ 2) for t in range(8)])
    return value + lax.ppermute(value, "tensor", [(t, t ^ 4) for t in range(8)])


def after(value, *events):
    return lax.optimization_barrier((value, *events))[0]


def over_side(value, axis):
    def from_step(step):
        def move(x, z, y, c):
            if axis == 0:
                return ((x + step) % SIDE, z, y, c)
            return (x, (z + step) % SIDE, y, c)

        return lax.ppermute(value, BOTH, pairs(move))

    return [value, from_step(1), from_step(2), from_step(3)]


def total_of(parts):
    return (parts[0] + parts[2]) + (parts[1] + parts[3])


def forward_kernel(count, many, start_ref, wide_ref, *refs):
    lines, outs, held, sems = refs[:count], refs[-2 - many : -2], refs[-2], refs[-1]
    copies = [pltpu.make_async_copy(lines[m], held.at[m], sems.at[m]) for m in range(count)]
    part = held.shape[3]
    order = [lax.rem(start_ref[0] + k, SIDE) for k in range(SIDE)]

    @pl.when(pl.program_id(0) == 0)
    def _():
        for copy in copies:
            copy.start()

    for m in range(count):

        @pl.when(pl.program_id(0) == m)
        def _():
            copies[m].wait()
            weights = jnp.concatenate([held[m, k] for k in order], axis=1)
            product = jnp.dot(wide_ref[...], weights, preferred_element_type=jnp.float32)
            product = product.astype(jnp.bfloat16)
            for k in range(SIDE):
                piece = product[:, k * part : (k + 1) * part]
                if many == 1:
                    outs[0][k] = piece
                else:
                    outs[k][...] = piece


def forward(start, wide, lines, apart=False, places=1, into=None):
    tokens, depth = wide.shape
    part = lines[0].shape[2]
    count = len(lines)
    cols = count * part
    many = SIDE if apart else 1
    if apart:
        outs = [pltpu.HBM((tokens, cols), jnp.bfloat16)] * SIDE
        specs = [pl.BlockSpec((tokens, part), lambda i, n: (0, i))] * SIDE
    else:
        place = 0 if into is None else count
        outs = [pltpu.HBM((SIDE, tokens, places * cols), jnp.bfloat16)]
        specs = [pl.BlockSpec((SIDE, tokens, part), lambda i, n: (0, 0, place + i))]
    extra = [] if into is None else [into]
    made = pl.pallas_call(
        functools.partial(forward_kernel, count, many),
        out_shape=outs,
        grid_spec=pltpu.PrefetchScalarGridSpec(
            num_scalar_prefetch=1,
            grid=(count,),
            in_specs=[pl.BlockSpec(memory_space=pltpu.VMEM)]
            + [pl.BlockSpec(memory_space=pl.ANY)] * (count + len(extra)),
            out_specs=specs,
            scratch_shapes=[
                pltpu.VMEM((count, SIDE, depth, part), jnp.bfloat16),
                pltpu.SemaphoreType.DMA((count,)),
            ],
        ),
        input_output_aliases={} if into is None else {count + 2: 0},
        compiler_params=pltpu.CompilerParams(vmem_limit_bytes=24 << 20),
        cost_estimate=pl.CostEstimate(
            flops=tokens * depth * count * part,
            bytes_accessed=depth * part * count,
            transcendentals=0,
        ),
        name="forward",
    )(start, wide, *lines, *extra)
    return made if apart else made[0]


def arrange_kernel(far_ref, here_ref, *refs):
    besides, out_ref = refs[:2], refs[2]
    part = here_ref.shape[2] // 2
    far = far_ref[0]

    def total(ref, lane):
        parts = [ref[y, :, lane : lane + part].astype(jnp.float32) for y in range(SIDE)]
        return (parts[0] + parts[1] + parts[2] + parts[3]).astype(out_ref.dtype)

    for h in range(2):
        lanes = slice(h * part, (h + 1) * part)
        out_ref[far, :, lanes] = total(here_ref, h * part)
        out_ref[lax.rem(far + 1, SIDE), :, lanes] = total(besides[h], 0)
        out_ref[lax.rem(far + 3, SIDE), :, lanes] = total(besides[h], part)
        out_ref[lax.rem(far + 2, SIDE), :, lanes] = jnp.zeros_like(here_ref[0, :, lanes])


def arrange(far, *slots):
    tokens, cols = slots[0].shape[1:]
    rows = tokens // 2
    block = pl.BlockSpec((SIDE, rows, cols), lambda i, n: (0, i, 0))
    return pl.pallas_call(
        arrange_kernel,
        out_shape=pltpu.HBM(slots[0].shape, slots[0].dtype),
        grid_spec=pltpu.PrefetchScalarGridSpec(
            num_scalar_prefetch=1, grid=(2,), in_specs=[block] * 3, out_specs=block
        ),
        compiler_params=pltpu.CompilerParams(vmem_limit_bytes=16 << 20),
        cost_estimate=pl.CostEstimate(
            flops=4 * slots[0].size, bytes_accessed=8 * slots[0].size, transcendentals=0
        ),
        name="arrange",
    )(far, *slots)


def backward_kernel(count, first, last, spots_ref, *refs):
    lines, grads = refs[:count], refs[count : count * 5]
    weights = jnp.concatenate([line[k] for line in lines for k in range(SIDE)], axis=1)
    cols = jnp.concatenate([g[...] for g in grads], axis=1)
    product = lax.dot_general(
        cols, weights, (((1,), (1,)), ((), ())), preferred_element_type=jnp.float32
    )
    if first:
        refs[-1][...] = product
    elif not last:
        refs[-1][...] = refs[-2][...] + product
    else:
        total = refs[-3][...] + product

        @pl.when(pl.program_id(0) < 2)
        def _():
            refs[-1][...] = total.astype(jnp.bfloat16)

        @pl.when(pl.program_id(0) >= 2)
        def _():
            refs[-2][...] = total


def backward(spots, grown, out_grad, lines, last=False):
    tokens = out_grad.shape[0]
    depth, part = lines[0].shape[1:]
    count = len(lines)
    block = depth // 4
    first = grown is None
    out_grad = pltpu.with_memory_space_constraint(out_grad, pltpu.HBM)

    def column(j):
        return pl.BlockSpec((tokens, part), lambda i, n: (0, n[j]))

    total = pl.BlockSpec((tokens, block), lambda i, n: (0, (i + 2) % 4))
    outs, specs = [pltpu.HBM((tokens, depth), jnp.float32)], [total]
    if last:
        outs = [
            jax.ShapeDtypeStruct((tokens, depth // 2), jnp.float32),
            jax.ShapeDtypeStruct((tokens, depth // 2), jnp.bfloat16),
        ]
        specs = [
            pl.BlockSpec((tokens, block), lambda i, n: (0, jnp.maximum(i - 2, 0))),
            pl.BlockSpec((tokens, block), lambda i, n: (0, jnp.minimum(i, 1))),
        ]
    made = pl.pallas_call(
        functools.partial(backward_kernel, count, first, last),
        out_shape=outs,
        grid_spec=pltpu.PrefetchScalarGridSpec(
            num_scalar_prefetch=1,
            grid=(4,),
            in_specs=[pl.BlockSpec((SIDE, block, part), lambda i, n: (0, (i + 2) % 4, 0))] * count
            + [column(j) for j in range(count * SIDE)]
            + ([] if first else [total]),
            out_specs=specs,
        ),
        input_output_aliases={} if first or last else {5 * count + 1: 0},
        compiler_params=pltpu.CompilerParams(vmem_limit_bytes=28 << 20),
        cost_estimate=pl.CostEstimate(
            flops=tokens * depth * count * part,
            bytes_accessed=depth * part * count,
            transcendentals=0,
        ),
        name="backward",
    )(spots, *lines, *([out_grad] * (count * SIDE)), *([] if first else [pltpu.with_memory_space_constraint(grown, pltpu.HBM)]))
    return made if last else made[0]


def compose(logits, indices, vector_bank):
    weights = jax.nn.sigmoid(logits - logits[..., ::-1])
    levels = jnp.arange(vector_bank.shape[0], dtype=jnp.int32)
    picked = (indices[..., None] == levels).astype(jnp.float32)
    mixing = jnp.sum(picked * weights[..., None], axis=2)
    blocks = jnp.einsum("rjb,bc->rjc", mixing, vector_bank, precision=lax.Precision.HIGHEST)
    return (weights, picked, mixing, blocks.reshape(blocks.shape[0], -1))


def compose_back(grad_rows, weights, picked, mixing, vector_bank):
    blocks = grad_rows.reshape(mixing.shape[0], mixing.shape[1], -1)
    bank_part = jnp.einsum("rjb,rjc->bc", mixing, blocks, precision=lax.Precision.HIGHEST)
    projected = jnp.einsum("rjc,bc->rjb", blocks, vector_bank, precision=lax.Precision.HIGHEST)
    dots = jnp.sum(picked * projected[:, :, None, :], axis=3)
    logit_grad = weights * (dots - jnp.sum(weights * dots, axis=2, keepdims=True))
    return (bank_part, logit_grad)


def settle(piece, step, z, core):
    def from_second(parity):
        def move(x, z, y, c):
            if c == 1 and y % 2 == parity:
                return (x, z, (x + step) % SIDE, y // 2)
            return None

        return lax.ppermute(piece, BOTH, pairs(move))

    def move(x, z, y, c):
        return (x, z, y, 1) if c == 0 and (z + step) % SIDE >= 2 else None

    crossed = lax.ppermute(piece, BOTH, pairs(move))
    spot = (z + step) % SIDE
    first = jnp.where(core == 0, piece, crossed)
    first = jnp.where(spot // 2 == core, first, jnp.zeros_like(first))
    return first, spot % 2, [from_second(0), from_second(1)]


def local(attn_out, frozen_weight, vector_bank, logits_a, index_a, logits_b, index_b, out_grad):
    tokens, height = attn_out.shape
    shard = frozen_weight.shape[1]
    half, part = shard // 2, shard // 4
    f32, bf16 = jnp.float32, jnp.bfloat16
    dp, tensor = lax.axis_index("dp"), lax.axis_index("tensor")
    x, z, core = dp // SIDE, dp % SIDE, tensor % 2
    near, far = jnp.where(core == 0, x, z), jnp.where(core == 0, z, x)
    side = tensor // 2
    turned = ((SIDE - near) % SIDE).astype(jnp.int32).reshape(1)
    turned_here = ((SIDE - near + side) % SIDE).astype(jnp.int32).reshape(1)

    left, right = frozen_weight[:, :half], frozen_weight[:, half:]
    mine = jnp.where(core == 0, left, right)
    theirs = jnp.where(core == 0, right, left)
    swapped = lax.ppermute(theirs, "tensor", SWAP)
    shards = []
    for h in range(2):
        cols = slice(h * part, (h + 1) * part)
        shards.append(jnp.concatenate([mine[:, cols], swapped[:, cols]], axis=0))
    logits_a, logits_b, *shards = lax.optimization_barrier((logits_a, logits_b, *shards))
    lines = [ring_gather(shards[h], 0, h) for h in range(2)]
    arrivals = [lines[0][1], lines[0][3]]
    lines[0] = jnp.stack(lines[0])
    lines[0], *lines[1] = lax.optimization_barrier((lines[0], *lines[1]))
    lines[1] = jnp.stack(lines[1])
    def columns(i, h):
        far_at = (far + i) % SIDE
        spots = []
        for k in range(SIDE):
            near_at = (near + k) % SIDE
            x_at = jnp.where(core == 0, near_at, far_at)
            z_at = jnp.where(core == 0, far_at, near_at)
            spots.append((x_at * SIDE + z_at) * 4 + core * 2 + h)
        return spots

    def spots_of(chunks):
        return jnp.stack([s for i, h in chunks for s in columns(i, h)]).astype(jnp.int32)

    wide = jnp.concatenate([attn_out, lax.ppermute(attn_out, "tensor", SWAP)], axis=1)

    weights_a, picked_a, mixing_a, rows_a = compose(logits_a, index_a, vector_bank)
    weights_b, picked_b, mixing_b, rows_b = compose(logits_b, index_b, vector_bank)
    down_a, up_b = rows_a.astype(bf16), rows_b.astype(bf16)
    rank = down_a.shape[0]
    grad_cols = lax.dynamic_slice_in_dim(out_grad, tensor * height, height, 1)
    cols_by_cols = (((1,), (1,)), ((), ()))
    rows_by_rows = (((0,), (0,)), ((), ()))
    low_part = lax.dot_general(down_a, attn_out, cols_by_cols, preferred_element_type=f32)
    back_part = lax.dot_general(up_b, grad_cols, cols_by_cols, preferred_element_type=f32)
    totals = jnp.concatenate([low_part, back_part], axis=0)
    totals = over_tensor(after(totals, *arrivals)).astype(bf16)
    low_bf, back_bf = totals[:rank], totals[rank:]

    factor = adapter_scale / (tokens * lax.axis_size("dp"))
    grad_a = jnp.dot(back_bf, attn_out, preferred_element_type=f32)
    grad_b = jnp.dot(low_bf, grad_cols, preferred_element_type=f32)
    both = factor * jnp.concatenate([grad_a, grad_b], axis=0)
    lines[0], both = lax.optimization_barrier((lines[0], both))
    both = total_of(over_side(both, 0))
    both = total_of(over_side(both, 1))
    lines[1], both = lax.optimization_barrier((lines[1], both))
    blocks = [ring_gather(lines[h], 1, h) for h in range(2)]

    here = [(0, 0), (0, 1)]
    beside = [[(1, 0), (3, 0)], [(1, 1), (3, 1)]]
    across = [(2, 0), (2, 1)]

    def take(chunks):
        return [blocks[h][i] for i, h in chunks]

    sent_here = forward(turned, wide, take(here))
    slots_here = exchange(sent_here, "tensor", LANES)
    sent_first = forward(after(turned, sent_here), wide, take(beside[0]))
    slots_here, sent_first = lax.optimization_barrier((slots_here, sent_first))
    slots_first = exchange(sent_first, "tensor", LANES)
    bank_a, logit_grad_a = compose_back(both[:rank], weights_a, picked_a, mixing_a, vector_bank)
    bank_b, logit_grad_b = compose_back(both[rank:], weights_b, picked_b, mixing_b, vector_bank)
    bank_part = bank_a + bank_b
    bank_grad = over_tensor(bank_part)
    chunks = here + beside[0]
    grown = backward(after(spots_of(chunks), sent_first, bank_part), None, out_grad, take(chunks))
    sent_second = forward(after(turned, grown, bank_grad), wide, take(beside[1]))
    slots_first, sent_second = lax.optimization_barrier((slots_first, sent_second))
    slots_second = exchange(sent_second, "tensor", LANES)
    grown = backward(after(spots_of(beside[1]), sent_second), grown, out_grad, take(beside[1]))
    slots = arrange(
        far.astype(jnp.int32).reshape(1), slots_here, slots_first, after(slots_second, grown)
    )
    moved = exchange(slots, "tensor", LANES)
    sent = forward(after(turned_here, slots), wide, take(across), apart=True)
    grown, other = backward(
        after(spots_of(across), *sent), grown, out_grad, take(across), last=True
    )
    crossed = lax.ppermute(jnp.where(core == 0, slots[2:], moved[:2]), "tensor", SWAP)
    firsts = jnp.where(core == 0, slots[:2], crossed)
    seconds = jnp.where(core == 0, crossed, moved[2:])

    arrived = [sent[0]]
    for step in range(1, SIDE):
        turns = [(t, (t + 2 * step) % 8) for t in range(8)]
        arrived.append(lax.ppermute(sent[step], "tensor", turns))
    piece = total_of([a.astype(f32) for a in arrived]).astype(bf16)
    first, place, second = settle(piece, 2, z, core)
    cols = []
    for s in range(2):
        cols.append(firsts[s] + jnp.where(place == s, first, jnp.zeros_like(first)))
        cols.append(seconds[s] + second[s])
    summed = jnp.concatenate(cols, axis=1)
    layer_out = (
        summed.astype(f32)
        + adapter_scale * lax.dot_general(low_bf, up_b, rows_by_rows, preferred_element_type=f32)
    ).astype(bf16)
    other = lax.ppermute(other, "tensor", SWAP)
    attn_grad = (
        grown
        + other.astype(f32)
        + adapter_scale * lax.dot_general(back_bf, down_a, rows_by_rows, preferred_element_type=f32)
    ).astype(bf16)
    return (layer_out, attn_grad, bank_grad, logit_grad_a, logit_grad_b)


def solution(mesh):
    return jax.shard_map(
        local,
        mesh=mesh,
        in_specs=(
            P("dp", "tensor"),
            P("tensor", "dp"),
            P(),
            P(None, "tensor", None),
            P(None, "tensor", None),
            P(None, "tensor", None),
            P(None, "tensor", None),
            P("dp", None),
        ),
        out_specs=(
            P("dp", "tensor"),
            P("dp", "tensor"),
            P(),
            P(None, "tensor", None),
            P(None, "tensor", None),
        ),
        check_vma=False,
    )
```

```python
import functools

import jax
import jax.numpy as jnp
from jax import lax
from jax.experimental import pallas as pl
from jax.experimental.pallas import tpu as pltpu
from jax.sharding import PartitionSpec as P

adapter_scale = 2.0
SIDE = 4
BOTH = ("dp", "tensor")
LANES = [[0, 2, 4, 6], [1, 3, 5, 7]]
SWAP = [(t, t ^ 1) for t in range(8)]


def device(x, z, y, c):
    return (x * SIDE + z) * 8 + y * 2 + c


def pairs(move):
    found = []
    for x in range(SIDE):
        for z in range(SIDE):
            for y in range(SIDE):
                for c in range(2):
                    to = move(x, z, y, c)
                    if to is not None:
                        found.append((device(x, z, y, c), device(*to)))
    return found


def ring(stage, step):
    def move(x, z, y, c):
        if (stage == 0) == (c == 0):
            return ((x + step) % SIDE, z, y, c)
        return (x, (z + step) % SIDE, y, c)

    return pairs(move)


def shift(value, stage, step):
    return lax.ppermute(value, BOTH, ring(stage, step))


def ring_gather(own, stage, h):
    below = shift(own, stage, 1)
    above = shift(own, stage, -1)
    across = shift(below, stage, 1) if h == 0 else shift(above, stage, -1)
    return [own, above, across, below]


def exchange(value, axis, groups=None):
    return lax.all_to_all(
        value, axis, split_axis=0, concat_axis=0, tiled=True, axis_index_groups=groups
    )


def over_tensor(value):
    value = value + lax.ppermute(value, "tensor", SWAP)
    value = value + lax.ppermute(value, "tensor", [(t, t ^ 2) for t in range(8)])
    return value + lax.ppermute(value, "tensor", [(t, t ^ 4) for t in range(8)])


def after(value, *events):
    return lax.optimization_barrier((value, *events))[0]


def with_partner(value, bit, *events):
    other = lax.ppermute(value, "dp", [(d, d ^ bit) for d in range(16)])
    return value + after(other, *events)


def total_of(parts):
    return (parts[0] + parts[2]) + (parts[1] + parts[3])


def forward_kernel(count, many, start_ref, wide_ref, *refs):
    lines, outs, held, sems = refs[:count], refs[-2 - many : -2], refs[-2], refs[-1]
    part = held.shape[2] // SIDE

    def copies(m):
        return [
            pltpu.make_async_copy(
                lines[m].at[lax.rem(start_ref[0] + k, SIDE)],
                held.at[m, :, pl.ds(k * part, part)],
                sems.at[m, k],
            )
            for k in range(SIDE)
        ]

    @pl.when(pl.program_id(0) == 0)
    def _():
        for m in range(count):
            for copy in copies(m):
                copy.start()

    for m in range(count):

        @pl.when(pl.program_id(0) == m)
        def _():
            for copy in copies(m):
                copy.wait()
            product = jnp.dot(wide_ref[...], held[m], preferred_element_type=jnp.float32)
            product = product.astype(jnp.bfloat16)
            for k in range(SIDE):
                piece = product[:, k * part : (k + 1) * part]
                if many == 1:
                    outs[0][k] = piece
                else:
                    outs[k][...] = piece


def forward(start, wide, lines, apart=False):
    tokens, depth = wide.shape
    part = lines[0].shape[2]
    count = len(lines)
    many = SIDE if apart else 1
    if apart:
        outs = [pltpu.HBM((tokens, count * part), jnp.bfloat16)] * SIDE
        specs = [pl.BlockSpec((tokens, part), lambda i, n: (0, i))] * SIDE
    else:
        outs = [pltpu.HBM((SIDE, tokens, count * part), jnp.bfloat16)]
        specs = [pl.BlockSpec((SIDE, tokens, part), lambda i, n: (0, 0, i))]
    made = pl.pallas_call(
        functools.partial(forward_kernel, count, many),
        out_shape=outs,
        grid_spec=pltpu.PrefetchScalarGridSpec(
            num_scalar_prefetch=1,
            grid=(count,),
            in_specs=[pl.BlockSpec(memory_space=pltpu.VMEM)]
            + [pl.BlockSpec(memory_space=pl.ANY)] * count,
            out_specs=specs,
            scratch_shapes=[
                pltpu.VMEM((count, depth, SIDE * part), jnp.bfloat16),
                pltpu.SemaphoreType.DMA((count, SIDE)),
            ],
        ),
        compiler_params=pltpu.CompilerParams(vmem_limit_bytes=24 << 20),
        cost_estimate=pl.CostEstimate(
            flops=tokens * depth * count * part,
            bytes_accessed=depth * part * count,
            transcendentals=0,
        ),
        name="forward",
    )(start, wide, *lines)
    return made if apart else made[0]


def arrange_kernel(far_ref, here_ref, beside_ref, out_ref):
    part = here_ref.shape[2] // 2
    far = far_ref[0]

    def total(ref, lane):
        parts = [ref[y, :, lane : lane + part].astype(jnp.float32) for y in range(SIDE)]
        return (parts[0] + parts[1] + parts[2] + parts[3]).astype(out_ref.dtype)

    for h in range(2):
        lanes = slice(h * part, (h + 1) * part)
        out_ref[far, :, lanes] = total(here_ref, h * part)
        out_ref[lax.rem(far + 1, SIDE), :, lanes] = total(beside_ref, 2 * h * part)
        out_ref[lax.rem(far + 3, SIDE), :, lanes] = total(beside_ref, (2 * h + 1) * part)
        out_ref[lax.rem(far + 2, SIDE), :, lanes] = jnp.zeros_like(here_ref[0, :, lanes])


def arrange(far, here, beside):
    tokens = here.shape[1]
    rows = tokens // 4
    return pl.pallas_call(
        arrange_kernel,
        out_shape=jax.ShapeDtypeStruct(here.shape, here.dtype),
        grid_spec=pltpu.PrefetchScalarGridSpec(
            num_scalar_prefetch=1,
            grid=(4,),
            in_specs=[
                pl.BlockSpec((SIDE, rows, here.shape[2]), lambda i, n: (0, i, 0)),
                pl.BlockSpec((SIDE, rows, beside.shape[2]), lambda i, n: (0, i, 0)),
            ],
            out_specs=pl.BlockSpec((SIDE, rows, here.shape[2]), lambda i, n: (0, i, 0)),
        ),
        compiler_params=pltpu.CompilerParams(vmem_limit_bytes=16 << 20),
        cost_estimate=pl.CostEstimate(
            flops=4 * here.size, bytes_accessed=2 * (2 * here.size + beside.size), transcendentals=0
        ),
        name="arrange",
    )(far, here, beside)


def backward_kernel(count, last, spots_ref, grad_ref, *refs):
    lines, held, cols, line_sems, col_sems = refs[:count], *refs[-4:]
    part = held.shape[2] // SIDE
    block = held.shape[1] // 4
    step = pl.program_id(0)

    def weights(m, i):
        rows = pl.ds(((i + 2) % 4) * block, block)
        return [
            pltpu.make_async_copy(
                lines[m].at[k, rows, :],
                held.at[m, rows, pl.ds(k * part, part)],
                line_sems.at[i, m * SIDE + k],
            )
            for k in range(SIDE)
        ]

    def gradients(j):
        start = pl.multiple_of(spots_ref[j] * part, part)
        return pltpu.make_async_copy(
            grad_ref.at[:, pl.ds(start, part)],
            cols.at[:, pl.ds(j * part, part)],
            col_sems.at[j],
        )

    @pl.when(step == 0)
    def _():
        for j in range(count * SIDE):
            gradients(j).start()
        for i in range(4):
            for m in range(count):
                for copy in weights(m, i):
                    copy.start()
        for j in range(count * SIDE):
            gradients(j).wait()

    for i in range(4):

        @pl.when(step == i)
        def _():
            for m in range(count):
                for copy in weights(m, i):
                    copy.wait()

    rows = pl.ds(pl.multiple_of(lax.rem(step + 2, 4) * block, block), block)
    total = refs[count][...] if last else 0.0
    for m in range(count):
        lanes = slice(m * SIDE * part, (m + 1) * SIDE * part)
        total = total + lax.dot_general(
            cols[:, lanes],
            held[m, rows, :],
            (((1,), (1,)), ((), ())),
            preferred_element_type=jnp.float32,
        )
    if not last:
        refs[-5][...] = total
    else:

        @pl.when(step < 2)
        def _():
            refs[-5][...] = total.astype(jnp.bfloat16)

        @pl.when(step >= 2)
        def _():
            refs[-6][...] = total


def backward(spots, grown, out_grad, lines):
    tokens = out_grad.shape[0]
    depth, part = lines[0].shape[1:]
    count = len(lines)
    block = depth // 4
    last = grown is not None
    total = pl.BlockSpec((tokens, block), lambda i, n: (0, (i + 2) % 4))
    outs, specs = [pltpu.HBM((tokens, depth), jnp.float32)], [total]
    if last:
        outs = [
            jax.ShapeDtypeStruct((tokens, depth // 2), jnp.float32),
            jax.ShapeDtypeStruct((tokens, depth // 2), jnp.bfloat16),
        ]
        specs = [
            pl.BlockSpec((tokens, block), lambda i, n: (0, jnp.maximum(i - 2, 0))),
            pl.BlockSpec((tokens, block), lambda i, n: (0, jnp.minimum(i, 1))),
        ]
        grown = [pltpu.with_memory_space_constraint(grown, pltpu.HBM)]
    made = pl.pallas_call(
        functools.partial(backward_kernel, count, last),
        out_shape=outs,
        grid_spec=pltpu.PrefetchScalarGridSpec(
            num_scalar_prefetch=1,
            grid=(4,),
            in_specs=[pl.BlockSpec(memory_space=pl.ANY)] * (count + 1) + ([total] if last else []),
            out_specs=specs,
            scratch_shapes=[
                pltpu.VMEM((count, depth, SIDE * part), jnp.bfloat16),
                pltpu.VMEM((tokens, count * SIDE * part), jnp.bfloat16),
                pltpu.SemaphoreType.DMA((4, count * SIDE)),
                pltpu.SemaphoreType.DMA((count * SIDE,)),
            ],
        ),
        compiler_params=pltpu.CompilerParams(vmem_limit_bytes=32 << 20),
        cost_estimate=pl.CostEstimate(
            flops=tokens * depth * count * part,
            bytes_accessed=depth * part * count,
            transcendentals=0,
        ),
        name="backward",
    )(
        spots,
        pltpu.with_memory_space_constraint(out_grad, pltpu.HBM),
        *lines,
        *(grown if last else []),
    )
    return made if last else made[0]


def compose(logits, indices, vector_bank):
    weights = jax.nn.sigmoid(logits - logits[..., ::-1])
    levels = jnp.arange(vector_bank.shape[0], dtype=jnp.int32)
    picked = (indices[..., None] == levels).astype(jnp.float32)
    mixing = jnp.sum(picked * weights[..., None], axis=2)
    blocks = jnp.einsum("rjb,bc->rjc", mixing, vector_bank, precision=lax.Precision.HIGHEST)
    return (weights, picked, mixing, blocks.reshape(blocks.shape[0], -1))


def compose_back(grad_rows, weights, picked, mixing, vector_bank):
    blocks = grad_rows.reshape(mixing.shape[0], mixing.shape[1], -1)
    bank_part = jnp.einsum("rjb,rjc->bc", mixing, blocks, precision=lax.Precision.HIGHEST)
    projected = jnp.einsum("rjc,bc->rjb", blocks, vector_bank, precision=lax.Precision.HIGHEST)
    dots = jnp.sum(picked * projected[:, :, None, :], axis=3)
    logit_grad = weights * (dots - jnp.sum(weights * dots, axis=2, keepdims=True))
    return (bank_part, logit_grad)


def settle(piece, step, z, core):
    def from_second(parity):
        def move(x, z, y, c):
            if c == 1 and y % 2 == parity:
                return (x, z, (x + step) % SIDE, y // 2)
            return None

        return lax.ppermute(piece, BOTH, pairs(move))

    def move(x, z, y, c):
        return (x, z, y, 1) if c == 0 and (z + step) % SIDE >= 2 else None

    crossed = lax.ppermute(piece, BOTH, pairs(move))
    spot = (z + step) % SIDE
    first = jnp.where(core == 0, piece, crossed)
    first = jnp.where(spot // 2 == core, first, jnp.zeros_like(first))
    return first, spot % 2, [from_second(0), from_second(1)]


def local(attn_out, frozen_weight, vector_bank, logits_a, index_a, logits_b, index_b, out_grad):
    tokens, height = attn_out.shape
    shard = frozen_weight.shape[1]
    half, part = shard // 2, shard // 4
    f32, bf16 = jnp.float32, jnp.bfloat16
    dp, tensor = lax.axis_index("dp"), lax.axis_index("tensor")
    x, z, core = dp // SIDE, dp % SIDE, tensor % 2
    near, far = jnp.where(core == 0, x, z), jnp.where(core == 0, z, x)
    side = tensor // 2
    turned = ((SIDE - near) % SIDE).astype(jnp.int32).reshape(1)
    turned_here = ((SIDE - near + side) % SIDE).astype(jnp.int32).reshape(1)

    left, right = frozen_weight[:, :half], frozen_weight[:, half:]
    mine = jnp.where(core == 0, left, right)
    theirs = jnp.where(core == 0, right, left)
    swapped = lax.ppermute(theirs, "tensor", SWAP)
    shards = []
    for h in range(2):
        cols = slice(h * part, (h + 1) * part)
        shards.append(jnp.concatenate([mine[:, cols], swapped[:, cols]], axis=0))
    logits_a, logits_b, *shards = lax.optimization_barrier((logits_a, logits_b, *shards))
    lines = [jnp.stack(ring_gather(shards[h], 0, h)) for h in range(2)]
    def columns(i, h):
        far_at = (far + i) % SIDE
        spots = []
        for k in range(SIDE):
            near_at = (near + k) % SIDE
            x_at = jnp.where(core == 0, near_at, far_at)
            z_at = jnp.where(core == 0, far_at, near_at)
            spots.append((x_at * SIDE + z_at) * 4 + core * 2 + h)
        return spots

    def spots_of(chunks):
        return jnp.stack([s for i, h in chunks for s in columns(i, h)]).astype(jnp.int32)

    wide = jnp.concatenate([attn_out, lax.ppermute(attn_out, "tensor", SWAP)], axis=1)

    weights_a, picked_a, mixing_a, rows_a = compose(logits_a, index_a, vector_bank)
    weights_b, picked_b, mixing_b, rows_b = compose(logits_b, index_b, vector_bank)
    down_a, up_b = rows_a.astype(bf16), rows_b.astype(bf16)
    rank = down_a.shape[0]
    grad_cols = lax.dynamic_slice_in_dim(out_grad, tensor * height, height, 1)
    cols_by_cols = (((1,), (1,)), ((), ()))
    rows_by_rows = (((0,), (0,)), ((), ()))
    low_part = lax.dot_general(down_a, attn_out, cols_by_cols, preferred_element_type=f32)
    back_part = lax.dot_general(up_b, grad_cols, cols_by_cols, preferred_element_type=f32)
    totals = jnp.concatenate([low_part, back_part], axis=0)
    lines[1], totals = lax.optimization_barrier((lines[1], totals))
    blocks = [ring_gather(lines[h], 1, h) for h in range(2)]
    totals = over_tensor(totals).astype(bf16)
    low_bf, back_bf = totals[:rank], totals[rank:]

    factor = adapter_scale / (tokens * lax.axis_size("dp"))
    grad_a = jnp.dot(back_bf, attn_out, preferred_element_type=f32)
    grad_b = jnp.dot(low_bf, grad_cols, preferred_element_type=f32)
    bank_a, logit_grad_a = compose_back(
        factor * grad_a, weights_a, picked_a, mixing_a, vector_bank
    )
    bank_b, logit_grad_b = compose_back(
        factor * grad_b, weights_b, picked_b, mixing_b, vector_bank
    )
    levels = vector_bank.shape[0]
    logit_grads = jnp.concatenate([logit_grad_a.ravel(), logit_grad_b.ravel()])
    logit_grads = jnp.pad(logit_grads.reshape(-1, vector_bank.shape[1]), ((0, 7), (0, 0)))
    small = jnp.concatenate([over_tensor(bank_a + bank_b), logit_grads], axis=0)

    here = [(0, 0), (0, 1)]
    beside = [(1, 0), (3, 0), (1, 1), (3, 1)]
    across = [(2, 0), (2, 1)]

    def take(chunks):
        return [blocks[h][i] for i, h in chunks]

    sent_here = forward(turned, wide, take(here))
    slots_here = exchange(sent_here, "tensor", LANES)
    sent_beside = forward(after(turned, sent_here, small), wide, take(beside))
    slots_here, sent_beside = lax.optimization_barrier((slots_here, sent_beside))
    slots_beside = exchange(sent_beside, "tensor", LANES)
    grown = backward(
        after(spots_of(here + beside), sent_beside), None, out_grad, take(here + beside)
    )
    small = with_partner(small, 1, grown)
    sent = forward(after(turned_here, grown), wide, take(across), apart=True)
    arrived = [sent[0]]
    for step in range(1, SIDE):
        turns = [(t, (t + 2 * step) % 8) for t in range(8)]
        arrived.append(lax.ppermute(sent[step], "tensor", turns))
    piece = total_of([a.astype(f32) for a in arrived]).astype(bf16)
    small = with_partner(small, 4, *sent)
    slots_beside = after(slots_beside, *sent)
    slots = arrange(far.astype(jnp.int32).reshape(1), slots_here, slots_beside)
    moved = exchange(slots, "tensor", LANES)
    crossed = lax.ppermute(jnp.where(core == 0, slots[2:], moved[:2]), "tensor", SWAP)
    firsts = jnp.where(core == 0, slots[:2], crossed)
    seconds = jnp.where(core == 0, crossed, moved[2:])

    small = with_partner(small, 2, slots)
    grown, other = backward(after(spots_of(across), slots, piece), grown, out_grad, take(across))
    small = with_partner(small, 8, grown)
    bank_grad = small[:levels]
    logit_grads = small[levels].reshape(2, *logits_a.shape)
    logit_grad_a, logit_grad_b = logit_grads[0], logit_grads[1]
    first, place, second = settle(piece, 2, z, core)
    cols = []
    for s in range(2):
        cols.append(firsts[s] + jnp.where(place == s, first, jnp.zeros_like(first)))
        cols.append(seconds[s] + second[s])
    summed = jnp.concatenate(cols, axis=1)
    layer_out = (
        summed.astype(f32)
        + adapter_scale * lax.dot_general(low_bf, up_b, rows_by_rows, preferred_element_type=f32)
    ).astype(bf16)
    other = lax.ppermute(other, "tensor", SWAP)
    attn_grad = (
        grown
        + other.astype(f32)
        + adapter_scale * lax.dot_general(back_bf, down_a, rows_by_rows, preferred_element_type=f32)
    ).astype(bf16)
    return (layer_out, attn_grad, bank_grad, logit_grad_a, logit_grad_b)


def solution(mesh):
    return jax.shard_map(
        local,
        mesh=mesh,
        in_specs=(
            P("dp", "tensor"),
            P("tensor", "dp"),
            P(),
            P(None, "tensor", None),
            P(None, "tensor", None),
            P(None, "tensor", None),
            P(None, "tensor", None),
            P("dp", None),
        ),
        out_specs=(
            P("dp", "tensor"),
            P("dp", "tensor"),
            P(),
            P(None, "tensor", None),
            P(None, "tensor", None),
        ),
        check_vma=False,
    )
```

```python
import functools

import jax
import jax.numpy as jnp
from jax import lax
from jax.experimental import pallas as pl
from jax.experimental.pallas import tpu as pltpu
from jax.sharding import PartitionSpec as P

adapter_scale = 2.0
SIDE = 4
BOTH = ("dp", "tensor")
LANES = [[0, 2, 4, 6], [1, 3, 5, 7]]
SWAP = [(t, t ^ 1) for t in range(8)]


def device(x, z, y, c):
    return (x * SIDE + z) * 8 + y * 2 + c


def pairs(move):
    found = []
    for x in range(SIDE):
        for z in range(SIDE):
            for y in range(SIDE):
                for c in range(2):
                    to = move(x, z, y, c)
                    if to is not None:
                        found.append((device(x, z, y, c), device(*to)))
    return found


def ring(stage, step):
    def move(x, z, y, c):
        if (stage == 0) == (c == 0):
            return ((x + step) % SIDE, z, y, c)
        return (x, (z + step) % SIDE, y, c)

    return pairs(move)


def shift(value, stage, step):
    return lax.ppermute(value, BOTH, ring(stage, step))


def ring_gather(own, stage, h):
    below = shift(own, stage, 1)
    above = shift(own, stage, -1)
    across = shift(below, stage, 1) if h == 0 else shift(above, stage, -1)
    return [own, above, across, below]


def exchange(value, axis, groups=None):
    return lax.all_to_all(
        value, axis, split_axis=0, concat_axis=0, tiled=True, axis_index_groups=groups
    )


def over_tensor(value):
    value = value + lax.ppermute(value, "tensor", SWAP)
    value = value + lax.ppermute(value, "tensor", [(t, t ^ 2) for t in range(8)])
    return value + lax.ppermute(value, "tensor", [(t, t ^ 4) for t in range(8)])


def over_side(value, axis):
    def from_step(step):
        def move(x, z, y, c):
            if axis == 0:
                return ((x + step) % SIDE, z, y, c)
            return (x, (z + step) % SIDE, y, c)

        return lax.ppermute(value, BOTH, pairs(move))

    return [value, from_step(1), from_step(2), from_step(3)]


def total_of(parts):
    return (parts[0] + parts[2]) + (parts[1] + parts[3])


def after(value, *events):
    return lax.optimization_barrier((value, *events))[0]


def forward_kernel(count, start_ref, wide_ref, *refs):
    lines, outs, held, sems = refs[:count], refs[-6:-2], refs[-2], refs[-1]
    outs = refs[-3:-2] if len(refs) < count + 6 else outs
    copies = [pltpu.make_async_copy(lines[m], held.at[m], sems.at[m]) for m in range(count)]
    for copy in copies:
        copy.start()
    part = held.shape[3]
    order = [lax.rem(start_ref[0] + k, SIDE) for k in range(SIDE)]
    for m in range(count):
        copies[m].wait()
        weights = jnp.concatenate([held[m, k] for k in order], axis=1)
        product = jnp.dot(wide_ref[...], weights, preferred_element_type=jnp.float32)
        product = product.astype(jnp.bfloat16)
        for k in range(SIDE):
            piece = product[:, k * part : (k + 1) * part]
            if len(outs) == 1:
                outs[0][k, :, m * part : (m + 1) * part] = piece
            else:
                outs[k][:, m * part : (m + 1) * part] = piece


def forward(start, wide, lines, apart=False, places=1, into=None):
    tokens, depth = wide.shape
    part = lines[0].shape[2]
    count = len(lines)
    cols = count * part
    if apart:
        outs = [pltpu.HBM((tokens, cols), jnp.bfloat16)] * SIDE
        specs = [pl.BlockSpec((tokens, cols), lambda i, n: (0, 0))] * SIDE
    else:
        place = 0 if into is None else 1
        outs = pltpu.HBM((SIDE, tokens, places * cols), jnp.bfloat16)
        specs = pl.BlockSpec((SIDE, tokens, cols), lambda i, n: (0, 0, place))
    extra = [] if into is None else [into]
    return pl.pallas_call(
        functools.partial(forward_kernel, count),
        out_shape=outs,
        grid_spec=pltpu.PrefetchScalarGridSpec(
            num_scalar_prefetch=1,
            grid=(1,),
            in_specs=[pl.BlockSpec((tokens, depth), lambda i, n: (0, 0))]
            + [pl.BlockSpec(memory_space=pl.ANY)] * (count + len(extra)),
            out_specs=specs,
            scratch_shapes=[
                pltpu.VMEM((count, SIDE, depth, part), jnp.bfloat16),
                pltpu.SemaphoreType.DMA((count,)),
            ],
        ),
        input_output_aliases={} if into is None else {count + 2: 0},
        compiler_params=pltpu.CompilerParams(vmem_limit_bytes=28 << 20),
        cost_estimate=pl.CostEstimate(
            flops=tokens * depth * count * part,
            bytes_accessed=depth * part * count,
            transcendentals=0,
        ),
        name="forward",
    )(start, wide, *lines, *extra)


def arrange_kernel(far_ref, here_ref, beside_ref, out_ref):
    part = here_ref.shape[2] // 2
    far = far_ref[0]

    def total(ref, lane):
        parts = [ref[y, :, lane : lane + part].astype(jnp.float32) for y in range(SIDE)]
        return (parts[0] + parts[1] + parts[2] + parts[3]).astype(out_ref.dtype)

    for h in range(2):
        lanes = slice(h * part, (h + 1) * part)
        out_ref[far, :, lanes] = total(here_ref, h * part)
        out_ref[lax.rem(far + 1, SIDE), :, lanes] = total(beside_ref, 2 * h * part)
        out_ref[lax.rem(far + 3, SIDE), :, lanes] = total(beside_ref, (2 * h + 1) * part)
        out_ref[lax.rem(far + 2, SIDE), :, lanes] = jnp.zeros_like(here_ref[0, :, lanes])


def arrange(far, here, beside):
    tokens = here.shape[1]
    rows = tokens // 2
    return pl.pallas_call(
        arrange_kernel,
        out_shape=jax.ShapeDtypeStruct(here.shape, here.dtype),
        grid_spec=pltpu.PrefetchScalarGridSpec(
            num_scalar_prefetch=1,
            grid=(2,),
            in_specs=[
                pl.BlockSpec((SIDE, rows, here.shape[2]), lambda i, n: (0, i, 0)),
                pl.BlockSpec((SIDE, rows, beside.shape[2]), lambda i, n: (0, i, 0)),
            ],
            out_specs=pl.BlockSpec((SIDE, rows, here.shape[2]), lambda i, n: (0, i, 0)),
        ),
        compiler_params=pltpu.CompilerParams(vmem_limit_bytes=16 << 20),
        cost_estimate=pl.CostEstimate(
            flops=4 * here.size, bytes_accessed=2 * (2 * here.size + beside.size), transcendentals=0
        ),
        name="arrange",
    )(far, here, beside)


def collect_kernel(spots_ref, grad_ref, out_ref, sems):
    chunks, _, cols = out_ref.shape
    part = cols // SIDE
    copies = []
    for j in range(chunks * SIDE):
        start = pl.multiple_of(spots_ref[j] * part, part)
        copies.append(
            pltpu.make_async_copy(
                grad_ref.at[:, pl.ds(start, part)],
                out_ref.at[j // SIDE, :, pl.ds(j % SIDE * part, part)],
                sems.at[j],
            )
        )
    for copy in copies:
        copy.start()
    for copy in copies:
        copy.wait()


def collect(spots, out_grad, part):
    tokens = out_grad.shape[0]
    count = spots.shape[0]
    return pl.pallas_call(
        collect_kernel,
        out_shape=pltpu.HBM((count // SIDE, tokens, SIDE * part), out_grad.dtype),
        grid_spec=pltpu.PrefetchScalarGridSpec(
            num_scalar_prefetch=1,
            grid=(1,),
            in_specs=[pl.BlockSpec(memory_space=pl.ANY)],
            out_specs=pl.BlockSpec(memory_space=pl.ANY),
            scratch_shapes=[pltpu.SemaphoreType.DMA((count,))],
        ),
        compiler_params=pltpu.CompilerParams(vmem_limit_bytes=8 << 20),
        cost_estimate=pl.CostEstimate(flops=0, bytes_accessed=1 << 21, transcendentals=0),
        name="collect",
    )(spots, pltpu.with_memory_space_constraint(out_grad, pltpu.HBM))


def backward_kernel(count, first, last, *refs):
    lines, grads = refs[:count], refs[count : 2 * count]
    total = 0.0 if first else refs[2 * count][...]
    for line, cols in zip(lines, grads):
        weights = jnp.concatenate([line[k] for k in range(SIDE)], axis=1)
        total = total + lax.dot_general(
            cols[0], weights, (((1,), (1,)), ((), ())), preferred_element_type=jnp.float32
        )
    if not last:
        refs[-1][...] = total
    else:

        @pl.when(pl.program_id(0) < 2)
        def _():
            refs[-1][...] = total.astype(jnp.bfloat16)

        @pl.when(pl.program_id(0) >= 2)
        def _():
            refs[-2][...] = total


def backward(places, grown, grads, lines, last=False):
    tokens, cols = grads.shape[1:]
    depth, part = lines[0].shape[1:]
    count = len(lines)
    block = depth // 4
    first = grown is None

    def chunk(place):
        return pl.BlockSpec((1, tokens, cols), lambda i: (place, 0, 0))

    total = pl.BlockSpec((tokens, block), lambda i: (0, (i + 2) % 4))
    outs, specs = [pltpu.HBM((tokens, depth), jnp.float32)], [total]
    if last:
        outs = [
            jax.ShapeDtypeStruct((tokens, depth // 2), jnp.float32),
            jax.ShapeDtypeStruct((tokens, depth // 2), jnp.bfloat16),
        ]
        specs = [
            pl.BlockSpec((tokens, block), lambda i: (0, jnp.maximum(i - 2, 0))),
            pl.BlockSpec((tokens, block), lambda i: (0, jnp.minimum(i, 1))),
        ]
    made = pl.pallas_call(
        functools.partial(backward_kernel, count, first, last),
        out_shape=outs,
        grid=(4,),
        in_specs=[pl.BlockSpec((SIDE, block, part), lambda i: (0, (i + 2) % 4, 0))] * count
        + [chunk(place) for place in places]
        + ([] if first else [total]),
        out_specs=specs,
        input_output_aliases={} if first or last else {2 * count: 0},
        compiler_params=pltpu.CompilerParams(vmem_limit_bytes=28 << 20),
        cost_estimate=pl.CostEstimate(
            flops=tokens * depth * count * part,
            bytes_accessed=depth * part * count,
            transcendentals=0,
        ),
        name="backward",
    )(
        *lines,
        *([pltpu.with_memory_space_constraint(grads, pltpu.HBM)] * count),
        *([] if first else [pltpu.with_memory_space_constraint(grown, pltpu.HBM)]),
    )
    return made if last else made[0]


def compose(logits, indices, vector_bank):
    weights = jax.nn.sigmoid(logits - logits[..., ::-1])
    levels = jnp.arange(vector_bank.shape[0], dtype=jnp.int32)
    picked = (indices[..., None] == levels).astype(jnp.float32)
    mixing = jnp.sum(picked * weights[..., None], axis=2)
    blocks = jnp.einsum("rjb,bc->rjc", mixing, vector_bank, precision=lax.Precision.HIGHEST)
    return (weights, picked, mixing, blocks.reshape(blocks.shape[0], -1))


def compose_back(grad_rows, weights, picked, mixing, vector_bank):
    blocks = grad_rows.reshape(mixing.shape[0], mixing.shape[1], -1)
    bank_part = jnp.einsum("rjb,rjc->bc", mixing, blocks, precision=lax.Precision.HIGHEST)
    projected = jnp.einsum("rjc,bc->rjb", blocks, vector_bank, precision=lax.Precision.HIGHEST)
    dots = jnp.sum(picked * projected[:, :, None, :], axis=3)
    logit_grad = weights * (dots - jnp.sum(weights * dots, axis=2, keepdims=True))
    return (bank_part, logit_grad)


def settle(piece, step, z, core):
    def from_second(parity):
        def move(x, z, y, c):
            if c == 1 and y % 2 == parity:
                return (x, z, (x + step) % SIDE, y // 2)
            return None

        return lax.ppermute(piece, BOTH, pairs(move))

    def move(x, z, y, c):
        return (x, z, y, 1) if c == 0 and (z + step) % SIDE >= 2 else None

    crossed = lax.ppermute(piece, BOTH, pairs(move))
    spot = (z + step) % SIDE
    first = jnp.where(core == 0, piece, crossed)
    first = jnp.where(spot // 2 == core, first, jnp.zeros_like(first))
    return first, spot % 2, [from_second(0), from_second(1)]


def local(attn_out, frozen_weight, vector_bank, logits_a, index_a, logits_b, index_b, out_grad):
    tokens, height = attn_out.shape
    shard = frozen_weight.shape[1]
    half, part = shard // 2, shard // 4
    f32, bf16 = jnp.float32, jnp.bfloat16
    dp, tensor = lax.axis_index("dp"), lax.axis_index("tensor")
    x, z, core = dp // SIDE, dp % SIDE, tensor % 2
    near, far = jnp.where(core == 0, x, z), jnp.where(core == 0, z, x)
    side = tensor // 2
    turned = ((SIDE - near) % SIDE).astype(jnp.int32).reshape(1)
    turned_here = ((SIDE - near + side) % SIDE).astype(jnp.int32).reshape(1)

    left, right = frozen_weight[:, :half], frozen_weight[:, half:]
    mine = jnp.where(core == 0, left, right)
    theirs = jnp.where(core == 0, right, left)
    swapped = lax.ppermute(theirs, "tensor", SWAP)
    shards = []
    for h in range(2):
        cols = slice(h * part, (h + 1) * part)
        shards.append(jnp.concatenate([mine[:, cols], swapped[:, cols]], axis=0))
    logits_a, logits_b, *shards = lax.optimization_barrier((logits_a, logits_b, *shards))
    def columns(i, h):
        far_at = (far + i) % SIDE
        spots = []
        for k in range(SIDE):
            near_at = (near + k) % SIDE
            x_at = jnp.where(core == 0, near_at, far_at)
            z_at = jnp.where(core == 0, far_at, near_at)
            spots.append((x_at * SIDE + z_at) * 4 + core * 2 + h)
        return spots

    chunks = [(i, h) for i in range(SIDE) for h in range(2)]
    spots = jnp.stack([s for i, h in chunks for s in columns(i, h)]).astype(jnp.int32)
    grads = collect(after(spots, *shards), out_grad, part)

    def places(chunks):
        return [i * 2 + h for i, h in chunks]

    lines = [jnp.stack(ring_gather(shards[h], 0, h)) for h in range(2)]
    lines[0], grads = lax.optimization_barrier((lines[0], grads))
    wide = jnp.concatenate([attn_out, lax.ppermute(attn_out, "tensor", SWAP)], axis=1)

    weights_a, picked_a, mixing_a, rows_a = compose(logits_a, index_a, vector_bank)
    weights_b, picked_b, mixing_b, rows_b = compose(logits_b, index_b, vector_bank)
    down_a, up_b = rows_a.astype(bf16), rows_b.astype(bf16)
    rank = down_a.shape[0]
    grad_cols = lax.dynamic_slice_in_dim(out_grad, tensor * height, height, 1)
    cols_by_cols = (((1,), (1,)), ((), ()))
    rows_by_rows = (((0,), (0,)), ((), ()))
    low_part = lax.dot_general(down_a, attn_out, cols_by_cols, preferred_element_type=f32)
    back_part = lax.dot_general(up_b, grad_cols, cols_by_cols, preferred_element_type=f32)
    totals = jnp.concatenate([low_part, back_part], axis=0)
    lines[1], totals = lax.optimization_barrier((lines[1], totals))
    blocks = [ring_gather(lines[h], 1, h) for h in range(2)]
    totals = over_tensor(totals).astype(bf16)
    low_bf, back_bf = totals[:rank], totals[rank:]

    factor = adapter_scale / (tokens * lax.axis_size("dp"))
    grad_a = jnp.dot(back_bf, attn_out, preferred_element_type=f32)
    grad_b = jnp.dot(low_bf, grad_cols, preferred_element_type=f32)
    both = factor * jnp.concatenate([grad_a, grad_b], axis=0)
    here = [(0, 0), (0, 1)]
    beside = [(1, 0), (3, 0), (1, 1), (3, 1)]
    across = [(2, 0), (2, 1)]

    def take(chunks):
        return [blocks[h][i] for i, h in chunks]

    sent_here = forward(turned, wide, take(here))
    slots_here = exchange(sent_here, "tensor", LANES)
    grads, sent_here = lax.optimization_barrier((grads, sent_here))
    grown = backward(places(here), None, grads, take(here))
    sent_beside = forward(after(turned, grown), wide, take(beside[:2]), places=2)
    sent_beside = forward(turned, wide, take(beside[2:]), places=2, into=sent_beside)
    slots_here, sent_beside, both = lax.optimization_barrier((slots_here, sent_beside, both))
    slots_beside = exchange(sent_beside, "tensor", LANES)
    both_parts = over_side(both, 0)
    grads, sent_beside = lax.optimization_barrier((grads, sent_beside))
    grown = backward(places(beside), grown, grads, take(beside))
    sent = forward(after(turned_here, grown), wide, take(across), apart=True)
    arrived = [sent[0]]
    for step in range(1, SIDE):
        turns = [(t, (t + 2 * step) % 8) for t in range(8)]
        arrived.append(lax.ppermute(sent[step], "tensor", turns))
    piece = total_of([a.astype(f32) for a in arrived]).astype(bf16)
    slots_beside, *both_parts = lax.optimization_barrier((slots_beside, *both_parts, *sent))[:5]
    both_parts = over_side(total_of(both_parts), 1)
    slots = arrange(far.astype(jnp.int32).reshape(1), slots_here, slots_beside)
    moved = exchange(slots, "tensor", LANES)
    both = total_of(lax.optimization_barrier((*both_parts, slots))[:SIDE])
    bank_a, logit_grad_a = compose_back(both[:rank], weights_a, picked_a, mixing_a, vector_bank)
    bank_b, logit_grad_b = compose_back(both[rank:], weights_b, picked_b, mixing_b, vector_bank)
    crossed = lax.ppermute(jnp.where(core == 0, slots[2:], moved[:2]), "tensor", SWAP)
    firsts = jnp.where(core == 0, slots[:2], crossed)
    seconds = jnp.where(core == 0, crossed, moved[2:])

    bank_grad = over_tensor(bank_a + bank_b)
    grads, slots, piece = lax.optimization_barrier((grads, slots, piece))
    grown, other = backward(places(across), grown, grads, take(across), last=True)
    first, place, second = settle(piece, 2, z, core)
    cols = []
    for s in range(2):
        cols.append(firsts[s] + jnp.where(place == s, first, jnp.zeros_like(first)))
        cols.append(seconds[s] + second[s])
    summed = jnp.concatenate(cols, axis=1)
    layer_out = (
        summed.astype(f32)
        + adapter_scale * lax.dot_general(low_bf, up_b, rows_by_rows, preferred_element_type=f32)
    ).astype(bf16)
    other = lax.ppermute(other, "tensor", SWAP)
    attn_grad = (
        grown
        + other.astype(f32)
        + adapter_scale * lax.dot_general(back_bf, down_a, rows_by_rows, preferred_element_type=f32)
    ).astype(bf16)
    return (layer_out, attn_grad, bank_grad, logit_grad_a, logit_grad_b)


def solution(mesh):
    return jax.shard_map(
        local,
        mesh=mesh,
        in_specs=(
            P("dp", "tensor"),
            P("tensor", "dp"),
            P(),
            P(None, "tensor", None),
            P(None, "tensor", None),
            P(None, "tensor", None),
            P(None, "tensor", None),
            P("dp", None),
        ),
        out_specs=(
            P("dp", "tensor"),
            P("dp", "tensor"),
            P(),
            P(None, "tensor", None),
            P(None, "tensor", None),
        ),
        check_vma=False,
    )
```

```python
import functools

import jax
import jax.numpy as jnp
from jax import lax
from jax.experimental import pallas as pl
from jax.experimental.pallas import tpu as pltpu
from jax.sharding import PartitionSpec as P

adapter_scale = 2.0
SIDE = 4
BOTH = ("dp", "tensor")
LANES = [[0, 2, 4, 6], [1, 3, 5, 7]]
SWAP = [(t, t ^ 1) for t in range(8)]


def device(x, z, y, c):
    return (x * SIDE + z) * 8 + y * 2 + c


def pairs(move):
    found = []
    for x in range(SIDE):
        for z in range(SIDE):
            for y in range(SIDE):
                for c in range(2):
                    to = move(x, z, y, c)
                    if to is not None:
                        found.append((device(x, z, y, c), device(*to)))
    return found


def ring(stage, step):
    def move(x, z, y, c):
        if (stage == 0) == (c == 0):
            return ((x + step) % SIDE, z, y, c)
        return (x, (z + step) % SIDE, y, c)

    return pairs(move)


def shift(value, stage, step):
    return lax.ppermute(value, BOTH, ring(stage, step))


def ring_gather(own, stage, h):
    below = shift(own, stage, 1)
    above = shift(own, stage, -1)
    across = shift(below, stage, 1) if h == 0 else shift(above, stage, -1)
    return [own, above, across, below]


def exchange(value, axis, groups=None):
    return lax.all_to_all(
        value, axis, split_axis=0, concat_axis=0, tiled=True, axis_index_groups=groups
    )


def over_tensor(value):
    value = value + lax.ppermute(value, "tensor", SWAP)
    value = value + lax.ppermute(value, "tensor", [(t, t ^ 2) for t in range(8)])
    return value + lax.ppermute(value, "tensor", [(t, t ^ 4) for t in range(8)])


def over_side(value, axis):
    def from_step(step):
        def move(x, z, y, c):
            if axis == 0:
                return ((x + step) % SIDE, z, y, c)
            return (x, (z + step) % SIDE, y, c)

        return lax.ppermute(value, BOTH, pairs(move))

    return [value, from_step(1), from_step(2), from_step(3)]


def after(value, *events):
    return lax.optimization_barrier((value, *events))[0]


def with_partner(value, bit, *events):
    other = lax.ppermute(value, "dp", [(d, d ^ bit) for d in range(16)])
    return value + after(other, *events)


def total_of(parts):
    return (parts[0] + parts[2]) + (parts[1] + parts[3])


def forward_kernel(count, many, start_ref, wide_ref, *refs):
    lines, outs, held, sems = refs[:count], refs[-2 - many : -2], refs[-2], refs[-1]
    copies = [pltpu.make_async_copy(lines[m], held.at[m], sems.at[m]) for m in range(count)]
    part = held.shape[3]
    order = [lax.rem(start_ref[0] + k, SIDE) for k in range(SIDE)]

    @pl.when(pl.program_id(0) == 0)
    def _():
        for copy in copies:
            copy.start()

    for m in range(count):

        @pl.when(pl.program_id(0) == m)
        def _():
            copies[m].wait()
            weights = jnp.concatenate([held[m, k] for k in order], axis=1)
            product = jnp.dot(wide_ref[...], weights, preferred_element_type=jnp.float32)
            product = product.astype(jnp.bfloat16)
            for k in range(SIDE):
                piece = product[:, k * part : (k + 1) * part]
                if many == 1:
                    outs[0][k] = piece
                else:
                    outs[k][...] = piece


def forward(start, wide, lines, apart=False, places=1, into=None):
    tokens, depth = wide.shape
    part = lines[0].shape[2]
    count = len(lines)
    cols = count * part
    many = SIDE if apart else 1
    if apart:
        outs = [pltpu.HBM((tokens, cols), jnp.bfloat16)] * SIDE
        specs = [pl.BlockSpec((tokens, part), lambda i, n: (0, i))] * SIDE
    else:
        place = 0 if into is None else count
        outs = [pltpu.HBM((SIDE, tokens, places * cols), jnp.bfloat16)]
        specs = [pl.BlockSpec((SIDE, tokens, part), lambda i, n: (0, 0, place + i))]
    extra = [] if into is None else [into]
    made = pl.pallas_call(
        functools.partial(forward_kernel, count, many),
        out_shape=outs,
        grid_spec=pltpu.PrefetchScalarGridSpec(
            num_scalar_prefetch=1,
            grid=(count,),
            in_specs=[pl.BlockSpec(memory_space=pltpu.VMEM)]
            + [pl.BlockSpec(memory_space=pl.ANY)] * (count + len(extra)),
            out_specs=specs,
            scratch_shapes=[
                pltpu.VMEM((count, SIDE, depth, part), jnp.bfloat16),
                pltpu.SemaphoreType.DMA((count,)),
            ],
        ),
        input_output_aliases={} if into is None else {count + 2: 0},
        compiler_params=pltpu.CompilerParams(vmem_limit_bytes=24 << 20),
        cost_estimate=pl.CostEstimate(
            flops=tokens * depth * count * part,
            bytes_accessed=depth * part * count,
            transcendentals=0,
        ),
        name="forward",
    )(start, wide, *lines, *extra)
    return made if apart else made[0]


def arrange_kernel(far_ref, here_ref, *refs):
    besides, out_ref = refs[:2], refs[2]
    part = here_ref.shape[2] // 2
    far = far_ref[0]

    def total(ref, lane):
        parts = [ref[y, :, lane : lane + part].astype(jnp.float32) for y in range(SIDE)]
        return (parts[0] + parts[1] + parts[2] + parts[3]).astype(out_ref.dtype)

    for h in range(2):
        lanes = slice(h * part, (h + 1) * part)
        out_ref[far, :, lanes] = total(here_ref, h * part)
        out_ref[lax.rem(far + 1, SIDE), :, lanes] = total(besides[1 - h], h * part)
        out_ref[lax.rem(far + 3, SIDE), :, lanes] = total(besides[h], h * part)
        out_ref[lax.rem(far + 2, SIDE), :, lanes] = jnp.zeros_like(here_ref[0, :, lanes])


def arrange(far, *slots):
    tokens, cols = slots[0].shape[1:]
    rows = tokens // 2
    block = pl.BlockSpec((SIDE, rows, cols), lambda i, n: (0, i, 0))
    return pl.pallas_call(
        arrange_kernel,
        out_shape=pltpu.HBM(slots[0].shape, slots[0].dtype),
        grid_spec=pltpu.PrefetchScalarGridSpec(
            num_scalar_prefetch=1, grid=(2,), in_specs=[block] * 3, out_specs=block
        ),
        compiler_params=pltpu.CompilerParams(vmem_limit_bytes=16 << 20),
        cost_estimate=pl.CostEstimate(
            flops=4 * slots[0].size, bytes_accessed=8 * slots[0].size, transcendentals=0
        ),
        name="arrange",
    )(far, *slots)


def backward_kernel(count, first, last, spots_ref, *refs):
    lines, grads = refs[:count], refs[count : count * 5]
    weights = jnp.concatenate([line[k] for line in lines for k in range(SIDE)], axis=1)
    cols = jnp.concatenate([g[...] for g in grads], axis=1)
    product = lax.dot_general(
        cols, weights, (((1,), (1,)), ((), ())), preferred_element_type=jnp.float32
    )
    if first:
        refs[-1][...] = product
    elif not last:
        refs[-1][...] = refs[-2][...] + product
    else:
        total = refs[-3][...] + product

        @pl.when(pl.program_id(0) < 2)
        def _():
            refs[-1][...] = total.astype(jnp.bfloat16)

        @pl.when(pl.program_id(0) >= 2)
        def _():
            refs[-2][...] = total


def backward(spots, grown, out_grad, lines, last=False):
    tokens = out_grad.shape[0]
    depth, part = lines[0].shape[1:]
    count = len(lines)
    block = depth // 4
    first = grown is None
    out_grad = pltpu.with_memory_space_constraint(out_grad, pltpu.HBM)

    def column(j):
        return pl.BlockSpec((tokens, part), lambda i, n: (0, n[j]))

    total = pl.BlockSpec((tokens, block), lambda i, n: (0, (i + 2) % 4))
    outs, specs = [pltpu.HBM((tokens, depth), jnp.float32)], [total]
    if last:
        outs = [
            jax.ShapeDtypeStruct((tokens, depth // 2), jnp.float32),
            jax.ShapeDtypeStruct((tokens, depth // 2), jnp.bfloat16),
        ]
        specs = [
            pl.BlockSpec((tokens, block), lambda i, n: (0, jnp.maximum(i - 2, 0))),
            pl.BlockSpec((tokens, block), lambda i, n: (0, jnp.minimum(i, 1))),
        ]
    made = pl.pallas_call(
        functools.partial(backward_kernel, count, first, last),
        out_shape=outs,
        grid_spec=pltpu.PrefetchScalarGridSpec(
            num_scalar_prefetch=1,
            grid=(4,),
            in_specs=[pl.BlockSpec((SIDE, block, part), lambda i, n: (0, (i + 2) % 4, 0))] * count
            + [column(j) for j in range(count * SIDE)]
            + ([] if first else [total]),
            out_specs=specs,
        ),
        input_output_aliases={} if first or last else {5 * count + 1: 0},
        compiler_params=pltpu.CompilerParams(vmem_limit_bytes=28 << 20),
        cost_estimate=pl.CostEstimate(
            flops=tokens * depth * count * part,
            bytes_accessed=depth * part * count,
            transcendentals=0,
        ),
        name="backward",
    )(spots, *lines, *([out_grad] * (count * SIDE)), *([] if first else [pltpu.with_memory_space_constraint(grown, pltpu.HBM)]))
    return made if last else made[0]


def compose(logits, indices, vector_bank):
    weights = jax.nn.sigmoid(logits - logits[..., ::-1])
    levels = jnp.arange(vector_bank.shape[0], dtype=jnp.int32)
    picked = (indices[..., None] == levels).astype(jnp.float32)
    mixing = jnp.sum(picked * weights[..., None], axis=2)
    blocks = jnp.einsum("rjb,bc->rjc", mixing, vector_bank, precision=lax.Precision.HIGHEST)
    return (weights, picked, mixing, blocks.reshape(blocks.shape[0], -1))


def compose_back(grad_rows, weights, picked, mixing, vector_bank):
    blocks = grad_rows.reshape(mixing.shape[0], mixing.shape[1], -1)
    bank_part = jnp.einsum("rjb,rjc->bc", mixing, blocks, precision=lax.Precision.HIGHEST)
    projected = jnp.einsum("rjc,bc->rjb", blocks, vector_bank, precision=lax.Precision.HIGHEST)
    dots = jnp.sum(picked * projected[:, :, None, :], axis=3)
    logit_grad = weights * (dots - jnp.sum(weights * dots, axis=2, keepdims=True))
    return (bank_part, logit_grad)


def settle(piece, step, z, core):
    def from_second(parity):
        def move(x, z, y, c):
            if c == 1 and y % 2 == parity:
                return (x, z, (x + step) % SIDE, y // 2)
            return None

        return lax.ppermute(piece, BOTH, pairs(move))

    def move(x, z, y, c):
        return (x, z, y, 1) if c == 0 and (z + step) % SIDE >= 2 else None

    crossed = lax.ppermute(piece, BOTH, pairs(move))
    spot = (z + step) % SIDE
    first = jnp.where(core == 0, piece, crossed)
    first = jnp.where(spot // 2 == core, first, jnp.zeros_like(first))
    return first, spot % 2, [from_second(0), from_second(1)]


def local(attn_out, frozen_weight, vector_bank, logits_a, index_a, logits_b, index_b, out_grad):
    tokens, height = attn_out.shape
    shard = frozen_weight.shape[1]
    half, part = shard // 2, shard // 4
    f32, bf16 = jnp.float32, jnp.bfloat16
    dp, tensor = lax.axis_index("dp"), lax.axis_index("tensor")
    x, z, core = dp // SIDE, dp % SIDE, tensor % 2
    near, far = jnp.where(core == 0, x, z), jnp.where(core == 0, z, x)
    side = tensor // 2
    turned = ((SIDE - near) % SIDE).astype(jnp.int32).reshape(1)
    turned_here = ((SIDE - near + side) % SIDE).astype(jnp.int32).reshape(1)

    left, right = frozen_weight[:, :half], frozen_weight[:, half:]
    mine = jnp.where(core == 0, left, right)
    theirs = jnp.where(core == 0, right, left)
    swapped = lax.ppermute(theirs, "tensor", SWAP)
    shards = []
    for h in range(2):
        cols = slice(h * part, (h + 1) * part)
        shards.append(jnp.concatenate([mine[:, cols], swapped[:, cols]], axis=0))
    logits_a, logits_b, *shards = lax.optimization_barrier((logits_a, logits_b, *shards))
    lines = [jnp.stack(ring_gather(shards[h], 0, h)) for h in range(2)]
    def columns(i, h):
        far_at = (far + i) % SIDE
        spots = []
        for k in range(SIDE):
            near_at = (near + k) % SIDE
            x_at = jnp.where(core == 0, near_at, far_at)
            z_at = jnp.where(core == 0, far_at, near_at)
            spots.append((x_at * SIDE + z_at) * 4 + core * 2 + h)
        return spots

    def spots_of(chunks):
        return jnp.stack([s for i, h in chunks for s in columns(i, h)]).astype(jnp.int32)

    wide = jnp.concatenate([attn_out, lax.ppermute(attn_out, "tensor", SWAP)], axis=1)

    weights_a, picked_a, mixing_a, rows_a = compose(logits_a, index_a, vector_bank)
    weights_b, picked_b, mixing_b, rows_b = compose(logits_b, index_b, vector_bank)
    down_a, up_b = rows_a.astype(bf16), rows_b.astype(bf16)
    rank = down_a.shape[0]
    grad_cols = lax.dynamic_slice_in_dim(out_grad, tensor * height, height, 1)
    cols_by_cols = (((1,), (1,)), ((), ()))
    rows_by_rows = (((0,), (0,)), ((), ()))
    low_part = lax.dot_general(down_a, attn_out, cols_by_cols, preferred_element_type=f32)
    back_part = lax.dot_general(up_b, grad_cols, cols_by_cols, preferred_element_type=f32)
    totals = jnp.concatenate([low_part, back_part], axis=0)
    lines[1], totals = lax.optimization_barrier((lines[1], totals))
    blocks = [ring_gather(lines[h], 1, h) for h in range(2)]
    totals = over_tensor(totals).astype(bf16)
    low_bf, back_bf = totals[:rank], totals[rank:]

    factor = adapter_scale / (tokens * lax.axis_size("dp"))
    grad_a = jnp.dot(back_bf, attn_out, preferred_element_type=f32)
    grad_b = jnp.dot(low_bf, grad_cols, preferred_element_type=f32)
    both = factor * jnp.concatenate([grad_a, grad_b], axis=0)
    here = [(0, 0), (0, 1)]
    beside = [[(3, 0), (1, 1)], [(1, 0), (3, 1)]]
    across = [(2, 0), (2, 1)]

    def take(chunks):
        return [blocks[h][i] for i, h in chunks]

    sent_here = forward(turned, wide, take(here))
    slots_here = exchange(sent_here, "tensor", LANES)
    grown = backward(after(spots_of(here), sent_here), None, out_grad, take(here))
    sent_first = forward(after(turned, grown), wide, take(beside[0]))
    slots_here, sent_first = lax.optimization_barrier((slots_here, sent_first))
    slots_first = exchange(sent_first, "tensor", LANES)
    sent_second = forward(after(turned, sent_first), wide, take(beside[1]))
    slots_first, sent_second, both = lax.optimization_barrier((slots_first, sent_second, both))
    slots_second = exchange(sent_second, "tensor", LANES)
    both_parts = over_side(both, 0)
    chunks = beside[0] + beside[1]
    grown = backward(after(spots_of(chunks), sent_second), grown, out_grad, take(chunks))
    slots = arrange(
        far.astype(jnp.int32).reshape(1), slots_here, slots_first, after(slots_second, grown)
    )
    moved = exchange(slots, "tensor", LANES)
    sent = forward(after(turned_here, slots), wide, take(across), apart=True)
    arrived = [sent[0]]
    for step in range(1, SIDE):
        turns = [(t, (t + 2 * step) % 8) for t in range(8)]
        arrived.append(lax.ppermute(sent[step], "tensor", turns))
    piece = total_of([a.astype(f32) for a in arrived]).astype(bf16)
    both = total_of(lax.optimization_barrier((*both_parts, *sent))[:SIDE])
    grown, other = backward(
        after(spots_of(across), *sent), grown, out_grad, take(across), last=True
    )
    both = with_partner(with_partner(both, 1, grown), 2)
    bank_a, logit_grad_a = compose_back(both[:rank], weights_a, picked_a, mixing_a, vector_bank)
    bank_b, logit_grad_b = compose_back(both[rank:], weights_b, picked_b, mixing_b, vector_bank)
    bank_grad = over_tensor(bank_a + bank_b)
    crossed = lax.ppermute(jnp.where(core == 0, slots[2:], moved[:2]), "tensor", SWAP)
    firsts = jnp.where(core == 0, slots[:2], crossed)
    seconds = jnp.where(core == 0, crossed, moved[2:])

    first, place, second = settle(piece, 2, z, core)
    cols = []
    for s in range(2):
        cols.append(firsts[s] + jnp.where(place == s, first, jnp.zeros_like(first)))
        cols.append(seconds[s] + second[s])
    summed = jnp.concatenate(cols, axis=1)
    layer_out = (
        summed.astype(f32)
        + adapter_scale * lax.dot_general(low_bf, up_b, rows_by_rows, preferred_element_type=f32)
    ).astype(bf16)
    other = lax.ppermute(other, "tensor", SWAP)
    attn_grad = (
        grown
        + other.astype(f32)
        + adapter_scale * lax.dot_general(back_bf, down_a, rows_by_rows, preferred_element_type=f32)
    ).astype(bf16)
    return (layer_out, attn_grad, bank_grad, logit_grad_a, logit_grad_b)


def solution(mesh):
    return jax.shard_map(
        local,
        mesh=mesh,
        in_specs=(
            P("dp", "tensor"),
            P("tensor", "dp"),
            P(),
            P(None, "tensor", None),
            P(None, "tensor", None),
            P(None, "tensor", None),
            P(None, "tensor", None),
            P("dp", None),
        ),
        out_specs=(
            P("dp", "tensor"),
            P("dp", "tensor"),
            P(),
            P(None, "tensor", None),
            P(None, "tensor", None),
        ),
        check_vma=False,
    )
```

```python
import functools

import jax
import jax.numpy as jnp
from jax import lax
from jax.experimental import pallas as pl
from jax.experimental.pallas import tpu as pltpu
from jax.sharding import PartitionSpec as P

adapter_scale = 2.0
SIDE = 4
BOTH = ("dp", "tensor")
LANES = [[0, 2, 4, 6], [1, 3, 5, 7]]
SWAP = [(t, t ^ 1) for t in range(8)]


def device(x, z, y, c):
    return (x * SIDE + z) * 8 + y * 2 + c


def pairs(move):
    found = []
    for x in range(SIDE):
        for z in range(SIDE):
            for y in range(SIDE):
                for c in range(2):
                    to = move(x, z, y, c)
                    if to is not None:
                        found.append((device(x, z, y, c), device(*to)))
    return found


def ring(stage, step):
    def move(x, z, y, c):
        if (stage == 0) == (c == 0):
            return ((x + step) % SIDE, z, y, c)
        return (x, (z + step) % SIDE, y, c)

    return pairs(move)


def shift(value, stage, step):
    return lax.ppermute(value, BOTH, ring(stage, step))


def ring_gather(own, stage, h):
    below = shift(own, stage, 1)
    above = shift(own, stage, -1)
    across = shift(below, stage, 1) if h == 0 else shift(above, stage, -1)
    return [own, above, across, below]


def exchange(value, axis, groups=None):
    return lax.all_to_all(
        value, axis, split_axis=0, concat_axis=0, tiled=True, axis_index_groups=groups
    )


def over_tensor(value):
    value = value + lax.ppermute(value, "tensor", SWAP)
    value = value + lax.ppermute(value, "tensor", [(t, t ^ 2) for t in range(8)])
    return value + lax.ppermute(value, "tensor", [(t, t ^ 4) for t in range(8)])


def over_side(value, axis):
    def from_step(step):
        def move(x, z, y, c):
            if axis == 0:
                return ((x + step) % SIDE, z, y, c)
            return (x, (z + step) % SIDE, y, c)

        return lax.ppermute(value, BOTH, pairs(move))

    return [value, from_step(1), from_step(2), from_step(3)]


def after(value, *events):
    return lax.optimization_barrier((value, *events))[0]


def with_partner(value, bit, *events):
    other = lax.ppermute(value, "dp", [(d, d ^ bit) for d in range(16)])
    return value + after(other, *events)


def total_of(parts):
    return (parts[0] + parts[2]) + (parts[1] + parts[3])


def forward_kernel(count, many, start_ref, wide_ref, *refs):
    lines, outs, held, sems = refs[:count], refs[-2 - many : -2], refs[-2], refs[-1]
    copies = [pltpu.make_async_copy(lines[m], held.at[m], sems.at[m]) for m in range(count)]
    part = held.shape[3]
    order = [lax.rem(start_ref[0] + k, SIDE) for k in range(SIDE)]

    @pl.when(pl.program_id(0) == 0)
    def _():
        for copy in copies:
            copy.start()

    for m in range(count):

        @pl.when(pl.program_id(0) == m)
        def _():
            copies[m].wait()
            weights = jnp.concatenate([held[m, k] for k in order], axis=1)
            product = jnp.dot(wide_ref[...], weights, preferred_element_type=jnp.float32)
            product = product.astype(jnp.bfloat16)
            for k in range(SIDE):
                piece = product[:, k * part : (k + 1) * part]
                if many == 1:
                    outs[0][k] = piece
                else:
                    outs[k][...] = piece


def forward(start, wide, lines, apart=False, places=1, into=None):
    tokens, depth = wide.shape
    part = lines[0].shape[2]
    count = len(lines)
    cols = count * part
    many = SIDE if apart else 1
    if apart:
        outs = [pltpu.HBM((tokens, cols), jnp.bfloat16)] * SIDE
        specs = [pl.BlockSpec((tokens, part), lambda i, n: (0, i))] * SIDE
    else:
        place = 0 if into is None else count
        outs = [pltpu.HBM((SIDE, tokens, places * cols), jnp.bfloat16)]
        specs = [pl.BlockSpec((SIDE, tokens, part), lambda i, n: (0, 0, place + i))]
    extra = [] if into is None else [into]
    made = pl.pallas_call(
        functools.partial(forward_kernel, count, many),
        out_shape=outs,
        grid_spec=pltpu.PrefetchScalarGridSpec(
            num_scalar_prefetch=1,
            grid=(count,),
            in_specs=[pl.BlockSpec(memory_space=pltpu.VMEM)]
            + [pl.BlockSpec(memory_space=pl.ANY)] * (count + len(extra)),
            out_specs=specs,
            scratch_shapes=[
                pltpu.VMEM((count, SIDE, depth, part), jnp.bfloat16),
                pltpu.SemaphoreType.DMA((count,)),
            ],
        ),
        input_output_aliases={} if into is None else {count + 2: 0},
        compiler_params=pltpu.CompilerParams(vmem_limit_bytes=24 << 20),
        cost_estimate=pl.CostEstimate(
            flops=tokens * depth * count * part,
            bytes_accessed=depth * part * count,
            transcendentals=0,
        ),
        name="forward",
    )(start, wide, *lines, *extra)
    return made if apart else made[0]


def arrange_kernel(far_ref, here_ref, *refs):
    besides, out_ref = refs[:2], refs[2]
    part = here_ref.shape[2] // 2
    far = far_ref[0]

    def total(ref, lane):
        parts = [ref[y, :, lane : lane + part].astype(jnp.float32) for y in range(SIDE)]
        return (parts[0] + parts[1] + parts[2] + parts[3]).astype(out_ref.dtype)

    for h in range(2):
        lanes = slice(h * part, (h + 1) * part)
        out_ref[far, :, lanes] = total(here_ref, h * part)
        out_ref[lax.rem(far + 1, SIDE), :, lanes] = total(besides[1 - h], h * part)
        out_ref[lax.rem(far + 3, SIDE), :, lanes] = total(besides[h], h * part)
        out_ref[lax.rem(far + 2, SIDE), :, lanes] = jnp.zeros_like(here_ref[0, :, lanes])


def arrange(far, *slots):
    tokens, cols = slots[0].shape[1:]
    rows = tokens // 2
    block = pl.BlockSpec((SIDE, rows, cols), lambda i, n: (0, i, 0))
    return pl.pallas_call(
        arrange_kernel,
        out_shape=pltpu.HBM(slots[0].shape, slots[0].dtype),
        grid_spec=pltpu.PrefetchScalarGridSpec(
            num_scalar_prefetch=1, grid=(2,), in_specs=[block] * 3, out_specs=block
        ),
        compiler_params=pltpu.CompilerParams(vmem_limit_bytes=16 << 20),
        cost_estimate=pl.CostEstimate(
            flops=4 * slots[0].size, bytes_accessed=8 * slots[0].size, transcendentals=0
        ),
        name="arrange",
    )(far, *slots)


def backward_kernel(count, first, last, spots_ref, *refs):
    lines, grads = refs[:count], refs[count : count * 5]
    weights = jnp.concatenate([line[k] for line in lines for k in range(SIDE)], axis=1)
    cols = jnp.concatenate([g[...] for g in grads], axis=1)
    product = lax.dot_general(
        cols, weights, (((1,), (1,)), ((), ())), preferred_element_type=jnp.float32
    )
    if first:
        refs[-1][...] = product
    elif not last:
        refs[-1][...] = refs[-2][...] + product
    else:
        total = refs[-3][...] + product

        @pl.when(pl.program_id(0) < 2)
        def _():
            refs[-1][...] = total.astype(jnp.bfloat16)

        @pl.when(pl.program_id(0) >= 2)
        def _():
            refs[-2][...] = total


def backward(spots, grown, out_grad, lines, last=False):
    tokens = out_grad.shape[0]
    depth, part = lines[0].shape[1:]
    count = len(lines)
    block = depth // 4
    first = grown is None
    out_grad = pltpu.with_memory_space_constraint(out_grad, pltpu.HBM)

    def column(j):
        return pl.BlockSpec((tokens, part), lambda i, n: (0, n[j]))

    total = pl.BlockSpec((tokens, block), lambda i, n: (0, (i + 2) % 4))
    outs, specs = [pltpu.HBM((tokens, depth), jnp.float32)], [total]
    if last:
        outs = [
            jax.ShapeDtypeStruct((tokens, depth // 2), jnp.float32),
            jax.ShapeDtypeStruct((tokens, depth // 2), jnp.bfloat16),
        ]
        specs = [
            pl.BlockSpec((tokens, block), lambda i, n: (0, jnp.maximum(i - 2, 0))),
            pl.BlockSpec((tokens, block), lambda i, n: (0, jnp.minimum(i, 1))),
        ]
    made = pl.pallas_call(
        functools.partial(backward_kernel, count, first, last),
        out_shape=outs,
        grid_spec=pltpu.PrefetchScalarGridSpec(
            num_scalar_prefetch=1,
            grid=(4,),
            in_specs=[pl.BlockSpec((SIDE, block, part), lambda i, n: (0, (i + 2) % 4, 0))] * count
            + [column(j) for j in range(count * SIDE)]
            + ([] if first else [total]),
            out_specs=specs,
        ),
        input_output_aliases={} if first or last else {5 * count + 1: 0},
        compiler_params=pltpu.CompilerParams(vmem_limit_bytes=28 << 20),
        cost_estimate=pl.CostEstimate(
            flops=tokens * depth * count * part,
            bytes_accessed=depth * part * count,
            transcendentals=0,
        ),
        name="backward",
    )(spots, *lines, *([out_grad] * (count * SIDE)), *([] if first else [pltpu.with_memory_space_constraint(grown, pltpu.HBM)]))
    return made if last else made[0]


def compose(logits, indices, vector_bank):
    weights = jax.nn.sigmoid(logits - logits[..., ::-1])
    levels = jnp.arange(vector_bank.shape[0], dtype=jnp.int32)
    picked = (indices[..., None] == levels).astype(jnp.float32)
    mixing = jnp.sum(picked * weights[..., None], axis=2)
    blocks = jnp.einsum("rjb,bc->rjc", mixing, vector_bank, precision=lax.Precision.HIGHEST)
    return (weights, picked, mixing, blocks.reshape(blocks.shape[0], -1))


def compose_back(grad_rows, weights, picked, mixing, vector_bank):
    blocks = grad_rows.reshape(mixing.shape[0], mixing.shape[1], -1)
    bank_part = jnp.einsum("rjb,rjc->bc", mixing, blocks, precision=lax.Precision.HIGHEST)
    projected = jnp.einsum("rjc,bc->rjb", blocks, vector_bank, precision=lax.Precision.HIGHEST)
    dots = jnp.sum(picked * projected[:, :, None, :], axis=3)
    logit_grad = weights * (dots - jnp.sum(weights * dots, axis=2, keepdims=True))
    return (bank_part, logit_grad)


def settle(piece, step, z, core):
    def from_second(parity):
        def move(x, z, y, c):
            if c == 1 and y % 2 == parity:
                return (x, z, (x + step) % SIDE, y // 2)
            return None

        return lax.ppermute(piece, BOTH, pairs(move))

    def move(x, z, y, c):
        return (x, z, y, 1) if c == 0 and (z + step) % SIDE >= 2 else None

    crossed = lax.ppermute(piece, BOTH, pairs(move))
    spot = (z + step) % SIDE
    first = jnp.where(core == 0, piece, crossed)
    first = jnp.where(spot // 2 == core, first, jnp.zeros_like(first))
    return first, spot % 2, [from_second(0), from_second(1)]


def local(attn_out, frozen_weight, vector_bank, logits_a, index_a, logits_b, index_b, out_grad):
    tokens, height = attn_out.shape
    shard = frozen_weight.shape[1]
    half, part = shard // 2, shard // 4
    f32, bf16 = jnp.float32, jnp.bfloat16
    dp, tensor = lax.axis_index("dp"), lax.axis_index("tensor")
    x, z, core = dp // SIDE, dp % SIDE, tensor % 2
    near, far = jnp.where(core == 0, x, z), jnp.where(core == 0, z, x)
    side = tensor // 2
    turned = ((SIDE - near) % SIDE).astype(jnp.int32).reshape(1)
    turned_here = ((SIDE - near + side) % SIDE).astype(jnp.int32).reshape(1)

    left, right = frozen_weight[:, :half], frozen_weight[:, half:]
    mine = jnp.where(core == 0, left, right)
    theirs = jnp.where(core == 0, right, left)
    swapped = lax.ppermute(theirs, "tensor", SWAP)
    shards = []
    for h in range(2):
        cols = slice(h * part, (h + 1) * part)
        shards.append(jnp.concatenate([mine[:, cols], swapped[:, cols]], axis=0))
    logits_a, logits_b, *shards = lax.optimization_barrier((logits_a, logits_b, *shards))
    lines = [jnp.stack(ring_gather(shards[h], 0, h)) for h in range(2)]
    def columns(i, h):
        far_at = (far + i) % SIDE
        spots = []
        for k in range(SIDE):
            near_at = (near + k) % SIDE
            x_at = jnp.where(core == 0, near_at, far_at)
            z_at = jnp.where(core == 0, far_at, near_at)
            spots.append((x_at * SIDE + z_at) * 4 + core * 2 + h)
        return spots

    def spots_of(chunks):
        return jnp.stack([s for i, h in chunks for s in columns(i, h)]).astype(jnp.int32)

    wide = jnp.concatenate([attn_out, lax.ppermute(attn_out, "tensor", SWAP)], axis=1)

    weights_a, picked_a, mixing_a, rows_a = compose(logits_a, index_a, vector_bank)
    weights_b, picked_b, mixing_b, rows_b = compose(logits_b, index_b, vector_bank)
    down_a, up_b = rows_a.astype(bf16), rows_b.astype(bf16)
    rank = down_a.shape[0]
    grad_cols = lax.dynamic_slice_in_dim(out_grad, tensor * height, height, 1)
    cols_by_cols = (((1,), (1,)), ((), ()))
    rows_by_rows = (((0,), (0,)), ((), ()))
    low_part = lax.dot_general(down_a, attn_out, cols_by_cols, preferred_element_type=f32)
    back_part = lax.dot_general(up_b, grad_cols, cols_by_cols, preferred_element_type=f32)
    totals = jnp.concatenate([low_part, back_part], axis=0)
    lines[1], totals = lax.optimization_barrier((lines[1], totals))
    below = [shift(line, 1, 1) for line in lines]
    above = [shift(line, 1, -1) for line in lines]
    totals = over_tensor(totals).astype(bf16)
    low_bf, back_bf = totals[:rank], totals[rank:]

    factor = adapter_scale / (tokens * lax.axis_size("dp"))
    grad_a = jnp.dot(back_bf, attn_out, preferred_element_type=f32)
    grad_b = jnp.dot(low_bf, grad_cols, preferred_element_type=f32)
    both = factor * jnp.concatenate([grad_a, grad_b], axis=0)
    here = [(0, 0), (0, 1)]
    beside = [[(3, 0), (1, 1)], [(1, 0), (3, 1)]]
    across = [(2, 0), (2, 1)]

    sent_here = forward(turned, wide, lines)
    slots_here = exchange(sent_here, "tensor", LANES)
    grown = backward(after(spots_of(here), sent_here), None, out_grad, lines)
    below[0], above[1], grown, totals = lax.optimization_barrier(
        (below[0], above[1], grown, totals)
    )
    corner = [shift(below[0], 1, 1), shift(above[1], 1, -1)]
    blocks = [[lines[h], above[h], corner[h], below[h]] for h in range(2)]

    def take(chunks):
        return [blocks[h][i] for i, h in chunks]

    sent_first = forward(turned, wide, take(beside[0]))
    slots_here, sent_first = lax.optimization_barrier((slots_here, sent_first))
    slots_first = exchange(sent_first, "tensor", LANES)
    sent_second = forward(after(turned, sent_first), wide, take(beside[1]))
    slots_first, sent_second, both = lax.optimization_barrier((slots_first, sent_second, both))
    slots_second = exchange(sent_second, "tensor", LANES)
    both_parts = over_side(both, 0)
    chunks = beside[0] + beside[1]
    grown = backward(after(spots_of(chunks), sent_second), grown, out_grad, take(chunks))
    both = total_of(lax.optimization_barrier((*both_parts, grown))[:SIDE])
    slots = arrange(
        far.astype(jnp.int32).reshape(1), slots_here, slots_first, after(slots_second, grown, both)
    )
    both = with_partner(both, 1, slots)
    moved = exchange(slots, "tensor", LANES)
    sent = forward(after(turned_here, slots, both), wide, take(across), apart=True)
    arrived = [sent[0]]
    for step in range(1, SIDE):
        turns = [(t, (t + 2 * step) % 8) for t in range(8)]
        arrived.append(lax.ppermute(sent[step], "tensor", turns))
    piece = total_of([a.astype(f32) for a in arrived]).astype(bf16)
    both = with_partner(both, 2, *sent)
    bank_a, logit_grad_a = compose_back(both[:rank], weights_a, picked_a, mixing_a, vector_bank)
    bank_b, logit_grad_b = compose_back(both[rank:], weights_b, picked_b, mixing_b, vector_bank)
    bank_part = bank_a + bank_b
    grown, other = backward(
        after(spots_of(across), *sent, bank_part), grown, out_grad, take(across), last=True
    )
    bank_grad = over_tensor(bank_part)
    crossed = lax.ppermute(jnp.where(core == 0, slots[2:], moved[:2]), "tensor", SWAP)
    firsts = jnp.where(core == 0, slots[:2], crossed)
    seconds = jnp.where(core == 0, crossed, moved[2:])

    first, place, second = settle(piece, 2, z, core)
    cols = []
    for s in range(2):
        cols.append(firsts[s] + jnp.where(place == s, first, jnp.zeros_like(first)))
        cols.append(seconds[s] + second[s])
    summed = jnp.concatenate(cols, axis=1)
    layer_out = (
        summed.astype(f32)
        + adapter_scale * lax.dot_general(low_bf, up_b, rows_by_rows, preferred_element_type=f32)
    ).astype(bf16)
    other = lax.ppermute(other, "tensor", SWAP)
    attn_grad = (
        grown
        + other.astype(f32)
        + adapter_scale * lax.dot_general(back_bf, down_a, rows_by_rows, preferred_element_type=f32)
    ).astype(bf16)
    return (layer_out, attn_grad, bank_grad, logit_grad_a, logit_grad_b)


def solution(mesh):
    return jax.shard_map(
        local,
        mesh=mesh,
        in_specs=(
            P("dp", "tensor"),
            P("tensor", "dp"),
            P(),
            P(None, "tensor", None),
            P(None, "tensor", None),
            P(None, "tensor", None),
            P(None, "tensor", None),
            P("dp", None),
        ),
        out_specs=(
            P("dp", "tensor"),
            P("dp", "tensor"),
            P(),
            P(None, "tensor", None),
            P(None, "tensor", None),
        ),
        check_vma=False,
    )
```

```python
import functools

import jax
import jax.numpy as jnp
from jax import lax
from jax.experimental import pallas as pl
from jax.experimental.pallas import tpu as pltpu
from jax.sharding import PartitionSpec as P

adapter_scale = 2.0
SIDE = 4
BOTH = ("dp", "tensor")
LANES = [[0, 2, 4, 6], [1, 3, 5, 7]]
SWAP = [(t, t ^ 1) for t in range(8)]


def device(x, z, y, c):
    return (x * SIDE + z) * 8 + y * 2 + c


def pairs(move):
    found = []
    for x in range(SIDE):
        for z in range(SIDE):
            for y in range(SIDE):
                for c in range(2):
                    to = move(x, z, y, c)
                    if to is not None:
                        found.append((device(x, z, y, c), device(*to)))
    return found


def ring(stage, step):
    def move(x, z, y, c):
        if (stage == 0) == (c == 0):
            return ((x + step) % SIDE, z, y, c)
        return (x, (z + step) % SIDE, y, c)

    return pairs(move)


def shift(value, stage, step):
    return lax.ppermute(value, BOTH, ring(stage, step))


def ring_gather(own, stage, h):
    below = shift(own, stage, 1)
    above = shift(own, stage, -1)
    across = shift(below, stage, 1) if h == 0 else shift(above, stage, -1)
    return [own, above, across, below]


def exchange(value, axis, groups=None):
    return lax.all_to_all(
        value, axis, split_axis=0, concat_axis=0, tiled=True, axis_index_groups=groups
    )


def over_tensor(value, bits=(1, 2, 4)):
    for bit in bits:
        value = value + lax.ppermute(value, "tensor", [(t, t ^ bit) for t in range(8)])
    return value


def over_side(value, axis):
    def from_step(step):
        def move(x, z, y, c):
            if axis == 0:
                return ((x + step) % SIDE, z, y, c)
            return (x, (z + step) % SIDE, y, c)

        return lax.ppermute(value, BOTH, pairs(move))

    return [value, from_step(1), from_step(2), from_step(3)]


def after(value, *events):
    return lax.optimization_barrier((value, *events))[0]


def with_partner(value, bit, *events):
    other = lax.ppermute(value, "dp", [(d, d ^ bit) for d in range(16)])
    return value + after(other, *events)


def total_of(parts):
    return (parts[0] + parts[2]) + (parts[1] + parts[3])


def forward_kernel(count, many, start_ref, wide_ref, *refs):
    lines, outs, held, sems = refs[:count], refs[-2 - many : -2], refs[-2], refs[-1]
    copies = [pltpu.make_async_copy(lines[m], held.at[m], sems.at[m]) for m in range(count)]
    part = held.shape[3]
    order = [lax.rem(start_ref[0] + k, SIDE) for k in range(SIDE)]

    @pl.when(pl.program_id(0) == 0)
    def _():
        for copy in copies:
            copy.start()

    for m in range(count):

        @pl.when(pl.program_id(0) == m)
        def _():
            copies[m].wait()
            weights = jnp.concatenate([held[m, k] for k in order], axis=1)
            product = jnp.dot(wide_ref[...], weights, preferred_element_type=jnp.float32)
            product = product.astype(jnp.bfloat16)
            for k in range(SIDE):
                piece = product[:, k * part : (k + 1) * part]
                if many == 1:
                    outs[0][k] = piece
                else:
                    outs[k][...] = piece


def forward(start, wide, lines, apart=False, places=1, into=None):
    tokens, depth = wide.shape
    part = lines[0].shape[2]
    count = len(lines)
    cols = count * part
    many = SIDE if apart else 1
    if apart:
        outs = [pltpu.HBM((tokens, cols), jnp.bfloat16)] * SIDE
        specs = [pl.BlockSpec((tokens, part), lambda i, n: (0, i))] * SIDE
    else:
        place = 0 if into is None else count
        outs = [pltpu.HBM((SIDE, tokens, places * cols), jnp.bfloat16)]
        specs = [pl.BlockSpec((SIDE, tokens, part), lambda i, n: (0, 0, place + i))]
    extra = [] if into is None else [into]
    made = pl.pallas_call(
        functools.partial(forward_kernel, count, many),
        out_shape=outs,
        grid_spec=pltpu.PrefetchScalarGridSpec(
            num_scalar_prefetch=1,
            grid=(count,),
            in_specs=[pl.BlockSpec(memory_space=pltpu.VMEM)]
            + [pl.BlockSpec(memory_space=pl.ANY)] * (count + len(extra)),
            out_specs=specs,
            scratch_shapes=[
                pltpu.VMEM((count, SIDE, depth, part), jnp.bfloat16),
                pltpu.SemaphoreType.DMA((count,)),
            ],
        ),
        input_output_aliases={} if into is None else {count + 2: 0},
        compiler_params=pltpu.CompilerParams(vmem_limit_bytes=24 << 20),
        cost_estimate=pl.CostEstimate(
            flops=tokens * depth * count * part,
            bytes_accessed=depth * part * count,
            transcendentals=0,
        ),
        name="forward",
    )(start, wide, *lines, *extra)
    return made if apart else made[0]


def arrange_kernel(far_ref, here_ref, *refs):
    besides, out_ref = refs[:2], refs[2]
    part = here_ref.shape[2] // 2
    far = far_ref[0]

    def total(ref, lane):
        parts = [ref[y, :, lane : lane + part].astype(jnp.float32) for y in range(SIDE)]
        return (parts[0] + parts[1] + parts[2] + parts[3]).astype(out_ref.dtype)

    for h in range(2):
        lanes = slice(h * part, (h + 1) * part)
        out_ref[far, :, lanes] = total(here_ref, h * part)
        out_ref[lax.rem(far + 1, SIDE), :, lanes] = total(besides[1 - h], h * part)
        out_ref[lax.rem(far + 3, SIDE), :, lanes] = total(besides[h], h * part)
        out_ref[lax.rem(far + 2, SIDE), :, lanes] = jnp.zeros_like(here_ref[0, :, lanes])


def arrange(far, *slots):
    tokens, cols = slots[0].shape[1:]
    rows = tokens // 2
    block = pl.BlockSpec((SIDE, rows, cols), lambda i, n: (0, i, 0))
    return pl.pallas_call(
        arrange_kernel,
        out_shape=pltpu.HBM(slots[0].shape, slots[0].dtype),
        grid_spec=pltpu.PrefetchScalarGridSpec(
            num_scalar_prefetch=1, grid=(2,), in_specs=[block] * 3, out_specs=block
        ),
        compiler_params=pltpu.CompilerParams(vmem_limit_bytes=16 << 20),
        cost_estimate=pl.CostEstimate(
            flops=4 * slots[0].size, bytes_accessed=8 * slots[0].size, transcendentals=0
        ),
        name="arrange",
    )(far, *slots)


def backward_kernel(count, first, last, spots_ref, *refs):
    lines, grads = refs[:count], refs[count : count * 5]
    weights = jnp.concatenate([line[k] for line in lines for k in range(SIDE)], axis=1)
    cols = jnp.concatenate([g[...] for g in grads], axis=1)
    product = lax.dot_general(
        cols, weights, (((1,), (1,)), ((), ())), preferred_element_type=jnp.float32
    )
    if first:
        refs[-1][...] = product.astype(jnp.bfloat16)
    elif not last:
        refs[-1][...] = (refs[-2][...].astype(jnp.float32) + product).astype(jnp.bfloat16)
    else:
        total = refs[-3][...].astype(jnp.float32) + product

        @pl.when(pl.program_id(0) < 2)
        def _():
            refs[-1][...] = total.astype(jnp.bfloat16)

        @pl.when(pl.program_id(0) >= 2)
        def _():
            refs[-2][...] = total


def backward(spots, grown, out_grad, lines, last=False):
    tokens = out_grad.shape[0]
    depth, part = lines[0].shape[1:]
    count = len(lines)
    block = depth // 4
    first = grown is None
    out_grad = pltpu.with_memory_space_constraint(out_grad, pltpu.HBM)

    def column(j):
        return pl.BlockSpec((tokens, part), lambda i, n: (0, n[j]))

    total = pl.BlockSpec((tokens, block), lambda i, n: (0, (i + 2) % 4))
    outs, specs = [pltpu.HBM((tokens, depth), jnp.bfloat16)], [total]
    if last:
        outs = [
            jax.ShapeDtypeStruct((tokens, depth // 2), jnp.float32),
            jax.ShapeDtypeStruct((tokens, depth // 2), jnp.bfloat16),
        ]
        specs = [
            pl.BlockSpec((tokens, block), lambda i, n: (0, jnp.maximum(i - 2, 0))),
            pl.BlockSpec((tokens, block), lambda i, n: (0, jnp.minimum(i, 1))),
        ]
    made = pl.pallas_call(
        functools.partial(backward_kernel, count, first, last),
        out_shape=outs,
        grid_spec=pltpu.PrefetchScalarGridSpec(
            num_scalar_prefetch=1,
            grid=(4,),
            in_specs=[pl.BlockSpec((SIDE, block, part), lambda i, n: (0, (i + 2) % 4, 0))] * count
            + [column(j) for j in range(count * SIDE)]
            + ([] if first else [total]),
            out_specs=specs,
        ),
        input_output_aliases={} if first or last else {5 * count + 1: 0},
        compiler_params=pltpu.CompilerParams(vmem_limit_bytes=28 << 20),
        cost_estimate=pl.CostEstimate(
            flops=tokens * depth * count * part,
            bytes_accessed=depth * part * count,
            transcendentals=0,
        ),
        name="backward",
    )(spots, *lines, *([out_grad] * (count * SIDE)), *([] if first else [pltpu.with_memory_space_constraint(grown, pltpu.HBM)]))
    return made if last else made[0]


def compose(logits, indices, vector_bank):
    weights = jax.nn.sigmoid(logits - logits[..., ::-1])
    levels = jnp.arange(vector_bank.shape[0], dtype=jnp.int32)
    picked = (indices[..., None] == levels).astype(jnp.float32)
    mixing = jnp.sum(picked * weights[..., None], axis=2)
    blocks = jnp.einsum("rjb,bc->rjc", mixing, vector_bank, precision=lax.Precision.HIGHEST)
    return (weights, picked, mixing, blocks.reshape(blocks.shape[0], -1))


def compose_back(grad_rows, weights, picked, mixing, vector_bank):
    blocks = grad_rows.reshape(mixing.shape[0], mixing.shape[1], -1)
    bank_part = jnp.einsum("rjb,rjc->bc", mixing, blocks, precision=lax.Precision.HIGHEST)
    projected = jnp.einsum("rjc,bc->rjb", blocks, vector_bank, precision=lax.Precision.HIGHEST)
    dots = jnp.sum(picked * projected[:, :, None, :], axis=3)
    logit_grad = weights * (dots - jnp.sum(weights * dots, axis=2, keepdims=True))
    return (bank_part, logit_grad)


def settle(piece, step, z, core):
    def from_second(parity):
        def move(x, z, y, c):
            if c == 1 and y % 2 == parity:
                return (x, z, (x + step) % SIDE, y // 2)
            return None

        return lax.ppermute(piece, BOTH, pairs(move))

    def move(x, z, y, c):
        return (x, z, y, 1) if c == 0 and (z + step) % SIDE >= 2 else None

    crossed = lax.ppermute(piece, BOTH, pairs(move))
    spot = (z + step) % SIDE
    first = jnp.where(core == 0, piece, crossed)
    first = jnp.where(spot // 2 == core, first, jnp.zeros_like(first))
    return first, spot % 2, [from_second(0), from_second(1)]


def local(attn_out, frozen_weight, vector_bank, logits_a, index_a, logits_b, index_b, out_grad):
    tokens, height = attn_out.shape
    shard = frozen_weight.shape[1]
    half, part = shard // 2, shard // 4
    f32, bf16 = jnp.float32, jnp.bfloat16
    dp, tensor = lax.axis_index("dp"), lax.axis_index("tensor")
    x, z, core = dp // SIDE, dp % SIDE, tensor % 2
    near, far = jnp.where(core == 0, x, z), jnp.where(core == 0, z, x)
    side = tensor // 2
    turned = ((SIDE - near) % SIDE).astype(jnp.int32).reshape(1)
    turned_here = ((SIDE - near + side) % SIDE).astype(jnp.int32).reshape(1)

    left, right = frozen_weight[:, :half], frozen_weight[:, half:]
    mine = jnp.where(core == 0, left, right)
    theirs = jnp.where(core == 0, right, left)
    swapped = lax.ppermute(theirs, "tensor", SWAP)
    shards = []
    for h in range(2):
        cols = slice(h * part, (h + 1) * part)
        shards.append(jnp.concatenate([mine[:, cols], swapped[:, cols]], axis=0))
    logits_a, logits_b, *shards = lax.optimization_barrier((logits_a, logits_b, *shards))
    lines = [jnp.stack(ring_gather(shards[h], 0, h)) for h in range(2)]
    def columns(i, h):
        far_at = (far + i) % SIDE
        spots = []
        for k in range(SIDE):
            near_at = (near + k) % SIDE
            x_at = jnp.where(core == 0, near_at, far_at)
            z_at = jnp.where(core == 0, far_at, near_at)
            spots.append((x_at * SIDE + z_at) * 4 + core * 2 + h)
        return spots

    def spots_of(chunks):
        return jnp.stack([s for i, h in chunks for s in columns(i, h)]).astype(jnp.int32)

    wide = jnp.concatenate([attn_out, lax.ppermute(attn_out, "tensor", SWAP)], axis=1)

    weights_a, picked_a, mixing_a, rows_a = compose(logits_a, index_a, vector_bank)
    weights_b, picked_b, mixing_b, rows_b = compose(logits_b, index_b, vector_bank)
    down_a, up_b = rows_a.astype(bf16), rows_b.astype(bf16)
    rank = down_a.shape[0]
    grad_cols = lax.dynamic_slice_in_dim(out_grad, tensor * height, height, 1)
    cols_by_cols = (((1,), (1,)), ((), ()))
    rows_by_rows = (((0,), (0,)), ((), ()))
    low_part = lax.dot_general(down_a, attn_out, cols_by_cols, preferred_element_type=f32)
    back_part = lax.dot_general(up_b, grad_cols, cols_by_cols, preferred_element_type=f32)
    totals = jnp.concatenate([low_part, back_part], axis=0)
    lines[1], totals = lax.optimization_barrier((lines[1], totals))
    below = [shift(line, 1, 1) for line in lines]
    above = [shift(line, 1, -1) for line in lines]
    totals = over_tensor(totals).astype(bf16)
    low_bf, back_bf = totals[:rank], totals[rank:]

    factor = adapter_scale / (tokens * lax.axis_size("dp"))
    grad_a = jnp.dot(back_bf, attn_out, preferred_element_type=f32)
    grad_b = jnp.dot(low_bf, grad_cols, preferred_element_type=f32)
    both = factor * jnp.concatenate([grad_a, grad_b], axis=0)
    here = [(0, 0), (0, 1)]
    beside = [[(3, 0), (1, 1)], [(1, 0), (3, 1)]]
    across = [(2, 0), (2, 1)]

    sent_here = forward(turned, wide, lines)
    sent_here, totals = lax.optimization_barrier((sent_here, totals))
    low_bf, back_bf = totals[:rank], totals[rank:]
    slots_here = exchange(sent_here, "tensor", LANES)
    grown = backward(after(spots_of(here), sent_here), None, out_grad, lines)
    below[0], above[1], grown, totals = lax.optimization_barrier(
        (below[0], above[1], grown, totals)
    )
    corner = [shift(below[0], 1, 1), shift(above[1], 1, -1)]
    blocks = [[lines[h], above[h], corner[h], below[h]] for h in range(2)]

    def take(chunks):
        return [blocks[h][i] for i, h in chunks]

    sent_first = forward(turned, wide, take(beside[0]))
    slots_here, sent_first = lax.optimization_barrier((slots_here, sent_first))
    slots_first = exchange(sent_first, "tensor", LANES)
    sent_second = forward(after(turned, sent_first), wide, take(beside[1]))
    slots_first, sent_second, both = lax.optimization_barrier((slots_first, sent_second, both))
    slots_second = exchange(sent_second, "tensor", LANES)
    both_parts = over_side(both, 0)
    chunks = beside[0] + beside[1]
    grown = backward(after(spots_of(chunks), sent_second), grown, out_grad, take(chunks))
    both = total_of(lax.optimization_barrier((*both_parts, grown))[:SIDE])
    slots = arrange(
        far.astype(jnp.int32).reshape(1), slots_here, slots_first, after(slots_second, grown, both)
    )
    both = with_partner(both, 1, slots)
    moved = exchange(slots, "tensor", LANES)
    sent = forward(after(turned_here, slots, both), wide, take(across), apart=True)
    arrived = [sent[0]]
    for step in range(1, SIDE):
        turns = [(t, (t + 2 * step) % 8) for t in range(8)]
        arrived.append(lax.ppermute(sent[step], "tensor", turns))
    piece = total_of([a.astype(f32) for a in arrived]).astype(bf16)
    both = with_partner(both, 2, *sent)
    bank_a, logit_grad_a = compose_back(both[:rank], weights_a, picked_a, mixing_a, vector_bank)
    bank_b, logit_grad_b = compose_back(both[rank:], weights_b, picked_b, mixing_b, vector_bank)
    bank_part = over_tensor(bank_a + bank_b, (1, 2))
    grown, other = backward(
        after(spots_of(across), *sent, bank_part), grown, out_grad, take(across), last=True
    )
    bank_grad = over_tensor(bank_part, (4,))
    crossed = lax.ppermute(jnp.where(core == 0, slots[2:], moved[:2]), "tensor", SWAP)
    firsts = jnp.where(core == 0, slots[:2], crossed)
    seconds = jnp.where(core == 0, crossed, moved[2:])

    first, place, second = settle(piece, 2, z, core)
    cols = []
    for s in range(2):
        cols.append(firsts[s] + jnp.where(place == s, first, jnp.zeros_like(first)))
        cols.append(seconds[s] + second[s])
    summed = jnp.concatenate(cols, axis=1)
    layer_out = (
        summed.astype(f32)
        + adapter_scale * lax.dot_general(low_bf, up_b, rows_by_rows, preferred_element_type=f32)
    ).astype(bf16)
    other = lax.ppermute(other, "tensor", SWAP)
    attn_grad = (
        grown
        + other.astype(f32)
        + adapter_scale * lax.dot_general(back_bf, down_a, rows_by_rows, preferred_element_type=f32)
    ).astype(bf16)
    return (layer_out, attn_grad, bank_grad, logit_grad_a, logit_grad_b)


def solution(mesh):
    return jax.shard_map(
        local,
        mesh=mesh,
        in_specs=(
            P("dp", "tensor"),
            P("tensor", "dp"),
            P(),
            P(None, "tensor", None),
            P(None, "tensor", None),
            P(None, "tensor", None),
            P(None, "tensor", None),
            P("dp", None),
        ),
        out_specs=(
            P("dp", "tensor"),
            P("dp", "tensor"),
            P(),
            P(None, "tensor", None),
            P(None, "tensor", None),
        ),
        check_vma=False,
    )
```

```python
import functools

import jax
import jax.numpy as jnp
from jax import lax
from jax.experimental import pallas as pl
from jax.experimental.pallas import tpu as pltpu
from jax.sharding import PartitionSpec as P

adapter_scale = 2.0
SIDE = 4
BOTH = ("dp", "tensor")
LANES = [[0, 2, 4, 6], [1, 3, 5, 7]]
SWAP = [(t, t ^ 1) for t in range(8)]


def device(x, z, y, c):
    return (x * SIDE + z) * 8 + y * 2 + c


def pairs(move):
    found = []
    for x in range(SIDE):
        for z in range(SIDE):
            for y in range(SIDE):
                for c in range(2):
                    to = move(x, z, y, c)
                    if to is not None:
                        found.append((device(x, z, y, c), device(*to)))
    return found


def ring(stage, step):
    def move(x, z, y, c):
        if (stage == 0) == (c == 0):
            return ((x + step) % SIDE, z, y, c)
        return (x, (z + step) % SIDE, y, c)

    return pairs(move)


def shift(value, stage, step):
    return lax.ppermute(value, BOTH, ring(stage, step))


def ring_gather(own, stage, h):
    below = shift(own, stage, 1)
    above = shift(own, stage, -1)
    across = shift(below, stage, 1) if h == 0 else shift(above, stage, -1)
    return [own, above, across, below]


def exchange(value, axis, groups=None):
    return lax.all_to_all(
        value, axis, split_axis=0, concat_axis=0, tiled=True, axis_index_groups=groups
    )


def over_tensor(value, bits=(1, 2, 4)):
    for bit in bits:
        value = value + lax.ppermute(value, "tensor", [(t, t ^ bit) for t in range(8)])
    return value


def over_side(value, axis):
    def from_step(step):
        def move(x, z, y, c):
            if axis == 0:
                return ((x + step) % SIDE, z, y, c)
            return (x, (z + step) % SIDE, y, c)

        return lax.ppermute(value, BOTH, pairs(move))

    return [value, from_step(1), from_step(2), from_step(3)]


def after(value, *events):
    return lax.optimization_barrier((value, *events))[0]


def with_partner(value, bit, *events):
    other = lax.ppermute(value, "dp", [(d, d ^ bit) for d in range(16)])
    return value + after(other, *events)


def total_of(parts):
    return (parts[0] + parts[2]) + (parts[1] + parts[3])


def forward_kernel(count, many, start_ref, wide_ref, *refs):
    lines, outs, held, sems = refs[:count], refs[-2 - many : -2], refs[-2], refs[-1]
    copies = [pltpu.make_async_copy(lines[m], held.at[m], sems.at[m]) for m in range(count)]
    part = held.shape[3]
    order = [lax.rem(start_ref[0] + k, SIDE) for k in range(SIDE)]

    @pl.when(pl.program_id(0) == 0)
    def _():
        for copy in copies:
            copy.start()

    for m in range(count):

        @pl.when(pl.program_id(0) == m)
        def _():
            copies[m].wait()
            weights = jnp.concatenate([held[m, k] for k in order], axis=1)
            product = jnp.dot(wide_ref[...], weights, preferred_element_type=jnp.float32)
            product = product.astype(jnp.bfloat16)
            for k in range(SIDE):
                piece = product[:, k * part : (k + 1) * part]
                if many == 1:
                    outs[0][k] = piece
                else:
                    outs[k][...] = piece


def forward(start, wide, lines, apart=False, places=1, into=None):
    tokens, depth = wide.shape
    part = lines[0].shape[2]
    count = len(lines)
    cols = count * part
    many = SIDE if apart else 1
    if apart:
        outs = [pltpu.HBM((tokens, cols), jnp.bfloat16)] * SIDE
        specs = [pl.BlockSpec((tokens, part), lambda i, n: (0, i))] * SIDE
    else:
        place = 0 if into is None else count
        outs = [pltpu.HBM((SIDE, tokens, places * cols), jnp.bfloat16)]
        specs = [pl.BlockSpec((SIDE, tokens, part), lambda i, n: (0, 0, place + i))]
    extra = [] if into is None else [into]
    made = pl.pallas_call(
        functools.partial(forward_kernel, count, many),
        out_shape=outs,
        grid_spec=pltpu.PrefetchScalarGridSpec(
            num_scalar_prefetch=1,
            grid=(count,),
            in_specs=[pl.BlockSpec(memory_space=pltpu.VMEM)]
            + [pl.BlockSpec(memory_space=pl.ANY)] * (count + len(extra)),
            out_specs=specs,
            scratch_shapes=[
                pltpu.VMEM((count, SIDE, depth, part), jnp.bfloat16),
                pltpu.SemaphoreType.DMA((count,)),
            ],
        ),
        input_output_aliases={} if into is None else {count + 2: 0},
        compiler_params=pltpu.CompilerParams(vmem_limit_bytes=24 << 20),
        cost_estimate=pl.CostEstimate(
            flops=tokens * depth * count * part,
            bytes_accessed=depth * part * count,
            transcendentals=0,
        ),
        name="forward",
    )(start, wide, *lines, *extra)
    return made if apart else made[0]


def arrange_kernel(far_ref, here_ref, *refs):
    besides, out_ref = refs[:2], refs[2]
    part = here_ref.shape[2] // 2
    far = far_ref[0]

    def total(ref, lane):
        parts = [ref[y, :, lane : lane + part].astype(jnp.float32) for y in range(SIDE)]
        return (parts[0] + parts[1] + parts[2] + parts[3]).astype(out_ref.dtype)

    for h in range(2):
        lanes = slice(h * part, (h + 1) * part)
        out_ref[far, :, lanes] = total(here_ref, h * part)
        out_ref[lax.rem(far + 1, SIDE), :, lanes] = total(besides[1 - h], h * part)
        out_ref[lax.rem(far + 3, SIDE), :, lanes] = total(besides[h], h * part)
        out_ref[lax.rem(far + 2, SIDE), :, lanes] = jnp.zeros_like(here_ref[0, :, lanes])


def arrange(far, *slots):
    tokens, cols = slots[0].shape[1:]
    rows = tokens // 2
    block = pl.BlockSpec((SIDE, rows, cols), lambda i, n: (0, i, 0))
    return pl.pallas_call(
        arrange_kernel,
        out_shape=pltpu.HBM(slots[0].shape, slots[0].dtype),
        grid_spec=pltpu.PrefetchScalarGridSpec(
            num_scalar_prefetch=1, grid=(2,), in_specs=[block] * 3, out_specs=block
        ),
        compiler_params=pltpu.CompilerParams(vmem_limit_bytes=16 << 20),
        cost_estimate=pl.CostEstimate(
            flops=4 * slots[0].size, bytes_accessed=8 * slots[0].size, transcendentals=0
        ),
        name="arrange",
    )(far, *slots)


def backward_kernel(count, first, last, spots_ref, *refs):
    lines, grads = refs[:count], refs[count : count * 5]
    weights = jnp.concatenate([line[k] for line in lines for k in range(SIDE)], axis=1)
    cols = jnp.concatenate([g[...] for g in grads], axis=1)
    product = lax.dot_general(
        cols, weights, (((1,), (1,)), ((), ())), preferred_element_type=jnp.float32
    )
    if first:
        refs[-1][...] = product.astype(jnp.bfloat16)
    elif not last:
        refs[-1][...] = (refs[-2][...].astype(jnp.float32) + product).astype(jnp.bfloat16)
    else:
        total = refs[-3][...].astype(jnp.float32) + product

        @pl.when(pl.program_id(0) < 2)
        def _():
            refs[-1][...] = total.astype(jnp.bfloat16)

        @pl.when(pl.program_id(0) >= 2)
        def _():
            refs[-2][...] = total


def backward(spots, grown, out_grad, lines, last=False):
    tokens = out_grad.shape[0]
    depth, part = lines[0].shape[1:]
    count = len(lines)
    block = depth // 4
    first = grown is None
    out_grad = pltpu.with_memory_space_constraint(out_grad, pltpu.HBM)

    def column(j):
        return pl.BlockSpec((tokens, part), lambda i, n: (0, n[j]))

    total = pl.BlockSpec((tokens, block), lambda i, n: (0, (i + 2) % 4))
    outs, specs = [pltpu.HBM((tokens, depth), jnp.bfloat16)], [total]
    if last:
        outs = [
            jax.ShapeDtypeStruct((tokens, depth // 2), jnp.float32),
            jax.ShapeDtypeStruct((tokens, depth // 2), jnp.bfloat16),
        ]
        specs = [
            pl.BlockSpec((tokens, block), lambda i, n: (0, jnp.maximum(i - 2, 0))),
            pl.BlockSpec((tokens, block), lambda i, n: (0, jnp.minimum(i, 1))),
        ]
    made = pl.pallas_call(
        functools.partial(backward_kernel, count, first, last),
        out_shape=outs,
        grid_spec=pltpu.PrefetchScalarGridSpec(
            num_scalar_prefetch=1,
            grid=(4,),
            in_specs=[pl.BlockSpec((SIDE, block, part), lambda i, n: (0, (i + 2) % 4, 0))] * count
            + [column(j) for j in range(count * SIDE)]
            + ([] if first else [total]),
            out_specs=specs,
        ),
        input_output_aliases={} if first or last else {5 * count + 1: 0},
        compiler_params=pltpu.CompilerParams(vmem_limit_bytes=28 << 20),
        cost_estimate=pl.CostEstimate(
            flops=tokens * depth * count * part,
            bytes_accessed=depth * part * count,
            transcendentals=0,
        ),
        name="backward",
    )(spots, *lines, *([out_grad] * (count * SIDE)), *([] if first else [pltpu.with_memory_space_constraint(grown, pltpu.HBM)]))
    return made if last else made[0]


def compose(logits, indices, vector_bank):
    weights = jax.nn.sigmoid(logits - logits[..., ::-1])
    levels = jnp.arange(vector_bank.shape[0], dtype=jnp.int32)
    picked = (indices[..., None] == levels).astype(jnp.float32)
    mixing = jnp.sum(picked * weights[..., None], axis=2)
    blocks = jnp.einsum("rjb,bc->rjc", mixing, vector_bank, precision=lax.Precision.HIGHEST)
    return (weights, picked, mixing, blocks.reshape(blocks.shape[0], -1))


def compose_back(grad_rows, weights, picked, mixing, vector_bank):
    blocks = grad_rows.reshape(mixing.shape[0], mixing.shape[1], -1)
    bank_part = jnp.einsum("rjb,rjc->bc", mixing, blocks, precision=lax.Precision.HIGHEST)
    projected = jnp.einsum("rjc,bc->rjb", blocks, vector_bank, precision=lax.Precision.HIGHEST)
    dots = jnp.sum(picked * projected[:, :, None, :], axis=3)
    logit_grad = weights * (dots - jnp.sum(weights * dots, axis=2, keepdims=True))
    return (bank_part, logit_grad)


def settle(piece, step, z, core):
    def from_second(parity):
        def move(x, z, y, c):
            if c == 1 and y % 2 == parity:
                return (x, z, (x + step) % SIDE, y // 2)
            return None

        return lax.ppermute(piece, BOTH, pairs(move))

    def move(x, z, y, c):
        return (x, z, y, 1) if c == 0 and (z + step) % SIDE >= 2 else None

    crossed = lax.ppermute(piece, BOTH, pairs(move))
    spot = (z + step) % SIDE
    first = jnp.where(core == 0, piece, crossed)
    first = jnp.where(spot // 2 == core, first, jnp.zeros_like(first))
    return first, spot % 2, [from_second(0), from_second(1)]


def local(attn_out, frozen_weight, vector_bank, logits_a, index_a, logits_b, index_b, out_grad):
    tokens, height = attn_out.shape
    shard = frozen_weight.shape[1]
    half, part = shard // 2, shard // 4
    f32, bf16 = jnp.float32, jnp.bfloat16
    dp, tensor = lax.axis_index("dp"), lax.axis_index("tensor")
    x, z, core = dp // SIDE, dp % SIDE, tensor % 2
    near, far = jnp.where(core == 0, x, z), jnp.where(core == 0, z, x)
    side = tensor // 2
    turned = ((SIDE - near) % SIDE).astype(jnp.int32).reshape(1)
    turned_here = ((SIDE - near + side) % SIDE).astype(jnp.int32).reshape(1)

    left, right = frozen_weight[:, :half], frozen_weight[:, half:]
    mine = jnp.where(core == 0, left, right)
    theirs = jnp.where(core == 0, right, left)
    swapped = lax.ppermute(theirs, "tensor", SWAP)
    shards = []
    for h in range(2):
        cols = slice(h * part, (h + 1) * part)
        shards.append(jnp.concatenate([mine[:, cols], swapped[:, cols]], axis=0))
    logits_a, logits_b, *shards = lax.optimization_barrier((logits_a, logits_b, *shards))
    lines = [jnp.stack(ring_gather(shards[h], 0, h)) for h in range(2)]
    def columns(i, h):
        far_at = (far + i) % SIDE
        spots = []
        for k in range(SIDE):
            near_at = (near + k) % SIDE
            x_at = jnp.where(core == 0, near_at, far_at)
            z_at = jnp.where(core == 0, far_at, near_at)
            spots.append((x_at * SIDE + z_at) * 4 + core * 2 + h)
        return spots

    def spots_of(chunks):
        return jnp.stack([s for i, h in chunks for s in columns(i, h)]).astype(jnp.int32)

    wide = jnp.concatenate([attn_out, lax.ppermute(attn_out, "tensor", SWAP)], axis=1)

    weights_a, picked_a, mixing_a, rows_a = compose(logits_a, index_a, vector_bank)
    weights_b, picked_b, mixing_b, rows_b = compose(logits_b, index_b, vector_bank)
    down_a, up_b = rows_a.astype(bf16), rows_b.astype(bf16)
    rank = down_a.shape[0]
    grad_cols = lax.dynamic_slice_in_dim(out_grad, tensor * height, height, 1)
    cols_by_cols = (((1,), (1,)), ((), ()))
    rows_by_rows = (((0,), (0,)), ((), ()))
    low_part = lax.dot_general(down_a, attn_out, cols_by_cols, preferred_element_type=f32)
    back_part = lax.dot_general(up_b, grad_cols, cols_by_cols, preferred_element_type=f32)
    totals = jnp.concatenate([low_part, back_part], axis=0)
    lines[1], totals = lax.optimization_barrier((lines[1], totals))
    below = [shift(line, 1, 1) for line in lines]
    above = [shift(line, 1, -1) for line in lines]
    totals = over_tensor(totals).astype(bf16)
    low_bf, back_bf = totals[:rank], totals[rank:]

    factor = adapter_scale / (tokens * lax.axis_size("dp"))
    grad_a = jnp.dot(back_bf, attn_out, preferred_element_type=f32)
    grad_b = jnp.dot(low_bf, grad_cols, preferred_element_type=f32)
    both = factor * jnp.concatenate([grad_a, grad_b], axis=0)
    here = [(0, 0), (0, 1)]
    beside = [[(3, 0), (1, 1)], [(1, 0), (3, 1)]]
    across = [(2, 0), (2, 1)]

    sent_here = forward(turned, wide, lines)
    sent_here, totals = lax.optimization_barrier((sent_here, totals))
    low_bf, back_bf = totals[:rank], totals[rank:]
    slots_here = exchange(sent_here, "tensor", LANES)
    grown = backward(after(spots_of(here), sent_here), None, out_grad, lines)
    below[0], above[1], grown, totals = lax.optimization_barrier(
        (below[0], above[1], grown, totals)
    )
    corner = [shift(below[0], 1, 1), shift(above[1], 1, -1)]
    blocks = [[lines[h], above[h], corner[h], below[h]] for h in range(2)]

    def take(chunks):
        return [blocks[h][i] for i, h in chunks]

    sent_first = forward(turned, wide, take(beside[0]))
    slots_here, sent_first = lax.optimization_barrier((slots_here, sent_first))
    slots_first = exchange(sent_first, "tensor", LANES)
    sent_second = forward(after(turned, sent_first), wide, take(beside[1]))
    slots_first, sent_second, both = lax.optimization_barrier((slots_first, sent_second, both))
    slots_second = exchange(sent_second, "tensor", LANES)
    both_parts = over_side(both, 0)
    chunks = beside[0] + beside[1]
    grown = backward(after(spots_of(chunks), sent_second), grown, out_grad, take(chunks))
    both = total_of(lax.optimization_barrier((*both_parts, grown))[:SIDE])
    slots = arrange(
        far.astype(jnp.int32).reshape(1), slots_here, slots_first, after(slots_second, grown, both)
    )
    moved = exchange(slots, "tensor", LANES)
    sent = forward(after(turned_here, slots), wide, take(across), apart=True)
    arrived = [sent[0]]
    for step in range(1, SIDE):
        turns = [(t, (t + 2 * step) % 8) for t in range(8)]
        arrived.append(lax.ppermute(sent[step], "tensor", turns))
    both = with_partner(both, 1, *sent)
    grown, other = backward(
        after(spots_of(across), *sent), grown, out_grad, take(across), last=True
    )
    both = with_partner(both, 2, other)
    arrived = lax.optimization_barrier((*arrived, other))[:SIDE]
    piece = total_of([a.astype(f32) for a in arrived]).astype(bf16)
    bank_a, logit_grad_a = compose_back(both[:rank], weights_a, picked_a, mixing_a, vector_bank)
    bank_b, logit_grad_b = compose_back(both[rank:], weights_b, picked_b, mixing_b, vector_bank)
    bank_grad = over_tensor(bank_a + bank_b)
    crossed = lax.ppermute(jnp.where(core == 0, slots[2:], moved[:2]), "tensor", SWAP)
    firsts = jnp.where(core == 0, slots[:2], crossed)
    seconds = jnp.where(core == 0, crossed, moved[2:])

    first, place, second = settle(piece, 2, z, core)
    cols = []
    for s in range(2):
        cols.append(firsts[s] + jnp.where(place == s, first, jnp.zeros_like(first)))
        cols.append(seconds[s] + second[s])
    summed = jnp.concatenate(cols, axis=1)
    layer_out = (
        summed.astype(f32)
        + adapter_scale * lax.dot_general(low_bf, up_b, rows_by_rows, preferred_element_type=f32)
    ).astype(bf16)
    other = lax.ppermute(other, "tensor", SWAP)
    attn_grad = (
        grown
        + other.astype(f32)
        + adapter_scale * lax.dot_general(back_bf, down_a, rows_by_rows, preferred_element_type=f32)
    ).astype(bf16)
    return (layer_out, attn_grad, bank_grad, logit_grad_a, logit_grad_b)


def solution(mesh):
    return jax.shard_map(
        local,
        mesh=mesh,
        in_specs=(
            P("dp", "tensor"),
            P("tensor", "dp"),
            P(),
            P(None, "tensor", None),
            P(None, "tensor", None),
            P(None, "tensor", None),
            P(None, "tensor", None),
            P("dp", None),
        ),
        out_specs=(
            P("dp", "tensor"),
            P("dp", "tensor"),
            P(),
            P(None, "tensor", None),
            P(None, "tensor", None),
        ),
        check_vma=False,
    )
```

```python
import functools

import jax
import jax.numpy as jnp
from jax import lax
from jax.experimental import pallas as pl
from jax.experimental.pallas import tpu as pltpu
from jax.sharding import PartitionSpec as P

adapter_scale = 2.0
SIDE = 4
BOTH = ("dp", "tensor")
LANES = [[0, 2, 4, 6], [1, 3, 5, 7]]
SWAP = [(t, t ^ 1) for t in range(8)]


def device(x, z, y, c):
    return (x * SIDE + z) * 8 + y * 2 + c


def pairs(move):
    found = []
    for x in range(SIDE):
        for z in range(SIDE):
            for y in range(SIDE):
                for c in range(2):
                    to = move(x, z, y, c)
                    if to is not None:
                        found.append((device(x, z, y, c), device(*to)))
    return found


def ring(stage, step):
    def move(x, z, y, c):
        if (stage == 0) == (c == 0):
            return ((x + step) % SIDE, z, y, c)
        return (x, (z + step) % SIDE, y, c)

    return pairs(move)


def shift(value, stage, step):
    return lax.ppermute(value, BOTH, ring(stage, step))


def ring_gather(own, stage, h):
    below = shift(own, stage, 1)
    above = shift(own, stage, -1)
    across = shift(below, stage, 1) if h == 0 else shift(above, stage, -1)
    return [own, above, across, below]


def exchange(value, axis, groups=None):
    return lax.all_to_all(
        value, axis, split_axis=0, concat_axis=0, tiled=True, axis_index_groups=groups
    )


def over_tensor(value, bits=(1, 2, 4)):
    for bit in bits:
        value = value + lax.ppermute(value, "tensor", [(t, t ^ bit) for t in range(8)])
    return value


def over_side(value, axis):
    def from_step(step):
        def move(x, z, y, c):
            if axis == 0:
                return ((x + step) % SIDE, z, y, c)
            return (x, (z + step) % SIDE, y, c)

        return lax.ppermute(value, BOTH, pairs(move))

    return [value, from_step(1), from_step(2), from_step(3)]


def after(value, *events):
    return lax.optimization_barrier((value, *events))[0]


def with_partner(value, bit, *events):
    other = lax.ppermute(value, "dp", [(d, d ^ bit) for d in range(16)])
    return value + after(other, *events)


def total_of(parts):
    return (parts[0] + parts[2]) + (parts[1] + parts[3])


def forward_kernel(count, many, start_ref, wide_ref, *refs):
    lines, outs, held, sems = refs[:count], refs[-2 - many : -2], refs[-2], refs[-1]
    copies = [pltpu.make_async_copy(lines[m], held.at[m], sems.at[m]) for m in range(count)]
    part = held.shape[3]
    order = [lax.rem(start_ref[0] + k, SIDE) for k in range(SIDE)]

    @pl.when(pl.program_id(0) == 0)
    def _():
        for copy in copies:
            copy.start()

    for m in range(count):

        @pl.when(pl.program_id(0) == m)
        def _():
            copies[m].wait()
            weights = jnp.concatenate([held[m, k] for k in order], axis=1)
            product = jnp.dot(wide_ref[...], weights, preferred_element_type=jnp.float32)
            product = product.astype(jnp.bfloat16)
            for k in range(SIDE):
                piece = product[:, k * part : (k + 1) * part]
                if many == 1:
                    outs[0][k] = piece
                else:
                    outs[k][...] = piece


def forward(start, wide, lines, apart=False, places=1, into=None):
    tokens, depth = wide.shape
    part = lines[0].shape[2]
    count = len(lines)
    cols = count * part
    many = SIDE if apart else 1
    if apart:
        outs = [pltpu.HBM((tokens, cols), jnp.bfloat16)] * SIDE
        specs = [pl.BlockSpec((tokens, part), lambda i, n: (0, i))] * SIDE
    else:
        place = 0 if into is None else count
        outs = [pltpu.HBM((SIDE, tokens, places * cols), jnp.bfloat16)]
        specs = [pl.BlockSpec((SIDE, tokens, part), lambda i, n: (0, 0, place + i))]
    extra = [] if into is None else [into]
    made = pl.pallas_call(
        functools.partial(forward_kernel, count, many),
        out_shape=outs,
        grid_spec=pltpu.PrefetchScalarGridSpec(
            num_scalar_prefetch=1,
            grid=(count,),
            in_specs=[pl.BlockSpec(memory_space=pltpu.VMEM)]
            + [pl.BlockSpec(memory_space=pl.ANY)] * (count + len(extra)),
            out_specs=specs,
            scratch_shapes=[
                pltpu.VMEM((count, SIDE, depth, part), jnp.bfloat16),
                pltpu.SemaphoreType.DMA((count,)),
            ],
        ),
        input_output_aliases={} if into is None else {count + 2: 0},
        compiler_params=pltpu.CompilerParams(vmem_limit_bytes=24 << 20),
        cost_estimate=pl.CostEstimate(
            flops=tokens * depth * count * part,
            bytes_accessed=depth * part * count,
            transcendentals=0,
        ),
        name="forward",
    )(start, wide, *lines, *extra)
    return made if apart else made[0]


def arrange_kernel(far_ref, here_ref, *refs):
    besides, out_ref = refs[:2], refs[2]
    part = here_ref.shape[2] // 2
    far = far_ref[0]

    def total(ref, lane):
        parts = [ref[y, :, lane : lane + part].astype(jnp.float32) for y in range(SIDE)]
        return (parts[0] + parts[1] + parts[2] + parts[3]).astype(out_ref.dtype)

    for h in range(2):
        lanes = slice(h * part, (h + 1) * part)
        out_ref[far, :, lanes] = total(here_ref, h * part)
        out_ref[lax.rem(far + 1, SIDE), :, lanes] = total(besides[1 - h], h * part)
        out_ref[lax.rem(far + 3, SIDE), :, lanes] = total(besides[h], h * part)
        out_ref[lax.rem(far + 2, SIDE), :, lanes] = jnp.zeros_like(here_ref[0, :, lanes])


def arrange(far, *slots):
    tokens, cols = slots[0].shape[1:]
    rows = tokens // 2
    block = pl.BlockSpec((SIDE, rows, cols), lambda i, n: (0, i, 0))
    return pl.pallas_call(
        arrange_kernel,
        out_shape=pltpu.HBM(slots[0].shape, slots[0].dtype),
        grid_spec=pltpu.PrefetchScalarGridSpec(
            num_scalar_prefetch=1, grid=(2,), in_specs=[block] * 3, out_specs=block
        ),
        compiler_params=pltpu.CompilerParams(vmem_limit_bytes=16 << 20),
        cost_estimate=pl.CostEstimate(
            flops=4 * slots[0].size, bytes_accessed=8 * slots[0].size, transcendentals=0
        ),
        name="arrange",
    )(far, *slots)


def backward_kernel(count, first, last, spots_ref, *refs):
    lines, grads = refs[:count], refs[count : count * 5]
    weights = jnp.concatenate([line[k] for line in lines for k in range(SIDE)], axis=1)
    cols = jnp.concatenate([g[...] for g in grads], axis=1)
    product = lax.dot_general(
        cols, weights, (((1,), (1,)), ((), ())), preferred_element_type=jnp.float32
    )
    if first:
        refs[-1][...] = product.astype(jnp.bfloat16)
    elif not last:
        refs[-1][...] = (refs[-2][...].astype(jnp.float32) + product).astype(jnp.bfloat16)
    else:
        total = refs[-3][...].astype(jnp.float32) + product

        @pl.when(pl.program_id(0) < 2)
        def _():
            refs[-1][...] = total.astype(jnp.bfloat16)

        @pl.when(pl.program_id(0) >= 2)
        def _():
            refs[-2][...] = total


def backward(spots, grown, out_grad, lines, last=False):
    tokens = out_grad.shape[0]
    depth, part = lines[0].shape[1:]
    count = len(lines)
    block = depth // 4
    first = grown is None
    out_grad = pltpu.with_memory_space_constraint(out_grad, pltpu.HBM)

    def column(j):
        return pl.BlockSpec((tokens, part), lambda i, n: (0, n[j]))

    total = pl.BlockSpec((tokens, block), lambda i, n: (0, (i + 2) % 4))
    outs, specs = [pltpu.HBM((tokens, depth), jnp.bfloat16)], [total]
    if last:
        outs = [
            jax.ShapeDtypeStruct((tokens, depth // 2), jnp.float32),
            jax.ShapeDtypeStruct((tokens, depth // 2), jnp.bfloat16),
        ]
        specs = [
            pl.BlockSpec((tokens, block), lambda i, n: (0, jnp.maximum(i - 2, 0))),
            pl.BlockSpec((tokens, block), lambda i, n: (0, jnp.minimum(i, 1))),
        ]
    made = pl.pallas_call(
        functools.partial(backward_kernel, count, first, last),
        out_shape=outs,
        grid_spec=pltpu.PrefetchScalarGridSpec(
            num_scalar_prefetch=1,
            grid=(4,),
            in_specs=[pl.BlockSpec((SIDE, block, part), lambda i, n: (0, (i + 2) % 4, 0))] * count
            + [column(j) for j in range(count * SIDE)]
            + ([] if first else [total]),
            out_specs=specs,
        ),
        input_output_aliases={} if first or last else {5 * count + 1: 0},
        compiler_params=pltpu.CompilerParams(vmem_limit_bytes=28 << 20),
        cost_estimate=pl.CostEstimate(
            flops=tokens * depth * count * part,
            bytes_accessed=depth * part * count,
            transcendentals=0,
        ),
        name="backward",
    )(spots, *lines, *([out_grad] * (count * SIDE)), *([] if first else [pltpu.with_memory_space_constraint(grown, pltpu.HBM)]))
    return made if last else made[0]


def compose(logits, indices, vector_bank):
    weights = jax.nn.sigmoid(logits - logits[..., ::-1])
    levels = jnp.arange(vector_bank.shape[0], dtype=jnp.int32)
    picked = (indices[..., None] == levels).astype(jnp.float32)
    mixing = jnp.sum(picked * weights[..., None], axis=2)
    blocks = jnp.einsum("rjb,bc->rjc", mixing, vector_bank, precision=lax.Precision.HIGHEST)
    return (weights, picked, mixing, blocks.reshape(blocks.shape[0], -1))


def compose_back(grad_rows, weights, picked, mixing, vector_bank):
    blocks = grad_rows.reshape(mixing.shape[0], mixing.shape[1], -1)
    bank_part = jnp.einsum("rjb,rjc->bc", mixing, blocks, precision=lax.Precision.HIGHEST)
    projected = jnp.einsum("rjc,bc->rjb", blocks, vector_bank, precision=lax.Precision.HIGHEST)
    dots = jnp.sum(picked * projected[:, :, None, :], axis=3)
    logit_grad = weights * (dots - jnp.sum(weights * dots, axis=2, keepdims=True))
    return (bank_part, logit_grad)


def settle(piece, step, z, core):
    def from_second(parity):
        def move(x, z, y, c):
            if c == 1 and y % 2 == parity:
                return (x, z, (x + step) % SIDE, y // 2)
            return None

        return lax.ppermute(piece, BOTH, pairs(move))

    def move(x, z, y, c):
        return (x, z, y, 1) if c == 0 and (z + step) % SIDE >= 2 else None

    crossed = lax.ppermute(piece, BOTH, pairs(move))
    spot = (z + step) % SIDE
    first = jnp.where(core == 0, piece, crossed)
    first = jnp.where(spot // 2 == core, first, jnp.zeros_like(first))
    return first, spot % 2, [from_second(0), from_second(1)]


def local(attn_out, frozen_weight, vector_bank, logits_a, index_a, logits_b, index_b, out_grad):
    tokens, height = attn_out.shape
    shard = frozen_weight.shape[1]
    half, part = shard // 2, shard // 4
    f32, bf16 = jnp.float32, jnp.bfloat16
    dp, tensor = lax.axis_index("dp"), lax.axis_index("tensor")
    x, z, core = dp // SIDE, dp % SIDE, tensor % 2
    near, far = jnp.where(core == 0, x, z), jnp.where(core == 0, z, x)
    side = tensor // 2
    turned = ((SIDE - near) % SIDE).astype(jnp.int32).reshape(1)
    turned_here = ((SIDE - near + side) % SIDE).astype(jnp.int32).reshape(1)

    left, right = frozen_weight[:, :half], frozen_weight[:, half:]
    mine = jnp.where(core == 0, left, right)
    theirs = jnp.where(core == 0, right, left)
    swapped = lax.ppermute(theirs, "tensor", SWAP)
    shards = []
    for h in range(2):
        cols = slice(h * part, (h + 1) * part)
        shards.append(jnp.concatenate([mine[:, cols], swapped[:, cols]], axis=0))
    logits_a, logits_b, *shards = lax.optimization_barrier((logits_a, logits_b, *shards))
    lines = [jnp.stack(ring_gather(shards[h], 0, h)) for h in range(2)]
    def columns(i, h):
        far_at = (far + i) % SIDE
        spots = []
        for k in range(SIDE):
            near_at = (near + k) % SIDE
            x_at = jnp.where(core == 0, near_at, far_at)
            z_at = jnp.where(core == 0, far_at, near_at)
            spots.append((x_at * SIDE + z_at) * 4 + core * 2 + h)
        return spots

    def spots_of(chunks):
        return jnp.stack([s for i, h in chunks for s in columns(i, h)]).astype(jnp.int32)

    wide = jnp.concatenate([attn_out, lax.ppermute(attn_out, "tensor", SWAP)], axis=1)

    weights_a, picked_a, mixing_a, rows_a = compose(logits_a, index_a, vector_bank)
    weights_b, picked_b, mixing_b, rows_b = compose(logits_b, index_b, vector_bank)
    down_a, up_b = rows_a.astype(bf16), rows_b.astype(bf16)
    rank = down_a.shape[0]
    grad_cols = lax.dynamic_slice_in_dim(out_grad, tensor * height, height, 1)
    cols_by_cols = (((1,), (1,)), ((), ()))
    rows_by_rows = (((0,), (0,)), ((), ()))
    low_part = lax.dot_general(down_a, attn_out, cols_by_cols, preferred_element_type=f32)
    back_part = lax.dot_general(up_b, grad_cols, cols_by_cols, preferred_element_type=f32)
    totals = jnp.concatenate([low_part, back_part], axis=0)
    lines[1], totals = lax.optimization_barrier((lines[1], totals))
    below = [shift(line, 1, 1) for line in lines]
    above = [shift(line, 1, -1) for line in lines]
    totals = over_tensor(totals).astype(bf16)
    low_bf, back_bf = totals[:rank], totals[rank:]

    factor = adapter_scale / (tokens * lax.axis_size("dp"))
    grad_a = jnp.dot(back_bf, attn_out, preferred_element_type=f32)
    grad_b = jnp.dot(low_bf, grad_cols, preferred_element_type=f32)
    both = factor * jnp.concatenate([grad_a, grad_b], axis=0)
    here = [(0, 0), (0, 1)]
    beside = [[(3, 0), (1, 1)], [(1, 0), (3, 1)]]
    across = [(2, 0), (2, 1)]

    sent_here = forward(turned, wide, lines)
    sent_here, totals = lax.optimization_barrier((sent_here, totals))
    low_bf, back_bf = totals[:rank], totals[rank:]
    slots_here = exchange(sent_here, "tensor", LANES)
    grown = backward(after(spots_of(here), sent_here), None, out_grad, lines)
    below[0], above[1], grown, totals = lax.optimization_barrier(
        (below[0], above[1], grown, totals)
    )
    corner = [shift(below[0], 1, 1), shift(above[1], 1, -1)]
    blocks = [[lines[h], above[h], corner[h], below[h]] for h in range(2)]

    def take(chunks):
        return [blocks[h][i] for i, h in chunks]

    sent_first = forward(turned, wide, take(beside[0]))
    slots_here, sent_first = lax.optimization_barrier((slots_here, sent_first))
    slots_first = exchange(sent_first, "tensor", LANES)
    sent_second = forward(after(turned, sent_first), wide, take(beside[1]))
    slots_first, sent_second, both = lax.optimization_barrier((slots_first, sent_second, both))
    slots_second = exchange(sent_second, "tensor", LANES)
    both_parts = over_side(both, 0)
    chunks = beside[0] + beside[1]
    grown = backward(after(spots_of(chunks), sent_second), grown, out_grad, take(chunks))
    both = total_of(lax.optimization_barrier((*both_parts, grown))[:SIDE])
    slots = arrange(
        far.astype(jnp.int32).reshape(1), slots_here, slots_first, after(slots_second, grown, both)
    )
    moved = exchange(slots, "tensor", LANES)
    sent = forward(after(turned_here, slots), wide, take(across), apart=True)
    arrived = [sent[0]]
    for step in range(1, SIDE):
        turns = [(t, (t + 2 * step) % 8) for t in range(8)]
        arrived.append(lax.ppermute(sent[step], "tensor", turns))
    both = with_partner(both, 1, *sent)
    both = with_partner(both, 2)
    bank_a, logit_grad_a = compose_back(both[:rank], weights_a, picked_a, mixing_a, vector_bank)
    bank_b, logit_grad_b = compose_back(both[rank:], weights_b, picked_b, mixing_b, vector_bank)
    bank_part = bank_a + bank_b
    grown, other = backward(
        after(spots_of(across), *sent, bank_part), grown, out_grad, take(across), last=True
    )
    moved, *arrived = lax.optimization_barrier((moved, *arrived, other))[: SIDE + 1]
    piece = total_of([a.astype(f32) for a in arrived]).astype(bf16)
    bank_part = bank_part + after(lax.ppermute(bank_part, "tensor", SWAP), other)
    bank_grad = over_tensor(bank_part, (2, 4))
    crossed = lax.ppermute(jnp.where(core == 0, slots[2:], moved[:2]), "tensor", SWAP)
    firsts = jnp.where(core == 0, slots[:2], crossed)
    seconds = jnp.where(core == 0, crossed, moved[2:])

    first, place, second = settle(piece, 2, z, core)
    cols = []
    for s in range(2):
        cols.append(firsts[s] + jnp.where(place == s, first, jnp.zeros_like(first)))
        cols.append(seconds[s] + second[s])
    summed = jnp.concatenate(cols, axis=1)
    layer_out = (
        summed.astype(f32)
        + adapter_scale * lax.dot_general(low_bf, up_b, rows_by_rows, preferred_element_type=f32)
    ).astype(bf16)
    other = lax.ppermute(other, "tensor", SWAP)
    attn_grad = (
        grown
        + other.astype(f32)
        + adapter_scale * lax.dot_general(back_bf, down_a, rows_by_rows, preferred_element_type=f32)
    ).astype(bf16)
    return (layer_out, attn_grad, bank_grad, logit_grad_a, logit_grad_b)


def solution(mesh):
    return jax.shard_map(
        local,
        mesh=mesh,
        in_specs=(
            P("dp", "tensor"),
            P("tensor", "dp"),
            P(),
            P(None, "tensor", None),
            P(None, "tensor", None),
            P(None, "tensor", None),
            P(None, "tensor", None),
            P("dp", None),
        ),
        out_specs=(
            P("dp", "tensor"),
            P("dp", "tensor"),
            P(),
            P(None, "tensor", None),
            P(None, "tensor", None),
        ),
        check_vma=False,
    )
```

```python
import functools

import jax
import jax.numpy as jnp
from jax import lax
from jax.experimental import pallas as pl
from jax.experimental.pallas import tpu as pltpu
from jax.sharding import PartitionSpec as P

adapter_scale = 2.0
SIDE = 4
BOTH = ("dp", "tensor")
LANES = [[0, 2, 4, 6], [1, 3, 5, 7]]
SWAP = [(t, t ^ 1) for t in range(8)]


def device(x, z, y, c):
    return (x * SIDE + z) * 8 + y * 2 + c


def pairs(move):
    found = []
    for x in range(SIDE):
        for z in range(SIDE):
            for y in range(SIDE):
                for c in range(2):
                    to = move(x, z, y, c)
                    if to is not None:
                        found.append((device(x, z, y, c), device(*to)))
    return found


def ring(stage, step):
    def move(x, z, y, c):
        if (stage == 0) == (c == 0):
            return ((x + step) % SIDE, z, y, c)
        return (x, (z + step) % SIDE, y, c)

    return pairs(move)


def shift(value, stage, step):
    return lax.ppermute(value, BOTH, ring(stage, step))


def ring_gather(own, stage, h):
    below = shift(own, stage, 1)
    above = shift(own, stage, -1)
    across = shift(below, stage, 1) if h == 0 else shift(above, stage, -1)
    return [own, above, across, below]


def exchange(value, axis, groups=None):
    return lax.all_to_all(
        value, axis, split_axis=0, concat_axis=0, tiled=True, axis_index_groups=groups
    )


def over_tensor(value, bits=(1, 2, 4)):
    for bit in bits:
        value = value + lax.ppermute(value, "tensor", [(t, t ^ bit) for t in range(8)])
    return value


def over_side(value, axis):
    def from_step(step):
        def move(x, z, y, c):
            if axis == 0:
                return ((x + step) % SIDE, z, y, c)
            return (x, (z + step) % SIDE, y, c)

        return lax.ppermute(value, BOTH, pairs(move))

    return [value, from_step(1), from_step(2), from_step(3)]


def after(value, *events):
    return lax.optimization_barrier((value, *events))[0]


def with_partner(value, bit, *events):
    other = lax.ppermute(value, "dp", [(d, d ^ bit) for d in range(16)])
    return value + after(other, *events)


def total_of(parts):
    return (parts[0] + parts[2]) + (parts[1] + parts[3])


def forward_kernel(count, many, start_ref, wide_ref, *refs):
    lines, outs, held, sems = refs[:count], refs[-2 - many : -2], refs[-2], refs[-1]
    copies = [pltpu.make_async_copy(lines[m], held.at[m], sems.at[m]) for m in range(count)]
    part = held.shape[3]
    order = [lax.rem(start_ref[0] + k, SIDE) for k in range(SIDE)]

    @pl.when(pl.program_id(0) == 0)
    def _():
        for copy in copies:
            copy.start()

    for m in range(count):

        @pl.when(pl.program_id(0) == m)
        def _():
            copies[m].wait()
            weights = jnp.concatenate([held[m, k] for k in order], axis=1)
            product = jnp.dot(wide_ref[...], weights, preferred_element_type=jnp.float32)
            product = product.astype(jnp.bfloat16)
            for k in range(SIDE):
                piece = product[:, k * part : (k + 1) * part]
                if many == 1:
                    outs[0][k] = piece
                else:
                    outs[k][...] = piece


def forward(start, wide, lines, apart=False, places=1, into=None):
    tokens, depth = wide.shape
    part = lines[0].shape[2]
    count = len(lines)
    cols = count * part
    many = SIDE if apart else 1
    if apart:
        outs = [pltpu.HBM((tokens, cols), jnp.bfloat16)] * SIDE
        specs = [pl.BlockSpec((tokens, part), lambda i, n: (0, i))] * SIDE
    else:
        place = 0 if into is None else count
        outs = [pltpu.HBM((SIDE, tokens, places * cols), jnp.bfloat16)]
        specs = [pl.BlockSpec((SIDE, tokens, part), lambda i, n: (0, 0, place + i))]
    extra = [] if into is None else [into]
    made = pl.pallas_call(
        functools.partial(forward_kernel, count, many),
        out_shape=outs,
        grid_spec=pltpu.PrefetchScalarGridSpec(
            num_scalar_prefetch=1,
            grid=(count,),
            in_specs=[pl.BlockSpec(memory_space=pltpu.VMEM)]
            + [pl.BlockSpec(memory_space=pl.ANY)] * (count + len(extra)),
            out_specs=specs,
            scratch_shapes=[
                pltpu.VMEM((count, SIDE, depth, part), jnp.bfloat16),
                pltpu.SemaphoreType.DMA((count,)),
            ],
        ),
        input_output_aliases={} if into is None else {count + 2: 0},
        compiler_params=pltpu.CompilerParams(vmem_limit_bytes=24 << 20),
        cost_estimate=pl.CostEstimate(
            flops=tokens * depth * count * part,
            bytes_accessed=depth * part * count,
            transcendentals=0,
        ),
        name="forward",
    )(start, wide, *lines, *extra)
    return made if apart else made[0]


def arrange_kernel(far_ref, here_ref, *refs):
    besides, out_ref = refs[:2], refs[2]
    part = here_ref.shape[2] // 2
    far = far_ref[0]

    def total(ref, lane):
        parts = [ref[y, :, lane : lane + part].astype(jnp.float32) for y in range(SIDE)]
        return (parts[0] + parts[1] + parts[2] + parts[3]).astype(out_ref.dtype)

    for h in range(2):
        lanes = slice(h * part, (h + 1) * part)
        out_ref[far, :, lanes] = total(here_ref, h * part)
        out_ref[lax.rem(far + 1, SIDE), :, lanes] = total(besides[1 - h], h * part)
        out_ref[lax.rem(far + 3, SIDE), :, lanes] = total(besides[h], h * part)
        out_ref[lax.rem(far + 2, SIDE), :, lanes] = jnp.zeros_like(here_ref[0, :, lanes])


def arrange(far, *slots):
    tokens, cols = slots[0].shape[1:]
    rows = tokens // 2
    block = pl.BlockSpec((SIDE, rows, cols), lambda i, n: (0, i, 0))
    return pl.pallas_call(
        arrange_kernel,
        out_shape=pltpu.HBM(slots[0].shape, slots[0].dtype),
        grid_spec=pltpu.PrefetchScalarGridSpec(
            num_scalar_prefetch=1, grid=(2,), in_specs=[block] * 3, out_specs=block
        ),
        compiler_params=pltpu.CompilerParams(vmem_limit_bytes=16 << 20),
        cost_estimate=pl.CostEstimate(
            flops=4 * slots[0].size, bytes_accessed=8 * slots[0].size, transcendentals=0
        ),
        name="arrange",
    )(far, *slots)


def backward_kernel(count, first, last, spots_ref, *refs):
    lines, grads = refs[:count], refs[count : count * 5]
    weights = jnp.concatenate([line[k] for line in lines for k in range(SIDE)], axis=1)
    cols = jnp.concatenate([g[...] for g in grads], axis=1)
    product = lax.dot_general(
        cols, weights, (((1,), (1,)), ((), ())), preferred_element_type=jnp.float32
    )
    if first:
        refs[-1][...] = product.astype(jnp.bfloat16)
    elif not last:
        refs[-1][...] = (refs[-2][...].astype(jnp.float32) + product).astype(jnp.bfloat16)
    else:
        total = refs[-3][...].astype(jnp.float32) + product

        @pl.when(pl.program_id(0) < 2)
        def _():
            refs[-1][...] = total.astype(jnp.bfloat16)

        @pl.when(pl.program_id(0) >= 2)
        def _():
            refs[-2][...] = total


def backward(spots, grown, out_grad, lines, last=False):
    tokens = out_grad.shape[0]
    depth, part = lines[0].shape[1:]
    count = len(lines)
    block = depth // 4
    first = grown is None
    out_grad = pltpu.with_memory_space_constraint(out_grad, pltpu.HBM)

    def column(j):
        return pl.BlockSpec((tokens, part), lambda i, n: (0, n[j]))

    total = pl.BlockSpec((tokens, block), lambda i, n: (0, (i + 2) % 4))
    outs, specs = [pltpu.HBM((tokens, depth), jnp.bfloat16)], [total]
    if last:
        outs = [
            jax.ShapeDtypeStruct((tokens, depth // 2), jnp.float32),
            jax.ShapeDtypeStruct((tokens, depth // 2), jnp.bfloat16),
        ]
        specs = [
            pl.BlockSpec((tokens, block), lambda i, n: (0, jnp.maximum(i - 2, 0))),
            pl.BlockSpec((tokens, block), lambda i, n: (0, jnp.minimum(i, 1))),
        ]
    made = pl.pallas_call(
        functools.partial(backward_kernel, count, first, last),
        out_shape=outs,
        grid_spec=pltpu.PrefetchScalarGridSpec(
            num_scalar_prefetch=1,
            grid=(4,),
            in_specs=[pl.BlockSpec((SIDE, block, part), lambda i, n: (0, (i + 2) % 4, 0))] * count
            + [column(j) for j in range(count * SIDE)]
            + ([] if first else [total]),
            out_specs=specs,
        ),
        input_output_aliases={} if first or last else {5 * count + 1: 0},
        compiler_params=pltpu.CompilerParams(vmem_limit_bytes=28 << 20),
        cost_estimate=pl.CostEstimate(
            flops=tokens * depth * count * part,
            bytes_accessed=depth * part * count,
            transcendentals=0,
        ),
        name="backward",
    )(spots, *lines, *([out_grad] * (count * SIDE)), *([] if first else [pltpu.with_memory_space_constraint(grown, pltpu.HBM)]))
    return made if last else made[0]


def compose(logits, indices, vector_bank):
    weights = jax.nn.sigmoid(logits - logits[..., ::-1])
    levels = jnp.arange(vector_bank.shape[0], dtype=jnp.int32)
    picked = (indices[..., None] == levels).astype(jnp.float32)
    mixing = jnp.sum(picked * weights[..., None], axis=2)
    blocks = jnp.einsum("rjb,bc->rjc", mixing, vector_bank, precision=lax.Precision.HIGHEST)
    return (weights, picked, mixing, blocks.reshape(blocks.shape[0], -1))


def compose_back(grad_rows, weights, picked, mixing, vector_bank):
    blocks = grad_rows.reshape(mixing.shape[0], mixing.shape[1], -1)
    bank_part = jnp.einsum("rjb,rjc->bc", mixing, blocks, precision=lax.Precision.HIGHEST)
    projected = jnp.einsum("rjc,bc->rjb", blocks, vector_bank, precision=lax.Precision.HIGHEST)
    dots = jnp.sum(picked * projected[:, :, None, :], axis=3)
    logit_grad = weights * (dots - jnp.sum(weights * dots, axis=2, keepdims=True))
    return (bank_part, logit_grad)


def settle(piece, step, z, core):
    def from_second(parity):
        def move(x, z, y, c):
            if c == 1 and y % 2 == parity:
                return (x, z, (x + step) % SIDE, y // 2)
            return None

        return lax.ppermute(piece, BOTH, pairs(move))

    def move(x, z, y, c):
        return (x, z, y, 1) if c == 0 and (z + step) % SIDE >= 2 else None

    crossed = lax.ppermute(piece, BOTH, pairs(move))
    spot = (z + step) % SIDE
    first = jnp.where(core == 0, piece, crossed)
    first = jnp.where(spot // 2 == core, first, jnp.zeros_like(first))
    return first, spot % 2, [from_second(0), from_second(1)]


def local(attn_out, frozen_weight, vector_bank, logits_a, index_a, logits_b, index_b, out_grad):
    tokens, height = attn_out.shape
    shard = frozen_weight.shape[1]
    half, part = shard // 2, shard // 4
    f32, bf16 = jnp.float32, jnp.bfloat16
    dp, tensor = lax.axis_index("dp"), lax.axis_index("tensor")
    x, z, core = dp // SIDE, dp % SIDE, tensor % 2
    near, far = jnp.where(core == 0, x, z), jnp.where(core == 0, z, x)
    side = tensor // 2
    turned = ((SIDE - near) % SIDE).astype(jnp.int32).reshape(1)
    turned_here = ((SIDE - near + side) % SIDE).astype(jnp.int32).reshape(1)

    left, right = frozen_weight[:, :half], frozen_weight[:, half:]
    mine = jnp.where(core == 0, left, right)
    theirs = jnp.where(core == 0, right, left)
    swapped = lax.ppermute(theirs, "tensor", SWAP)
    shards = []
    for h in range(2):
        cols = slice(h * part, (h + 1) * part)
        shards.append(jnp.concatenate([mine[:, cols], swapped[:, cols]], axis=0))
    logits_a, logits_b, *shards = lax.optimization_barrier((logits_a, logits_b, *shards))
    lines = [jnp.stack(ring_gather(shards[h], 0, h)) for h in range(2)]
    def columns(i, h):
        far_at = (far + i) % SIDE
        spots = []
        for k in range(SIDE):
            near_at = (near + k) % SIDE
            x_at = jnp.where(core == 0, near_at, far_at)
            z_at = jnp.where(core == 0, far_at, near_at)
            spots.append((x_at * SIDE + z_at) * 4 + core * 2 + h)
        return spots

    def spots_of(chunks):
        return jnp.stack([s for i, h in chunks for s in columns(i, h)]).astype(jnp.int32)

    wide = jnp.concatenate([attn_out, lax.ppermute(attn_out, "tensor", SWAP)], axis=1)

    weights_a, picked_a, mixing_a, rows_a = compose(logits_a, index_a, vector_bank)
    weights_b, picked_b, mixing_b, rows_b = compose(logits_b, index_b, vector_bank)
    down_a, up_b = rows_a.astype(bf16), rows_b.astype(bf16)
    rank = down_a.shape[0]
    grad_cols = lax.dynamic_slice_in_dim(out_grad, tensor * height, height, 1)
    cols_by_cols = (((1,), (1,)), ((), ()))
    rows_by_rows = (((0,), (0,)), ((), ()))
    low_part = lax.dot_general(down_a, attn_out, cols_by_cols, preferred_element_type=f32)
    back_part = lax.dot_general(up_b, grad_cols, cols_by_cols, preferred_element_type=f32)
    totals = jnp.concatenate([low_part, back_part], axis=0)
    lines[1], totals = lax.optimization_barrier((lines[1], totals))
    below = [shift(line, 1, 1) for line in lines]
    above = [shift(line, 1, -1) for line in lines]
    totals = over_tensor(totals).astype(bf16)
    low_bf, back_bf = totals[:rank], totals[rank:]

    factor = adapter_scale / (tokens * lax.axis_size("dp"))
    grad_a = jnp.dot(back_bf, attn_out, preferred_element_type=f32)
    grad_b = jnp.dot(low_bf, grad_cols, preferred_element_type=f32)
    both = factor * jnp.concatenate([grad_a, grad_b], axis=0)
    here = [(0, 0), (0, 1)]
    beside = [[(3, 0), (1, 1)], [(1, 0), (3, 1)]]
    across = [(2, 0), (2, 1)]

    sent_here = forward(turned, wide, lines)
    sent_here, totals = lax.optimization_barrier((sent_here, totals))
    low_bf, back_bf = totals[:rank], totals[rank:]
    slots_here = exchange(sent_here, "tensor", LANES)
    grown = backward(after(spots_of(here), sent_here), None, out_grad, lines)
    below[0], above[1], grown, totals = lax.optimization_barrier(
        (below[0], above[1], grown, totals)
    )
    corner = [shift(below[0], 1, 1), shift(above[1], 1, -1)]
    blocks = [[lines[h], above[h], corner[h], below[h]] for h in range(2)]

    def take(chunks):
        return [blocks[h][i] for i, h in chunks]

    sent_first = forward(turned, wide, take(beside[0]))
    slots_here, sent_first = lax.optimization_barrier((slots_here, sent_first))
    slots_first = exchange(sent_first, "tensor", LANES)
    sent_second = forward(after(turned, sent_first), wide, take(beside[1]))
    slots_first, sent_second, both = lax.optimization_barrier((slots_first, sent_second, both))
    slots_second = exchange(sent_second, "tensor", LANES)
    both_parts = over_side(both, 0)
    chunks = beside[0] + beside[1]
    grown = backward(after(spots_of(chunks), sent_second), grown, out_grad, take(chunks))
    both = total_of(lax.optimization_barrier((*both_parts, grown))[:SIDE])
    slots = arrange(
        far.astype(jnp.int32).reshape(1), slots_here, slots_first, after(slots_second, grown, both)
    )
    moved = exchange(slots, "tensor", LANES)
    sent = forward(after(turned_here, slots), wide, take(across), apart=True)
    arrived = [sent[0]]
    for step in range(1, SIDE):
        turns = [(t, (t + 2 * step) % 8) for t in range(8)]
        arrived.append(lax.ppermute(sent[step], "tensor", turns))
    piece = total_of([a.astype(f32) for a in arrived]).astype(bf16)
    both = with_partner(with_partner(both, 1, *sent), 2, *arrived)
    bank_a, logit_grad_a = compose_back(both[:rank], weights_a, picked_a, mixing_a, vector_bank)
    bank_b, logit_grad_b = compose_back(both[rank:], weights_b, picked_b, mixing_b, vector_bank)
    bank_part = over_tensor(bank_a + bank_b, (1, 2))
    grown, other = backward(
        after(spots_of(across), *sent, bank_part), grown, out_grad, take(across), last=True
    )
    bank_grad = over_tensor(bank_part, (4,))
    crossed = lax.ppermute(jnp.where(core == 0, slots[2:], moved[:2]), "tensor", SWAP)
    firsts = jnp.where(core == 0, slots[:2], crossed)
    seconds = jnp.where(core == 0, crossed, moved[2:])

    first, place, second = settle(piece, 2, z, core)
    cols = []
    for s in range(2):
        cols.append(firsts[s] + jnp.where(place == s, first, jnp.zeros_like(first)))
        cols.append(seconds[s] + second[s])
    summed = jnp.concatenate(cols, axis=1)
    layer_out = (
        summed.astype(f32)
        + adapter_scale * lax.dot_general(low_bf, up_b, rows_by_rows, preferred_element_type=f32)
    ).astype(bf16)
    other = lax.ppermute(other, "tensor", SWAP)
    attn_grad = (
        grown
        + other.astype(f32)
        + adapter_scale * lax.dot_general(back_bf, down_a, rows_by_rows, preferred_element_type=f32)
    ).astype(bf16)
    return (layer_out, attn_grad, bank_grad, logit_grad_a, logit_grad_b)


def solution(mesh):
    return jax.shard_map(
        local,
        mesh=mesh,
        in_specs=(
            P("dp", "tensor"),
            P("tensor", "dp"),
            P(),
            P(None, "tensor", None),
            P(None, "tensor", None),
            P(None, "tensor", None),
            P(None, "tensor", None),
            P("dp", None),
        ),
        out_specs=(
            P("dp", "tensor"),
            P("dp", "tensor"),
            P(),
            P(None, "tensor", None),
            P(None, "tensor", None),
        ),
        check_vma=False,
    )
```

```python
import functools

import jax
import jax.numpy as jnp
from jax import lax
from jax.experimental import pallas as pl
from jax.experimental.pallas import tpu as pltpu
from jax.sharding import PartitionSpec as P

adapter_scale = 2.0
SIDE = 4
BOTH = ("dp", "tensor")
LANES = [[0, 2, 4, 6], [1, 3, 5, 7]]
SWAP = [(t, t ^ 1) for t in range(8)]


def device(x, z, y, c):
    return (x * SIDE + z) * 8 + y * 2 + c


def pairs(move):
    found = []
    for x in range(SIDE):
        for z in range(SIDE):
            for y in range(SIDE):
                for c in range(2):
                    to = move(x, z, y, c)
                    if to is not None:
                        found.append((device(x, z, y, c), device(*to)))
    return found


def ring(stage, step):
    def move(x, z, y, c):
        if (stage == 0) == (c == 0):
            return ((x + step) % SIDE, z, y, c)
        return (x, (z + step) % SIDE, y, c)

    return pairs(move)


def shift(value, stage, step):
    return lax.ppermute(value, BOTH, ring(stage, step))


def ring_gather(own, stage, h):
    below = shift(own, stage, 1)
    above = shift(own, stage, -1)
    across = shift(below, stage, 1) if h == 0 else shift(above, stage, -1)
    return [own, above, across, below]


def exchange(value, axis, groups=None):
    return lax.all_to_all(
        value, axis, split_axis=0, concat_axis=0, tiled=True, axis_index_groups=groups
    )


def over_tensor(value, bits=(1, 2, 4)):
    for bit in bits:
        value = value + lax.ppermute(value, "tensor", [(t, t ^ bit) for t in range(8)])
    return value


def over_side(value, axis):
    def from_step(step):
        def move(x, z, y, c):
            if axis == 0:
                return ((x + step) % SIDE, z, y, c)
            return (x, (z + step) % SIDE, y, c)

        return lax.ppermute(value, BOTH, pairs(move))

    return [value, from_step(1), from_step(2), from_step(3)]


def after(value, *events):
    return lax.optimization_barrier((value, *events))[0]


def with_partner(value, bit, *events):
    other = lax.ppermute(value, "dp", [(d, d ^ bit) for d in range(16)])
    return value + after(other, *events)


def total_of(parts):
    return (parts[0] + parts[2]) + (parts[1] + parts[3])


def forward_kernel(count, many, start_ref, wide_ref, *refs):
    lines, outs, held, sems = refs[:count], refs[-2 - many : -2], refs[-2], refs[-1]
    copies = [pltpu.make_async_copy(lines[m], held.at[m], sems.at[m]) for m in range(count)]
    part = held.shape[3]
    order = [lax.rem(start_ref[0] + k, SIDE) for k in range(SIDE)]

    @pl.when(pl.program_id(0) == 0)
    def _():
        for copy in copies:
            copy.start()

    for m in range(count):

        @pl.when(pl.program_id(0) == m)
        def _():
            copies[m].wait()
            weights = jnp.concatenate([held[m, k] for k in order], axis=1)
            product = jnp.dot(wide_ref[...], weights, preferred_element_type=jnp.float32)
            product = product.astype(jnp.bfloat16)
            for k in range(SIDE):
                piece = product[:, k * part : (k + 1) * part]
                if many == 1:
                    outs[0][k] = piece
                else:
                    outs[k][...] = piece


def forward(start, wide, lines, apart=False, places=1, into=None):
    tokens, depth = wide.shape
    part = lines[0].shape[2]
    count = len(lines)
    cols = count * part
    many = SIDE if apart else 1
    if apart:
        outs = [pltpu.HBM((tokens, cols), jnp.bfloat16)] * SIDE
        specs = [pl.BlockSpec((tokens, part), lambda i, n: (0, i))] * SIDE
    else:
        place = 0 if into is None else count
        outs = [pltpu.HBM((SIDE, tokens, places * cols), jnp.bfloat16)]
        specs = [pl.BlockSpec((SIDE, tokens, part), lambda i, n: (0, 0, place + i))]
    extra = [] if into is None else [into]
    made = pl.pallas_call(
        functools.partial(forward_kernel, count, many),
        out_shape=outs,
        grid_spec=pltpu.PrefetchScalarGridSpec(
            num_scalar_prefetch=1,
            grid=(count,),
            in_specs=[pl.BlockSpec(memory_space=pltpu.VMEM)]
            + [pl.BlockSpec(memory_space=pl.ANY)] * (count + len(extra)),
            out_specs=specs,
            scratch_shapes=[
                pltpu.VMEM((count, SIDE, depth, part), jnp.bfloat16),
                pltpu.SemaphoreType.DMA((count,)),
            ],
        ),
        input_output_aliases={} if into is None else {count + 2: 0},
        compiler_params=pltpu.CompilerParams(vmem_limit_bytes=24 << 20),
        cost_estimate=pl.CostEstimate(
            flops=tokens * depth * count * part,
            bytes_accessed=depth * part * count,
            transcendentals=0,
        ),
        name="forward",
    )(start, wide, *lines, *extra)
    return made if apart else made[0]


def arrange_kernel(far_ref, here_ref, *refs):
    besides, out_ref = refs[:2], refs[2]
    part = here_ref.shape[2] // 2
    far = far_ref[0]

    def total(ref, lane):
        parts = [ref[y, :, lane : lane + part].astype(jnp.float32) for y in range(SIDE)]
        return (parts[0] + parts[1] + parts[2] + parts[3]).astype(out_ref.dtype)

    for h in range(2):
        lanes = slice(h * part, (h + 1) * part)
        out_ref[far, :, lanes] = total(here_ref, h * part)
        out_ref[lax.rem(far + 1, SIDE), :, lanes] = total(besides[1 - h], h * part)
        out_ref[lax.rem(far + 3, SIDE), :, lanes] = total(besides[h], h * part)
        out_ref[lax.rem(far + 2, SIDE), :, lanes] = jnp.zeros_like(here_ref[0, :, lanes])


def arrange(far, *slots):
    tokens, cols = slots[0].shape[1:]
    rows = tokens // 2
    block = pl.BlockSpec((SIDE, rows, cols), lambda i, n: (0, i, 0))
    return pl.pallas_call(
        arrange_kernel,
        out_shape=pltpu.HBM(slots[0].shape, slots[0].dtype),
        grid_spec=pltpu.PrefetchScalarGridSpec(
            num_scalar_prefetch=1, grid=(2,), in_specs=[block] * 3, out_specs=block
        ),
        compiler_params=pltpu.CompilerParams(vmem_limit_bytes=16 << 20),
        cost_estimate=pl.CostEstimate(
            flops=4 * slots[0].size, bytes_accessed=8 * slots[0].size, transcendentals=0
        ),
        name="arrange",
    )(far, *slots)


def backward_kernel(count, first, last, spots_ref, *refs):
    lines, grads = refs[:count], refs[count : count * 5]
    weights = jnp.concatenate([line[k] for line in lines for k in range(SIDE)], axis=1)
    cols = jnp.concatenate([g[...] for g in grads], axis=1)
    product = lax.dot_general(
        cols, weights, (((1,), (1,)), ((), ())), preferred_element_type=jnp.float32
    )
    if first:
        refs[-1][...] = product.astype(jnp.bfloat16)
    elif not last:
        refs[-1][...] = (refs[-2][...].astype(jnp.float32) + product).astype(jnp.bfloat16)
    else:
        total = refs[-3][...].astype(jnp.float32) + product

        @pl.when(pl.program_id(0) < 2)
        def _():
            refs[-1][...] = total.astype(jnp.bfloat16)

        @pl.when(pl.program_id(0) >= 2)
        def _():
            refs[-2][...] = total


def backward(spots, grown, out_grad, lines, last=False):
    tokens = out_grad.shape[0]
    depth, part = lines[0].shape[1:]
    count = len(lines)
    block = depth // 4
    first = grown is None
    out_grad = pltpu.with_memory_space_constraint(out_grad, pltpu.HBM)

    def column(j):
        return pl.BlockSpec((tokens, part), lambda i, n: (0, n[j]))

    total = pl.BlockSpec((tokens, block), lambda i, n: (0, (i + 2) % 4))
    outs, specs = [pltpu.HBM((tokens, depth), jnp.bfloat16)], [total]
    if last:
        outs = [
            jax.ShapeDtypeStruct((tokens, depth // 2), jnp.float32),
            jax.ShapeDtypeStruct((tokens, depth // 2), jnp.bfloat16),
        ]
        specs = [
            pl.BlockSpec((tokens, block), lambda i, n: (0, jnp.maximum(i - 2, 0))),
            pl.BlockSpec((tokens, block), lambda i, n: (0, jnp.minimum(i, 1))),
        ]
    made = pl.pallas_call(
        functools.partial(backward_kernel, count, first, last),
        out_shape=outs,
        grid_spec=pltpu.PrefetchScalarGridSpec(
            num_scalar_prefetch=1,
            grid=(4,),
            in_specs=[pl.BlockSpec((SIDE, block, part), lambda i, n: (0, (i + 2) % 4, 0))] * count
            + [column(j) for j in range(count * SIDE)]
            + ([] if first else [total]),
            out_specs=specs,
        ),
        input_output_aliases={} if first or last else {5 * count + 1: 0},
        compiler_params=pltpu.CompilerParams(vmem_limit_bytes=28 << 20),
        cost_estimate=pl.CostEstimate(
            flops=tokens * depth * count * part,
            bytes_accessed=depth * part * count,
            transcendentals=0,
        ),
        name="backward",
    )(spots, *lines, *([out_grad] * (count * SIDE)), *([] if first else [pltpu.with_memory_space_constraint(grown, pltpu.HBM)]))
    return made if last else made[0]


def compose(logits, indices, vector_bank):
    weights = jax.nn.sigmoid(logits - logits[..., ::-1])
    levels = jnp.arange(vector_bank.shape[0], dtype=jnp.int32)
    picked = (indices[..., None] == levels).astype(jnp.float32)
    mixing = jnp.sum(picked * weights[..., None], axis=2)
    blocks = jnp.einsum("rjb,bc->rjc", mixing, vector_bank, precision=lax.Precision.HIGHEST)
    return (weights, picked, mixing, blocks.reshape(blocks.shape[0], -1))


def compose_back(grad_rows, weights, picked, mixing, vector_bank):
    blocks = grad_rows.reshape(mixing.shape[0], mixing.shape[1], -1)
    bank_part = jnp.einsum("rjb,rjc->bc", mixing, blocks, precision=lax.Precision.HIGHEST)
    projected = jnp.einsum("rjc,bc->rjb", blocks, vector_bank, precision=lax.Precision.HIGHEST)
    dots = jnp.sum(picked * projected[:, :, None, :], axis=3)
    logit_grad = weights * (dots - jnp.sum(weights * dots, axis=2, keepdims=True))
    return (bank_part, logit_grad)


def settle(piece, step, z, core):
    def from_second(parity):
        def move(x, z, y, c):
            if c == 1 and y % 2 == parity:
                return (x, z, (x + step) % SIDE, y // 2)
            return None

        return lax.ppermute(piece, BOTH, pairs(move))

    def move(x, z, y, c):
        return (x, z, y, 1) if c == 0 and (z + step) % SIDE >= 2 else None

    crossed = lax.ppermute(piece, BOTH, pairs(move))
    spot = (z + step) % SIDE
    first = jnp.where(core == 0, piece, crossed)
    first = jnp.where(spot // 2 == core, first, jnp.zeros_like(first))
    return first, spot % 2, [from_second(0), from_second(1)]


def local(attn_out, frozen_weight, vector_bank, logits_a, index_a, logits_b, index_b, out_grad):
    tokens, height = attn_out.shape
    shard = frozen_weight.shape[1]
    half, part = shard // 2, shard // 4
    f32, bf16 = jnp.float32, jnp.bfloat16
    dp, tensor = lax.axis_index("dp"), lax.axis_index("tensor")
    x, z, core = dp // SIDE, dp % SIDE, tensor % 2
    near, far = jnp.where(core == 0, x, z), jnp.where(core == 0, z, x)
    side = tensor // 2
    turned = ((SIDE - near) % SIDE).astype(jnp.int32).reshape(1)
    turned_here = ((SIDE - near + side) % SIDE).astype(jnp.int32).reshape(1)

    left, right = frozen_weight[:, :half], frozen_weight[:, half:]
    mine = jnp.where(core == 0, left, right)
    theirs = jnp.where(core == 0, right, left)
    swapped = lax.ppermute(theirs, "tensor", SWAP)
    shards = []
    for h in range(2):
        cols = slice(h * part, (h + 1) * part)
        shards.append(jnp.concatenate([mine[:, cols], swapped[:, cols]], axis=0))
    logits_a, logits_b, *shards = lax.optimization_barrier((logits_a, logits_b, *shards))
    lines = [jnp.stack(ring_gather(shards[h], 0, h)) for h in range(2)]
    def columns(i, h):
        far_at = (far + i) % SIDE
        spots = []
        for k in range(SIDE):
            near_at = (near + k) % SIDE
            x_at = jnp.where(core == 0, near_at, far_at)
            z_at = jnp.where(core == 0, far_at, near_at)
            spots.append((x_at * SIDE + z_at) * 4 + core * 2 + h)
        return spots

    def spots_of(chunks):
        return jnp.stack([s for i, h in chunks for s in columns(i, h)]).astype(jnp.int32)

    wide = jnp.concatenate([attn_out, lax.ppermute(attn_out, "tensor", SWAP)], axis=1)

    weights_a, picked_a, mixing_a, rows_a = compose(logits_a, index_a, vector_bank)
    weights_b, picked_b, mixing_b, rows_b = compose(logits_b, index_b, vector_bank)
    down_a, up_b = rows_a.astype(bf16), rows_b.astype(bf16)
    rank = down_a.shape[0]
    grad_cols = lax.dynamic_slice_in_dim(out_grad, tensor * height, height, 1)
    cols_by_cols = (((1,), (1,)), ((), ()))
    rows_by_rows = (((0,), (0,)), ((), ()))
    low_part = lax.dot_general(down_a, attn_out, cols_by_cols, preferred_element_type=f32)
    back_part = lax.dot_general(up_b, grad_cols, cols_by_cols, preferred_element_type=f32)
    totals = jnp.concatenate([low_part, back_part], axis=0)
    lines[1], totals = lax.optimization_barrier((lines[1], totals))
    below = [shift(line, 1, 1) for line in lines]
    above = [shift(line, 1, -1) for line in lines]
    totals = over_tensor(totals).astype(bf16)
    low_bf, back_bf = totals[:rank], totals[rank:]

    factor = adapter_scale / (tokens * lax.axis_size("dp"))
    grad_a = jnp.dot(back_bf, attn_out, preferred_element_type=f32)
    grad_b = jnp.dot(low_bf, grad_cols, preferred_element_type=f32)
    both = factor * jnp.concatenate([grad_a, grad_b], axis=0)
    here = [(0, 0), (0, 1)]
    beside = [[(3, 0), (1, 1)], [(1, 0), (3, 1)]]
    across = [(2, 0), (2, 1)]

    sent_here = forward(turned, wide, lines)
    sent_here, totals = lax.optimization_barrier((sent_here, totals))
    low_bf, back_bf = totals[:rank], totals[rank:]
    slots_here = exchange(sent_here, "tensor", LANES)
    grown = backward(after(spots_of(here), sent_here), None, out_grad, lines)
    below[0], above[1], grown, totals = lax.optimization_barrier(
        (below[0], above[1], grown, totals)
    )
    corner = [shift(below[0], 1, 1), shift(above[1], 1, -1)]
    blocks = [[lines[h], above[h], corner[h], below[h]] for h in range(2)]

    def take(chunks):
        return [blocks[h][i] for i, h in chunks]

    sent_first = forward(turned, wide, take(beside[0]))
    slots_here, sent_first = lax.optimization_barrier((slots_here, sent_first))
    slots_first = exchange(sent_first, "tensor", LANES)
    sent_second = forward(after(turned, sent_first), wide, take(beside[1]))
    slots_first, sent_second, both = lax.optimization_barrier((slots_first, sent_second, both))
    slots_second = exchange(sent_second, "tensor", LANES)
    both_parts = over_side(both, 0)
    chunks = beside[0] + beside[1]
    grown = backward(after(spots_of(chunks), sent_second), grown, out_grad, take(chunks))
    both = total_of(lax.optimization_barrier((*both_parts, grown))[:SIDE])
    slots = arrange(
        far.astype(jnp.int32).reshape(1), slots_here, slots_first, after(slots_second, grown, both)
    )
    both = with_partner(both, 1, slots)
    moved = exchange(slots, "tensor", LANES)
    sent = forward(after(turned_here, slots, both), wide, take(across), apart=True)
    arrived = [sent[0]]
    for step in range(1, SIDE):
        turns = [(t, (t + 2 * step) % 8) for t in range(8)]
        arrived.append(lax.ppermute(sent[step], "tensor", turns))
    piece = total_of([a.astype(f32) for a in arrived]).astype(bf16)
    both = with_partner(both, 2, *sent)
    bank_a, logit_grad_a = compose_back(both[:rank], weights_a, picked_a, mixing_a, vector_bank)
    bank_b, logit_grad_b = compose_back(both[rank:], weights_b, picked_b, mixing_b, vector_bank)
    bank_part = over_tensor(bank_a + bank_b, (1,))
    grown, other = backward(
        after(spots_of(across), *sent, bank_part), grown, out_grad, take(across), last=True
    )
    bank_grad = over_tensor(bank_part, (2, 4))
    crossed = lax.ppermute(jnp.where(core == 0, slots[2:], moved[:2]), "tensor", SWAP)
    firsts = jnp.where(core == 0, slots[:2], crossed)
    seconds = jnp.where(core == 0, crossed, moved[2:])

    first, place, second = settle(piece, 2, z, core)
    cols = []
    for s in range(2):
        cols.append(firsts[s] + jnp.where(place == s, first, jnp.zeros_like(first)))
        cols.append(seconds[s] + second[s])
    summed = jnp.concatenate(cols, axis=1)
    layer_out = (
        summed.astype(f32)
        + adapter_scale * lax.dot_general(low_bf, up_b, rows_by_rows, preferred_element_type=f32)
    ).astype(bf16)
    other = lax.ppermute(other, "tensor", SWAP)
    attn_grad = (
        grown
        + other.astype(f32)
        + adapter_scale * lax.dot_general(back_bf, down_a, rows_by_rows, preferred_element_type=f32)
    ).astype(bf16)
    return (layer_out, attn_grad, bank_grad, logit_grad_a, logit_grad_b)


def solution(mesh):
    return jax.shard_map(
        local,
        mesh=mesh,
        in_specs=(
            P("dp", "tensor"),
            P("tensor", "dp"),
            P(),
            P(None, "tensor", None),
            P(None, "tensor", None),
            P(None, "tensor", None),
            P(None, "tensor", None),
            P("dp", None),
        ),
        out_specs=(
            P("dp", "tensor"),
            P("dp", "tensor"),
            P(),
            P(None, "tensor", None),
            P(None, "tensor", None),
        ),
        check_vma=False,
    )
```
